32 devices in a mesh: wide: 8 (over z, y), narrow: 4 (over x, core).
Axes of the slice: x: 2, y: 2, z: 4, core: 2. Of those that a mesh axis runs over, the one named last changes fastest.
Arguments:
- codons: int32 [32, 1024], P(('wide', 'narrow')), may hold values from 0 to 69
- offsets: int32 [32], P(('wide', 'narrow')), may hold values from 0 to 112
- positions: int32 [32, 912], P(('wide', 'narrow')), may hold values from 0 to 1023
- targets: int32 [32, 912], P(('wide', 'narrow')), may hold values from 0 to 69
- table_weight: float32 [70, 768], P(None, 'wide'), may hold values from -0.21875 to 0.21875
- attend_weight: float32 [2304, 768], P('wide'), may hold values from -0.21875 to 0.21875
- mixing_weight: float32 [768, 768], P('wide'), may hold values from -1.5 to 1.5
- expand_weight: float32 [3072, 768], P('wide'), may hold values from -0.21875 to 0.21875
- reduce_weight: float32 [3072, 768], P('wide'), may hold values from -0.109375 to 0.109375
- vector_params: float32 [15, 768], P(None, 'wide'), may hold values from -1.5 to 1.5
- attend_moment: float32 [2304, 768], P('wide'), may hold values from -10 to 10
- mixing_moment: float32 [768, 768], P('wide'), may hold values from -10 to 10
- expand_moment: float32 [3072, 768], P('wide'), may hold values from -10 to 10
- reduce_moment: float32 [3072, 768], P('wide'), may hold values from -10 to 10
- table_mean: float32 [70, 768], P(None, 'wide'), may hold values from -6 to 6
- table_square: float32 [70, 768], P(None, 'wide'), may hold values from 2.04288 to 29.184
- vector_mean: float32 [15, 768], P(None, 'wide'), may hold values from -2 to 2
- vector_square: float32 [15, 768], P(None, 'wide'), may hold values from 0.29184 to 4.96128
- step_count: int32 [], replicated, may hold values from 2 to 20
Outputs:
- block_output: bfloat16 [32, 912, 768], P(('wide', 'narrow'))
- entry_gradient: float32 [32, 912, 768], P(('wide', 'narrow'))
- attend_gradient: float32 [2304, 768], P('wide')
- mixing_gradient: float32 [768, 768], P('wide')
- expand_gradient: float32 [3072, 768], P('wide')
- reduce_gradient: float32 [3072, 768], P('wide')
- table_gradient: float32 [70, 768], P(None, 'wide')
- vector_gradient: float32 [15, 768], P(None, 'wide')
- attend_updated: float32 [2304, 768], P('wide')
- mixing_updated: float32 [768, 768], P('wide')
- expand_updated: float32 [3072, 768], P('wide')
- reduce_updated: float32 [3072, 768], P('wide')
- attend_momentum: float32 [2304, 768], P('wide')
- mixing_momentum: float32 [768, 768], P('wide')
- expand_momentum: float32 [3072, 768], P('wide')
- reduce_momentum: float32 [3072, 768], P('wide')
- table_updated: float32 [70, 768], P(None, 'wide')
- table_mean_next: float32 [70, 768], P(None, 'wide')
- table_square_next: float32 [70, 768], P(None, 'wide')
- vector_updated: float32 [15, 768], P(None, 'wide')
- vector_mean_next: float32 [15, 768], P(None, 'wide')
- vector_square_next: float32 [15, 768], P(None, 'wide')
- histogram: float32 [70], replicated
The draws below stay inside these ranges and needn't reach their ends.
All inputs are finite; a program needn't handle non-finite values.
Results may differ from the reference program's by a relative error of at most 0.012.
The reference program's roundings to bfloat16 on the way count: a program that leaves them out, or rounds other values in their place, can miss the bound.
Values may be sent and summed in bfloat16 or wider, within the bound.
No kernel may reach another device: no remote copies, remote signals or barrier semaphores. Data moves between devices by JAX's collectives and lax.ppermute only.
A program may use at most 192 MiB of HBM per device.

```python
import math
import jax
import jax.numpy as jnp
import numpy as np
from jax import lax

D = 768
HEADS = 12
HEAD_DIM = 64
FF = 3072
VOCAB = 70
SEQ_LEN = 912
GENE_LEN = 1024
NS_ITERS = 5
SEQS = 32
TOKENS = 29184


def draw_vector_params(key, part):
    gain_key, bias_key = jax.random.split(key)
    gains = jax.random.uniform(gain_key, (15, D), jnp.float32, 0.5, 1.5)
    biases = jnp.clip(0.3 * jax.random.normal(bias_key, (15, D), jnp.float32), -1.5, 1.5)
    row_ids = jnp.arange(15)
    is_gain = ((row_ids < 6) & (row_ids % 2 == 0))[:, None]
    return jnp.where(is_gain, gains, biases)


def place_ends(result, rng, low, largest):
    spot = [jax.random.randint(jax.random.fold_in(rng, axis), (), 0, length) for axis, length in enumerate(result.shape)]
    main_axis = result.shape.index(max(result.shape))
    beside = spot[:main_axis] + [(spot[main_axis] + 1) % result.shape[main_axis]] + spot[main_axis + 1:]
    return result.at[tuple(spot)].set(low).at[tuple(beside)].set(largest)


def steps_of(key, extent, shards, least, largest):
    gain, own = 1.0, jax.random.fold_in(key, 6)
    for position, parts in shards:
        draws = jnp.exp(jax.random.uniform(jax.random.fold_in(own, position), (parts,), jnp.float32, least / len(shards), largest / len(shards)))
        gain = gain * jnp.repeat(draws, extent[position] // parts).reshape([-1 if axis == position else 1 for axis in range(len(extent))])
    return gain


def rank_table(number_of, slope):
    weights = [(1 << 20) // math.isqrt(standing ** slope) + 1 for standing in range(1, number_of + 1)]
    deviation = 1 + sum(weights) // (1 << 30)
    return np.cumsum(np.array([max(1, weight // deviation) for weight in weights]))


def ranked_ids(stream_key, shape, amount, skew):
    table = rank_table(amount, skew)
    pick = jax.random.randint(jax.random.fold_in(stream_key, 1), shape, 0, int(table[amount - 1]))
    standing = jnp.searchsorted(jnp.asarray(table, jnp.int32), pick, side="right")
    return jax.random.permutation(jax.random.fold_in(stream_key, 2), amount)[standing].astype(jnp.int32)


def centred(key, extent, scale, most, shards=(), held_as=jnp.bfloat16):
    values = jax.random.normal(key, extent, jnp.float32) * scale
    if len(shards) > 0:
        values = steps_of(key, extent, shards, -0.22, 0.18) * values
    return jnp.clip(values, min=-most, max=most).astype(held_as)


def setup_inputs(seed: int = 0) -> dict:
    streams_of = jax.random.split(jax.random.key(seed), 20)
    return {
        "codons": place_ends(ranked_ids(streams_of[0], (SEQS, GENE_LEN), VOCAB, 1), jax.random.fold_in(streams_of[0], 3), 0, VOCAB - 1).astype(jnp.int32),
        "offsets": place_ends(jax.random.randint(streams_of[1], (SEQS,), 0, GENE_LEN - SEQ_LEN + 1), jax.random.fold_in(streams_of[1], 1), 0, GENE_LEN - SEQ_LEN).astype(jnp.int32),
        "positions": place_ends(jax.random.randint(streams_of[2], (SEQS, SEQ_LEN), 0, GENE_LEN), jax.random.fold_in(streams_of[2], 1), 0, GENE_LEN - 1).astype(jnp.int32),
        "targets": place_ends(ranked_ids(streams_of[3], (SEQS, SEQ_LEN), VOCAB, 1), jax.random.fold_in(streams_of[3], 3), 0, VOCAB - 1).astype(jnp.int32),
        "table_weight": centred(streams_of[4], (VOCAB, D), D ** -0.5, 0.21875, ((1, 8),), jnp.float32),
        "attend_weight": centred(streams_of[5], (3 * D, D), D ** -0.5, 0.21875, ((0, 8),), jnp.float32),
        "mixing_weight": centred(streams_of[6], (D, D), 16 ** -0.5, 1.5, ((0, 8),), jnp.float32),
        "expand_weight": centred(streams_of[7], (FF, D), D ** -0.5, 0.21875, ((0, 8),), jnp.float32),
        "reduce_weight": centred(streams_of[8], (FF, D), FF ** -0.5, 0.109375, ((0, 8),), jnp.float32),
        "vector_params": draw_vector_params(jax.random.fold_in(streams_of[19], 71), 0),
        "attend_moment": centred(streams_of[10], (3 * D, D), (0.01 * (SEQS * SEQ_LEN) ** 0.5), 10.0, ((0, 8),), jnp.float32),
        "mixing_moment": centred(streams_of[11], (D, D), (0.01 * (SEQS * SEQ_LEN) ** 0.5), 10.0, ((0, 8),), jnp.float32),
        "expand_moment": centred(streams_of[12], (FF, D), (0.01 * (SEQS * SEQ_LEN) ** 0.5), 10.0, ((0, 8),), jnp.float32),
        "reduce_moment": centred(streams_of[13], (FF, D), (0.01 * (SEQS * SEQ_LEN) ** 0.5), 10.0, ((0, 8),), jnp.float32),
        "table_mean": centred(streams_of[14], (VOCAB, D), (0.006 * (SEQS * SEQ_LEN) ** 0.5), 6.0, ((1, 8),), jnp.float32),
        "table_square": jnp.clip(jnp.exp(math.log(29.184) - 2.65926 * jax.random.uniform(streams_of[15], (VOCAB, D), jnp.float32) ** steps_of(streams_of[15], (VOCAB, D), ((1, 8),), -0.2, 0.2)), 2.04288, 29.184),
        "vector_mean": centred(streams_of[16], (15, D), (0.0022 * (SEQS * SEQ_LEN) ** 0.5), 2.0, ((1, 8),), jnp.float32),
        "vector_square": jnp.clip(jnp.exp(math.log(4.96128) - 2.8332134 * jax.random.uniform(streams_of[17], (15, D), jnp.float32) ** steps_of(streams_of[17], (15, D), ((1, 8),), -0.2, 0.2)), 0.29184, 4.96128),
        "step_count": jax.random.randint(streams_of[18], (), 2, 21).astype(jnp.int32),
    }


@jax.custom_vjp
def low(v):
    return lax.optimization_barrier(v.astype(jnp.bfloat16)).astype(jnp.float32)

@jax.custom_vjp
def low_back(v):
    return v

def low_keep(v):
    return (low(v), None)

def low_pass(kept, grad):
    return (grad,)

def back_keep(v):
    return (v, None)

def back_low(kept, grad):
    return (low(grad),)
low.defvjp(low_keep, low_pass)
low_back.defvjp(back_keep, back_low)
NORM_EPS = 1e-05
ROPE_BASE = 10000.0
NEWTON_A = 3.4445
NEWTON_B = -4.775
NEWTON_C = 2.0315
MUON_MU = 0.95
MUON_RATE = 0.3
MUON_DECAY = 0.1
SHAPE_FACTOR = 0.2
ADAM_BETA1 = 0.9
ADAM_BETA2 = 0.95
ADAM_EPS = 1e-08
TABLE_RATE = 0.03
TABLE_DECAY = 0.01
VECTOR_RATE = 0.2

def product(left_side, right_side):
    return jnp.dot(left_side, right_side, precision=lax.Precision.HIGHEST, preferred_element_type=jnp.float32)

def layer_norm(values, gain_row, bias_row):
    center = values - lax.optimization_barrier(jnp.mean(values, axis=-1, keepdims=True))
    spread = lax.optimization_barrier(jnp.mean(center * center, axis=-1, keepdims=True))
    return center * lax.rsqrt(spread + NORM_EPS) * gain_row + bias_row

def rotate(values, cosine, sine_table):
    half_dim = values.shape[-1] // 2
    first_half = values[..., :half_dim]
    second_half = values[..., half_dim:]
    return jnp.concatenate([first_half * cosine - second_half * sine_table, second_half * cosine + first_half * sine_table], axis=-1)

def angles(position_row):
    half_dim = HEAD_DIM // 2
    frequency = ROPE_BASE ** (-(jnp.arange(half_dim, dtype=jnp.float32) * 2.0 / HEAD_DIM))
    turned = position_row.astype(jnp.float32)[:, None] * frequency[None, :]
    return (jnp.cos(turned)[:, None, :], jnp.sin(turned)[:, None, :])

def one_sequence(table_low, attend_low, mixing_low, expand_low, reduce_low, vector_low, codon_row, offset, position_row, target_row, shift_row):
    tokens = lax.dynamic_slice_in_dim(codon_row, offset, SEQ_LEN)
    stream = math.sqrt(D) * table_low[tokens] + shift_row
    attend_bias = vector_low[6:9].reshape(3 * D)
    mixing_bias = vector_low[9]
    reduce_bias = vector_low[10]
    expand_bias = vector_low[11:15].reshape(FF)
    normed_one = layer_norm(stream, vector_low[0], vector_low[1])
    projected = low_back(product(low(normed_one), attend_low.T) + attend_bias)
    head_shape = (SEQ_LEN, HEADS, HEAD_DIM)
    cosine, sine_table = angles(position_row)
    query_low = low(rotate(projected[:, :D].reshape(head_shape), cosine, sine_table))
    key_low = low(rotate(projected[:, D:2 * D].reshape(head_shape), cosine, sine_table))
    value_low = low(projected[:, 2 * D:].reshape(head_shape))
    scores = low_back(jnp.einsum('qhd,khd->hqk', query_low, key_low, precision=lax.Precision.HIGHEST) * HEAD_DIM ** (-0.5))
    soft_weights = jax.nn.softmax(scores, axis=-1)
    mixed_heads = jnp.einsum('hqk,khd->qhd', low(soft_weights), value_low, precision=lax.Precision.HIGHEST).reshape(SEQ_LEN, D)
    mixed_low = low(low_back(mixed_heads))
    branch = low_back(product(mixed_low, mixing_low.T) + mixing_bias)
    middle = stream + branch
    normed_two = layer_norm(middle, vector_low[2], vector_low[3])
    hidden_pre = low_back(product(low(normed_two), expand_low.T) + expand_bias)
    hidden_low = low(jax.nn.gelu(hidden_pre, approximate=False))
    feed_out = low_back(product(hidden_low, reduce_low) + reduce_bias)
    output = middle + feed_out
    final_norm = layer_norm(output, vector_low[4], vector_low[5])
    logits = low_back(product(low(final_norm), table_low.T))
    log_total = jax.nn.logsumexp(logits, axis=-1)
    picked = jnp.take_along_axis(logits, target_row[:, None], axis=1)[:, 0]
    loss_value = jnp.sum(log_total - picked)
    prob_rows = jnp.exp(logits - log_total[:, None])
    return (loss_value, output, lax.optimization_barrier(jnp.sum(prob_rows, axis=0)))

def forward(params, shift_zero, codons, offsets, positions, targets):
    table_weight, attend_weight, mixing_weight, expand_weight, reduce_weight, vector_params = params
    lowered = (low(table_weight), low(attend_weight), low(mixing_weight), low(expand_weight), low(reduce_weight), low(vector_params))
    checked = jax.checkpoint(one_sequence)

    def scan_step(carry_sum, seq_item):
        loss_value, output, prob_sum = checked(lowered[0], lowered[1], lowered[2], lowered[3], lowered[4], lowered[5], seq_item[0], seq_item[1], seq_item[2], seq_item[3], seq_item[4])
        return ((carry_sum[0] + loss_value, carry_sum[1] + prob_sum), output)
    start_sums = (jnp.zeros((), jnp.float32), jnp.zeros((VOCAB,), jnp.float32))
    sums_out, outputs = lax.scan(scan_step, start_sums, (codons, offsets, positions, targets, shift_zero))
    return (sums_out[0], (outputs, sums_out[1]))

def newton(update):
    current = update / (jnp.sqrt(jnp.sum(update * update)) + 1e-07)
    for sweep_step in range(NS_ITERS):
        gram = product(current.T, current)
        moved_rows = product(current, gram)
        current = NEWTON_A * current + NEWTON_B * moved_rows + NEWTON_C * product(moved_rows, gram)
    return current

def muon(weight, moment, gradient):
    moment_next = MUON_MU * moment + (1.0 - MUON_MU) * gradient
    update = (1.0 - MUON_MU) * gradient + MUON_MU * moment_next
    ortho_rows = newton(update)
    shape_scale = SHAPE_FACTOR * math.sqrt(max(weight.shape[0], weight.shape[1]))
    return (weight * (1.0 - MUON_RATE * MUON_DECAY) - MUON_RATE * shape_scale * ortho_rows, moment_next)

def adam_step(weight, mean_state, square, gradient, step_rate, decay_rate, step_count):
    mean_next = ADAM_BETA1 * mean_state + (1.0 - ADAM_BETA1) * gradient
    square_next = ADAM_BETA2 * square + (1.0 - ADAM_BETA2) * gradient * gradient
    step_float = step_count.astype(jnp.float32)
    mean_hat = mean_next / (1.0 - ADAM_BETA1 ** step_float)
    square_hat = square_next / (1.0 - ADAM_BETA2 ** step_float)
    updated = weight - step_rate * (mean_hat / (jnp.sqrt(square_hat) + ADAM_EPS) + decay_rate * weight)
    return (updated, mean_next, square_next)

def reference(codons, offsets, positions, targets, table_weight, attend_weight, mixing_weight, expand_weight, reduce_weight, vector_params, attend_moment, mixing_moment, expand_moment, reduce_moment, table_mean, table_square, vector_mean, vector_square, step_count):
    params = (table_weight, attend_weight, mixing_weight, expand_weight, reduce_weight, vector_params)
    shift_zero = jnp.zeros((SEQS, SEQ_LEN, D), jnp.float32)

    def loss_of(params_in, shift_in):
        return forward(params_in, shift_in, codons, offsets, positions, targets)
    loss_value, pullback, aux_pair = jax.vjp(loss_of, params, shift_zero, has_aux=True)
    outputs, prob_total = aux_pair
    param_grads, entry_gradient = pullback(jnp.ones((), jnp.float32))
    table_grad, attend_grad, mixing_grad, expand_grad, reduce_grad, vector_grad = param_grads
    attend_new, attend_next = muon(attend_weight, attend_moment, attend_grad)
    mixing_new, mixing_next = muon(mixing_weight, mixing_moment, mixing_grad)
    expand_new, expand_next = muon(expand_weight, expand_moment, expand_grad)
    reduce_new, reduce_next = muon(reduce_weight, reduce_moment, reduce_grad)
    table_new, table_mean_next, table_square_next = adam_step(table_weight, table_mean, table_square, table_grad, TABLE_RATE, TABLE_DECAY, step_count)
    vector_new, vector_mean_next, vector_square_next = adam_step(vector_params, vector_mean, vector_square, vector_grad, VECTOR_RATE, 0.0, step_count)
    histogram = VOCAB * prob_total / TOKENS
    return (outputs.astype(jnp.bfloat16), entry_gradient, attend_grad, mixing_grad, expand_grad, reduce_grad, table_grad, vector_grad, attend_new, mixing_new, expand_new, reduce_new, attend_next, mixing_next, expand_next, reduce_next, table_new, table_mean_next, table_square_next, vector_new, vector_mean_next, vector_square_next, histogram)
```

```python
from functools import partial
import math

import jax
import jax.numpy as jnp
import numpy as np
from jax import lax
from jax.experimental import pallas as pl
from jax.experimental.pallas import tpu as pltpu
from jax.sharding import PartitionSpec as P

D = 768
HEADS = 12
HEAD_DIM = 64
FF = 3072
VOCAB = 70
SEQ_LEN = 912
NS_ITERS = 5


NORM_EPS = 1e-05
ROPE_BASE = 10000.0
NEWTON_A = 3.4445
NEWTON_B = -4.775
NEWTON_C = 2.0315
MUON_MU = 0.95
MUON_RATE = 0.3
MUON_DECAY = 0.1
SHAPE_FACTOR = 0.2
ADAM_BETA1 = 0.9
ADAM_BETA2 = 0.95
ADAM_EPS = 1e-08
TABLE_RATE = 0.03
TABLE_DECAY = 0.01
VECTOR_RATE = 0.2


def times_plain(left_side, right_side):
    return jnp.dot(left_side, right_side, preferred_element_type=jnp.float32)


def times_trans(left_side, right_side):
    return lax.dot_general(
        left_side, right_side, (((1,), (1,)), ((), ())), preferred_element_type=jnp.float32
    )


def trans_times(left_side, right_side):
    return lax.dot_general(
        left_side, right_side, (((0,), (0,)), ((), ())), preferred_element_type=jnp.float32
    )


def exact_times(left_side, right_side):
    return jnp.dot(
        left_side, right_side, precision=lax.Precision.HIGHEST, preferred_element_type=jnp.float32
    )


def norm_forward(values, gain_row, bias_row):
    center = values - jnp.mean(values, axis=-1, keepdims=True)
    spread = jnp.mean(center * center, axis=-1, keepdims=True)
    inverse = lax.rsqrt(spread + NORM_EPS)
    normal = center * inverse
    return (normal * gain_row + bias_row, normal, inverse)


def norm_backward(upstream, normal, inverse, gain_row):
    scaled = upstream * gain_row
    inner_part = (
        scaled
        - jnp.mean(scaled, axis=-1, keepdims=True)
        - normal * jnp.mean(scaled * normal, axis=-1, keepdims=True)
    )
    return (inverse * inner_part, jnp.sum(upstream * normal, axis=0), jnp.sum(upstream, axis=0))


def rotary_tables(positions):
    half_dim = HEAD_DIM // 2
    frequency = ROPE_BASE ** (-(jnp.arange(half_dim, dtype=jnp.float32) * 2.0 / HEAD_DIM))
    turned = positions.astype(jnp.float32)[..., None] * frequency
    return (jnp.cos(turned)[..., None, :], jnp.sin(turned)[..., None, :])


def rotate(values, cosine, sine_table):
    half_dim = values.shape[-1] // 2
    first_half = values[..., :half_dim]
    second_half = values[..., half_dim:]
    return jnp.concatenate(
        [
            first_half * cosine - second_half * sine_table,
            second_half * cosine + first_half * sine_table,
        ],
        axis=-1,
    )


def unrotate(values, cosine, sine_table):
    half_dim = values.shape[-1] // 2
    first_half = values[..., :half_dim]
    second_half = values[..., half_dim:]
    return jnp.concatenate(
        [
            first_half * cosine + second_half * sine_table,
            second_half * cosine - first_half * sine_table,
        ],
        axis=-1,
    )


def attend_head(operands):
    query_head, key_head, value_head = operands
    scores = jnp.einsum(
        "sqd,skd->sqk", query_head, key_head, preferred_element_type=jnp.float32
    ) * HEAD_DIM ** (-0.5)
    row_peak = jnp.max(scores, axis=-1, keepdims=True)
    exp_scores = jnp.exp(scores - row_peak)
    row_total = jnp.sum(exp_scores, axis=-1, keepdims=True)
    prob_low = (exp_scores / row_total).astype(jnp.bfloat16)
    mixed_head = jnp.einsum(
        "sqk,skd->sqd", prob_low, value_head, preferred_element_type=jnp.float32
    )
    return (mixed_head, (row_peak + jnp.log(row_total))[..., 0])


def attend_back(operands):
    query_head, key_head, value_head, grad_head, log_total = operands
    scores = jnp.einsum(
        "sqd,skd->sqk", query_head, key_head, preferred_element_type=jnp.float32
    ) * HEAD_DIM ** (-0.5)
    prob_rows = jnp.exp(scores - log_total[..., None])
    prob_low = prob_rows.astype(jnp.bfloat16)
    value_grad = jnp.einsum("sqk,sqd->skd", prob_low, grad_head, preferred_element_type=jnp.float32)
    prob_grad = jnp.einsum(
        "sqd,skd->sqk", grad_head, value_head, preferred_element_type=jnp.float32
    )
    row_delta = jnp.sum(prob_grad * prob_rows, axis=-1, keepdims=True)
    score_grad = (prob_rows * (prob_grad - row_delta)).astype(jnp.bfloat16)
    query_grad = jnp.einsum(
        "sqk,skd->sqd", score_grad, key_head, preferred_element_type=jnp.float32
    ) * HEAD_DIM ** (-0.5)
    key_grad = jnp.einsum(
        "sqk,sqd->skd", score_grad, query_head, preferred_element_type=jnp.float32
    ) * HEAD_DIM ** (-0.5)
    return (query_grad, key_grad, value_grad)


BOTH = ("wide", "narrow")
GRAM_TILE = 256
GRAM_SPOTS = ((0, 0), (0, 1), (0, 2), (1, 1), (1, 2), (2, 2))


def swap(value, mask):
    total = lax.axis_size(BOTH)
    return lax.ppermute(value, BOTH, [(spot, spot ^ mask) for spot in range(total)])


def my_index():
    return lax.axis_index("wide") * lax.axis_size("narrow") + lax.axis_index("narrow")


def wide_masks():
    narrow_size = lax.axis_size("narrow")
    count = lax.axis_size("wide").bit_length() - 1
    return [narrow_size << bit for bit in reversed(range(count))]


def offsets_of(masks):
    table = [0]
    for mask in masks:
        table = table + [offset ^ mask for offset in table]
    return np.array(table)


def gather_blocks(piece, masks):
    for mask in masks:
        piece = jnp.concatenate([piece, swap(piece, mask)], axis=0)
    return piece


def take_blocks(array, index):
    return jnp.take(array, index, axis=0, mode="clip")


def in_order(blocks, masks, unit, base):
    offsets = offsets_of(masks) // unit
    place = np.zeros_like(offsets)
    place[offsets] = np.arange(offsets.size)
    return take_blocks(blocks, jnp.asarray(place)[jnp.arange(offsets.size) ^ base])


def out_of_order(blocks, masks, unit, base):
    offsets = offsets_of(masks) // unit
    return take_blocks(blocks, jnp.asarray(offsets) ^ base)


def gather_wide(piece):
    blocks = gather_blocks(piece[None], wide_masks())
    return in_order(blocks, wide_masks(), lax.axis_size("narrow"), lax.axis_index("wide"))


def quarter_rows(array):
    count = array.shape[0] // lax.axis_size("narrow")
    return lax.dynamic_slice_in_dim(array, lax.axis_index("narrow") * count, count, 0)


def scatter_blocks(keep, send, masks, wide_type):
    for step, mask in enumerate(masks):
        send_type = wide_type if step + 2 >= len(masks) else jnp.bfloat16
        total = keep + swap(send.astype(send_type), mask).astype(jnp.float32)
        half = total.shape[0] // 2
        keep, send = total[:half], total[half:]
    return total


def narrow_rows(piece):
    spot = lax.axis_index("narrow")
    other = swap(piece, 2)
    pair = jnp.where(spot // 2 == 0, jnp.stack([piece, other]), jnp.stack([other, piece]))
    other = swap(pair, 1)
    quad = jnp.where(
        spot % 2 == 0, jnp.stack([pair, other], axis=1), jnp.stack([other, pair], axis=1)
    )
    return quad.reshape(4 * piece.shape[0], piece.shape[1])


def sum_small(blocks):
    masks = wide_masks()
    blocks = blocks + swap(blocks, 1)
    blocks = out_of_order(blocks, masks, lax.axis_size("narrow"), lax.axis_index("wide"))
    for mask in reversed(masks):
        half = blocks.shape[0] // 2
        blocks = blocks[:half] + swap(blocks[half:], mask)
    piece = blocks[0]
    return piece + swap(piece, 2)


def sum_gram(blocks):
    wide_at = lax.axis_index("wide")
    narrow_size = lax.axis_size("narrow")
    masks = wide_masks()
    bits = [(mask // narrow_size).bit_length() - 1 for mask in masks]
    order = list(zip(masks, bits))
    order = list(reversed(order))
    for mask, bit in order:
        side = (wide_at >> bit) % 2
        half = blocks.shape[0] // 2
        keep = lax.dynamic_slice_in_dim(blocks, side * half, half, 0)
        send = lax.dynamic_slice_in_dim(blocks, (1 - side) * half, half, 0)
        blocks = keep + swap(send, mask)
    for mask, bit in reversed(order):
        side = (wide_at >> bit) % 2
        other = swap(blocks, mask)
        blocks = jnp.where(
            side == 0,
            jnp.concatenate([blocks, other], axis=0),
            jnp.concatenate([other, blocks], axis=0),
        )
    return blocks


def split_two(values):
    high = values.astype(jnp.bfloat16)
    return high, (values - high.astype(jnp.float32)).astype(jnp.bfloat16)


def newton_kernel(gram_ref, out_ref, gram_now, total, left, right):
    tile = GRAM_TILE
    trace = jnp.zeros((1, 1), jnp.float32)
    spot_mask = lax.broadcasted_iota(jnp.int32, (tile, tile), 0) == lax.broadcasted_iota(
        jnp.int32, (tile, tile), 1
    )
    for number, (row, column) in enumerate(GRAM_SPOTS):
        block = gram_ref[number * tile : (number + 1) * tile, :]
        if row == column:
            picked = jnp.where(spot_mask, block, 0.0)
            trace = trace + jnp.sum(jnp.sum(picked, axis=0, keepdims=True), axis=1, keepdims=True)
    length = jnp.sqrt(trace) + 1e-07
    inverse = 1.0 / length
    scale = inverse * inverse
    for number, (row, column) in enumerate(GRAM_SPOTS):
        block = gram_ref[number * tile : (number + 1) * tile, :] * scale
        gram_now[row * tile : (row + 1) * tile, column * tile : (column + 1) * tile] = block
        if row != column:
            gram_now[column * tile : (column + 1) * tile, row * tile : (row + 1) * tile] = block.T

    def set_left(values):
        high, low = split_two(values)
        left[:, 0:D] = high
        left[:, D : 2 * D] = high
        left[:, 2 * D : 3 * D] = low

    def set_right(values):
        high, low = split_two(values)
        right[0:D, :] = high
        right[D : 2 * D, :] = low
        right[2 * D : 3 * D, :] = high

    def product():
        return jnp.dot(left[...], right[...], preferred_element_type=jnp.float32)

    diagonal = lax.broadcasted_iota(jnp.int32, (D, D), 0) == lax.broadcasted_iota(
        jnp.int32, (D, D), 1
    )

    def set_factor():
        set_left(gram_now[...])
        set_right(gram_now[...])
        factor = NEWTON_B * gram_now[...] + NEWTON_C * product()
        factor = factor + jnp.where(diagonal, NEWTON_A, 0.0)
        set_right(factor)
        return factor

    def advance():
        moved = product()
        set_left(moved)
        gram_now[...] = product()

    total[...] = set_factor()
    advance()

    def body(step, carry):
        set_factor()
        advance()
        set_left(total[...])
        total[...] = product()
        return carry

    lax.fori_loop(0, NS_ITERS - 2, body, 0)
    set_factor()
    set_left(total[...])
    out_ref[...] = product() * inverse


def newton_product(gram_blocks):
    return pl.pallas_call(
        newton_kernel,
        out_shape=jax.ShapeDtypeStruct((D, D), jnp.float32),
        in_specs=[pl.BlockSpec(memory_space=pltpu.VMEM)],
        out_specs=pl.BlockSpec(memory_space=pltpu.VMEM),
        scratch_shapes=[
            pltpu.VMEM((D, D), jnp.float32),
            pltpu.VMEM((D, D), jnp.float32),
            pltpu.VMEM((D, 3 * D), jnp.bfloat16),
            pltpu.VMEM((3 * D, D), jnp.bfloat16),
        ],
        compiler_params=pltpu.CompilerParams(vmem_limit_bytes=48 << 20),
        name="newton",
    )(gram_blocks)


def pick_rows(parts, spot):
    most = max(part.shape[0] for part in parts)
    padded = [jnp.pad(part, ((0, most - part.shape[0]), (0, 0))) for part in parts]
    picked = padded[-1]
    for number in reversed(range(len(parts) - 1)):
        picked = jnp.where(spot == number, padded[number], picked)
    return picked


def local_gram(rows):
    tiles = [rows[:, at * GRAM_TILE : (at + 1) * GRAM_TILE] for at in range(D // GRAM_TILE)]
    return jnp.concatenate(
        [
            lax.dot_general(
                tiles[row],
                tiles[column],
                (((0,), (0,)), ((), ())),
                precision=lax.Precision.HIGHEST,
                preferred_element_type=jnp.float32,
            )
            for row, column in GRAM_SPOTS
        ],
        axis=0,
    )


def muon_rows(weights, moments, gradients):
    spot = lax.axis_index("narrow")
    moment_next = tuple(
        MUON_MU * moment + (1.0 - MUON_MU) * gradient
        for moment, gradient in zip(moments, gradients)
    )
    updates = tuple(
        (1.0 - MUON_MU) * gradient + MUON_MU * moment
        for moment, gradient in zip(moment_next, gradients)
    )
    rows = pick_rows(updates, spot)
    factor = newton_product(sum_gram(local_gram(rows)))
    ortho = exact_times(rows, factor).astype(jnp.bfloat16)
    pair = jnp.stack([ortho, swap(ortho, 2)])
    quad = jnp.concatenate([pair, swap(pair, 1)], axis=0)
    place = np.array([0, 2, 1, 3])
    rows_whole = (3 * D, D, FF, FF)
    updated = []
    for number, weight in enumerate(weights):
        mine = lax.dynamic_index_in_dim(quad, jnp.asarray(place)[spot ^ number], 0, keepdims=False)
        mine = mine[: weight.shape[0]].astype(jnp.float32)
        rate = MUON_RATE * SHAPE_FACTOR * math.sqrt(max(rows_whole[number], D))
        updated.append(weight * (1.0 - MUON_RATE * MUON_DECAY) - rate * mine)
    return tuple(updated), moment_next


def adam_step(weight, mean_state, square, gradient, step_rate, decay_rate, step_count):
    mean_next = ADAM_BETA1 * mean_state + (1.0 - ADAM_BETA1) * gradient
    square_next = ADAM_BETA2 * square + (1.0 - ADAM_BETA2) * gradient * gradient
    step_float = step_count.astype(jnp.float32)
    mean_hat = mean_next / (1.0 - ADAM_BETA1**step_float)
    square_hat = square_next / (1.0 - ADAM_BETA2**step_float)
    updated = weight - step_rate * (
        mean_hat / (jnp.sqrt(square_hat) + ADAM_EPS) + decay_rate * weight
    )
    return (updated, mean_next, square_next)


def on_device(
    codons,
    offsets,
    positions,
    targets,
    table_weight,
    attend_weight,
    mixing_weight,
    expand_weight,
    reduce_weight,
    vector_params,
    attend_moment,
    mixing_moment,
    expand_moment,
    reduce_moment,
    table_mean,
    table_square,
    vector_mean,
    vector_square,
    step_count,
):
    low_type = jnp.bfloat16
    wide_at = lax.axis_index("wide")
    me = my_index()
    devices = lax.axis_size(BOTH)
    all_masks = wide_masks() + [2, 1]
    small = gather_wide(jnp.concatenate([table_weight, vector_params], axis=0).astype(low_type))
    small = jnp.transpose(small, (1, 0, 2)).reshape(VOCAB + 15, D)
    table_low = small[:VOCAB]
    vector_full = small[VOCAB:].astype(jnp.float32)
    gain_one = vector_full[0]
    bias_one = vector_full[1]
    gain_two = vector_full[2]
    bias_two = vector_full[3]
    gain_last = vector_full[4]
    bias_last = vector_full[5]
    attend_bias = vector_full[6:9].reshape(3 * D)
    mixing_bias = vector_full[9]
    reduce_bias = vector_full[10]
    expand_bias = out_of_order(
        vector_full[11:15].reshape(devices, FF // devices), all_masks, 1, me
    ).reshape(FF)
    embed_scale = math.sqrt(D)
    table_stream = embed_scale * table_low.astype(jnp.float32)
    table_normed = norm_forward(table_stream, gain_one, bias_one)[0].astype(low_type)
    attend_own = attend_weight.astype(low_type)
    table_own = times_trans(table_normed, attend_own)
    table_heads = jnp.transpose(gather_wide(table_own), (1, 0, 2)).reshape(VOCAB, 3 * D)
    table_heads = table_heads + attend_bias

    mixing_low = gather_blocks(quarter_rows(mixing_weight).astype(low_type)[None], all_masks)
    mixing_low = in_order(mixing_low, all_masks, 1, me).reshape(D, D)
    expand_low = gather_blocks(quarter_rows(expand_weight).astype(low_type), all_masks)
    reduce_low = gather_blocks(quarter_rows(reduce_weight).astype(low_type), all_masks)
    attend_low = gather_blocks(quarter_rows(attend_weight).astype(low_type)[None], all_masks)
    attend_low = in_order(attend_low, all_masks, 1, me).reshape(3 * D, D)

    seq_count = codons.shape[0]
    row_count = seq_count * SEQ_LEN
    window = jax.vmap(partial(lax.dynamic_slice_in_dim, slice_size=SEQ_LEN))(codons, offsets)
    vocab_ids = jnp.arange(VOCAB, dtype=jnp.int32)
    token_hot = window.reshape(row_count)[:, None] == vocab_ids[None, :]
    token_low = token_hot.astype(low_type)
    target_hot = (targets.reshape(row_count)[:, None] == vocab_ids[None, :]).astype(jnp.float32)
    stream = embed_scale * times_plain(token_low, table_low)
    heads_high, heads_low = split_two(table_heads)
    projected = times_plain(
        jnp.concatenate([token_low, token_low], axis=1),
        jnp.concatenate([heads_high, heads_low], axis=0),
    )
    cosine, sine_table = rotary_tables(positions)
    head_shape = (seq_count, SEQ_LEN, HEADS, HEAD_DIM)
    query_rot = rotate(projected[:, :D].reshape(head_shape), cosine, sine_table).astype(low_type)
    key_rot = rotate(projected[:, D : 2 * D].reshape(head_shape), cosine, sine_table).astype(
        low_type
    )
    value_low = projected[:, 2 * D :].reshape(head_shape).astype(low_type)
    query_heads = jnp.transpose(query_rot, (2, 0, 1, 3))
    key_heads = jnp.transpose(key_rot, (2, 0, 1, 3))
    value_heads = jnp.transpose(value_low, (2, 0, 1, 3))
    mixed_heads, log_totals = lax.map(attend_head, (query_heads, key_heads, value_heads))
    mixed_low = jnp.transpose(mixed_heads, (1, 2, 0, 3)).reshape(row_count, D).astype(low_type)
    branch = times_trans(mixed_low, mixing_low) + mixing_bias
    middle = stream + branch
    normed_two, normal_two, inverse_two = norm_forward(middle, gain_two, bias_two)
    normed_two_low = normed_two.astype(low_type)
    hidden_pre = times_trans(normed_two_low, expand_low) + expand_bias
    hidden_act, gelu_back = jax.vjp(partial(jax.nn.gelu, approximate=False), hidden_pre)
    hidden_low = hidden_act.astype(low_type)
    feed_out = times_plain(hidden_low, reduce_low) + reduce_bias
    output = middle + feed_out
    final_norm, normal_last, inverse_last = norm_forward(output, gain_last, bias_last)
    final_low = final_norm.astype(low_type)
    logits = times_trans(final_low, table_low)
    row_peak = jnp.max(logits, axis=-1, keepdims=True)
    shifted = jnp.exp(logits - row_peak)
    prob_rows = shifted / jnp.sum(shifted, axis=-1, keepdims=True)
    prob_sum = jnp.sum(prob_rows, axis=0)
    logit_grad = (prob_rows - target_hot).astype(low_type)
    final_grad = times_plain(logit_grad, table_low)
    table_head = trans_times(logit_grad, final_low)
    output_grad, gain_last_grad, bias_last_grad = norm_backward(
        final_grad, normal_last, inverse_last, gain_last
    )
    feed_low = output_grad.astype(low_type)
    reduce_bias_grad = jnp.sum(feed_low, axis=0, dtype=jnp.float32)
    scatter_masks = list(reversed(all_masks))
    half_ff = FF // 2
    reduce_part = scatter_blocks(
        trans_times(hidden_low[:, :half_ff], feed_low),
        trans_times(hidden_low[:, half_ff:], feed_low),
        scatter_masks,
        jnp.float32,
    )
    reduce_total = narrow_rows(reduce_part)
    hidden_grad = times_trans(feed_low, reduce_low)
    pre_grad = gelu_back(hidden_grad)[0].astype(low_type)
    expand_bias_grad = jnp.sum(pre_grad, axis=0, dtype=jnp.float32)
    expand_bias_grad = in_order(
        expand_bias_grad.reshape(devices, FF // devices), all_masks, 1, me
    )
    expand_part = scatter_blocks(
        trans_times(pre_grad[:, :half_ff], normed_two_low),
        trans_times(pre_grad[:, half_ff:], normed_two_low),
        scatter_masks,
        jnp.float32,
    )
    expand_total = narrow_rows(expand_part)
    normed_two_grad = times_plain(pre_grad, expand_low)
    middle_part, gain_two_grad, bias_two_grad = norm_backward(
        normed_two_grad, normal_two, inverse_two, gain_two
    )
    middle_grad = output_grad + middle_part
    branch_low = middle_grad.astype(low_type)
    mixing_bias_grad = jnp.sum(branch_low, axis=0, dtype=jnp.float32)
    mixing_grad = trans_times(branch_low, mixed_low).reshape(devices, D // devices, D)
    mixing_grad = out_of_order(mixing_grad, all_masks, 1, me)
    mixing_part = scatter_blocks(
        mixing_grad[: devices // 2], mixing_grad[devices // 2 :], scatter_masks, jnp.float32
    )
    mixing_total = narrow_rows(mixing_part[0])
    mixed_grad = times_plain(branch_low, mixing_low).astype(low_type)
    grad_heads = jnp.transpose(mixed_grad.reshape(head_shape), (2, 0, 1, 3))
    query_back, key_back, value_back = lax.map(
        attend_back, (query_heads, key_heads, value_heads, grad_heads, log_totals)
    )
    query_grad = unrotate(jnp.transpose(query_back, (1, 2, 0, 3)), cosine, sine_table).reshape(
        row_count, D
    )
    key_grad = unrotate(jnp.transpose(key_back, (1, 2, 0, 3)), cosine, sine_table).reshape(
        row_count, D
    )
    value_grad = jnp.transpose(value_back, (1, 2, 0, 3)).reshape(row_count, D)
    projected_low = jnp.concatenate([query_grad, key_grad, value_grad], axis=1).astype(low_type)
    attend_bias_grad = jnp.sum(projected_low, axis=0, dtype=jnp.float32)
    wide_size = lax.axis_size("wide")
    token_sums = trans_times(token_low, projected_low)
    token_sums = jnp.transpose(token_sums.reshape(VOCAB, wide_size, 3 * D // wide_size), (1, 0, 2))
    token_sums = sum_small(token_sums)
    attend_total = lax.dot_general(
        token_sums,
        table_normed.astype(jnp.float32),
        (((0,), (0,)), ((), ())),
        precision=lax.Precision.HIGHEST,
        preferred_element_type=jnp.float32,
    )
    normed_one_grad = times_plain(projected_low, attend_low)
    normed_one, normal_one, inverse_one = norm_forward(stream, gain_one, bias_one)
    stream_part, gain_one_grad, bias_one_grad = norm_backward(
        normed_one_grad, normal_one, inverse_one, gain_one
    )
    entry_gradient = middle_grad + stream_part
    table_grad = (
        embed_scale * exact_times(token_hot.astype(jnp.float32).T, entry_gradient) + table_head
    )
    vector_grad = jnp.concatenate(
        [
            jnp.stack(
                [
                    gain_one_grad,
                    bias_one_grad,
                    gain_two_grad,
                    bias_two_grad,
                    gain_last_grad,
                    bias_last_grad,
                ]
            ),
            attend_bias_grad.reshape(3, D),
            mixing_bias_grad[None, :],
            reduce_bias_grad[None, :],
            expand_bias_grad.reshape(4, D),
        ],
        axis=0,
    )
    columns = D // wide_size
    rows_hist = -(-VOCAB // columns)
    hist_part = jnp.pad(prob_sum, (0, rows_hist * columns - VOCAB)).reshape(rows_hist, columns)
    small_grads = jnp.concatenate([table_grad, vector_grad], axis=0)
    small_grads = jnp.transpose(small_grads.reshape(VOCAB + 15, wide_size, columns), (1, 0, 2))
    small_grads = jnp.concatenate(
        [small_grads, jnp.broadcast_to(hist_part, (wide_size, rows_hist, columns))], axis=1
    )
    small_total = sum_small(small_grads)
    table_total = small_total[:VOCAB]
    vector_total = small_total[VOCAB : VOCAB + 15]
    prob_total = small_total[VOCAB + 15 :].reshape(rows_hist * columns)[:VOCAB]
    histogram = prob_total * (VOCAB / (row_count * devices))
    totals = (attend_total, mixing_total, expand_total, reduce_total)
    matrix_new, moment_next = muon_rows(
        (attend_weight, mixing_weight, expand_weight, reduce_weight),
        (attend_moment, mixing_moment, expand_moment, reduce_moment),
        totals,
    )
    table_new, table_mean_next, table_square_next = adam_step(
        table_weight, table_mean, table_square, table_total, TABLE_RATE, TABLE_DECAY, step_count
    )
    vector_new, vector_mean_next, vector_square_next = adam_step(
        vector_params, vector_mean, vector_square, vector_total, VECTOR_RATE, 0.0, step_count
    )
    results = (
        totals
        + (table_total, vector_total)
        + matrix_new
        + moment_next
        + (
            table_new,
            table_mean_next,
            table_square_next,
            vector_new,
            vector_mean_next,
            vector_square_next,
        )
    )
    block_output = output.astype(low_type).reshape(seq_count, SEQ_LEN, D)
    return (block_output, entry_gradient.reshape(seq_count, SEQ_LEN, D)) + results + (histogram,)


def solution(mesh):
    in_specs = (
        P(("wide", "narrow"), None),
        P(("wide", "narrow")),
        P(("wide", "narrow"), None),
        P(("wide", "narrow"), None),
        P(None, "wide"),
        P("wide", None),
        P("wide", None),
        P("wide", None),
        P("wide", None),
        P(None, "wide"),
        P("wide", None),
        P("wide", None),
        P("wide", None),
        P("wide", None),
        P(None, "wide"),
        P(None, "wide"),
        P(None, "wide"),
        P(None, "wide"),
        P(),
    )
    out_specs = (
        P(("wide", "narrow"), None, None),
        P(("wide", "narrow"), None, None),
        P("wide", None),
        P("wide", None),
        P("wide", None),
        P("wide", None),
        P(None, "wide"),
        P(None, "wide"),
        P("wide", None),
        P("wide", None),
        P("wide", None),
        P("wide", None),
        P("wide", None),
        P("wide", None),
        P("wide", None),
        P("wide", None),
        P(None, "wide"),
        P(None, "wide"),
        P(None, "wide"),
        P(None, "wide"),
        P(None, "wide"),
        P(None, "wide"),
        P(),
    )
    return jax.shard_map(
        on_device, mesh=mesh, in_specs=in_specs, out_specs=out_specs, check_vma=False
    )
```

```python
from functools import partial
import math

import jax
import jax.numpy as jnp
import numpy as np
from jax import lax
from jax.experimental import pallas as pl
from jax.experimental.pallas import tpu as pltpu
from jax.sharding import PartitionSpec as P

D = 768
HEADS = 12
HEAD_DIM = 64
FF = 3072
VOCAB = 70
SEQ_LEN = 912
NS_ITERS = 5


NORM_EPS = 1e-05
ROPE_BASE = 10000.0
NEWTON_A = 3.4445
NEWTON_B = -4.775
NEWTON_C = 2.0315
MUON_MU = 0.95
MUON_RATE = 0.3
MUON_DECAY = 0.1
SHAPE_FACTOR = 0.2
ADAM_BETA1 = 0.9
ADAM_BETA2 = 0.95
ADAM_EPS = 1e-08
TABLE_RATE = 0.03
TABLE_DECAY = 0.01
VECTOR_RATE = 0.2


def times_plain(left_side, right_side):
    return jnp.dot(left_side, right_side, preferred_element_type=jnp.float32)


def times_trans(left_side, right_side):
    return lax.dot_general(
        left_side, right_side, (((1,), (1,)), ((), ())), preferred_element_type=jnp.float32
    )


def trans_times(left_side, right_side):
    return lax.dot_general(
        left_side, right_side, (((0,), (0,)), ((), ())), preferred_element_type=jnp.float32
    )


def exact_times(left_side, right_side):
    return jnp.dot(
        left_side, right_side, precision=lax.Precision.HIGHEST, preferred_element_type=jnp.float32
    )


def norm_forward(values, gain_row, bias_row):
    center = values - jnp.mean(values, axis=-1, keepdims=True)
    spread = jnp.mean(center * center, axis=-1, keepdims=True)
    inverse = lax.rsqrt(spread + NORM_EPS)
    normal = center * inverse
    return (normal * gain_row + bias_row, normal, inverse)


def norm_backward(upstream, normal, inverse, gain_row):
    scaled = upstream * gain_row
    inner_part = (
        scaled
        - jnp.mean(scaled, axis=-1, keepdims=True)
        - normal * jnp.mean(scaled * normal, axis=-1, keepdims=True)
    )
    return (inverse * inner_part, jnp.sum(upstream * normal, axis=0), jnp.sum(upstream, axis=0))


def rotary_tables(positions):
    half_dim = HEAD_DIM // 2
    frequency = ROPE_BASE ** (-(jnp.arange(half_dim, dtype=jnp.float32) * 2.0 / HEAD_DIM))
    turned = positions.astype(jnp.float32)[..., None] * frequency
    return (jnp.cos(turned), jnp.sin(turned))


PAIR = 2 * HEAD_DIM
SPAN = 1024
STRIP = 256
PARTS = 4
LANES = 128
ATTEND_CALLS = 3


BOTH = ("wide", "narrow")
GRAM_TILE = 256
GRAM_SPOTS = ((0, 0), (0, 1), (0, 2), (1, 1), (1, 2), (2, 2))


def swap(value, mask):
    total = lax.axis_size(BOTH)
    return lax.ppermute(value, BOTH, [(spot, spot ^ mask) for spot in range(total)])


def my_index():
    return lax.axis_index("wide") * lax.axis_size("narrow") + lax.axis_index("narrow")


def wide_masks():
    narrow_size = lax.axis_size("narrow")
    count = lax.axis_size("wide").bit_length() - 1
    return [narrow_size << bit for bit in reversed(range(count))]


def offsets_of(masks):
    table = [0]
    for mask in masks:
        table = table + [offset ^ mask for offset in table]
    return np.array(table)


def gather_blocks(piece, masks):
    for mask in masks:
        piece = jnp.concatenate([piece, swap(piece, mask)], axis=0)
    return piece


def take_blocks(array, index):
    return jnp.take(array, index, axis=0, mode="clip")


def in_order(blocks, masks, unit, base):
    offsets = offsets_of(masks) // unit
    place = np.zeros_like(offsets)
    place[offsets] = np.arange(offsets.size)
    return take_blocks(blocks, jnp.asarray(place)[jnp.arange(offsets.size) ^ base])


def out_of_order(blocks, masks, unit, base):
    offsets = offsets_of(masks) // unit
    return take_blocks(blocks, jnp.asarray(offsets) ^ base)


def gather_wide(piece):
    blocks = gather_blocks(piece[None], wide_masks())
    return in_order(blocks, wide_masks(), lax.axis_size("narrow"), lax.axis_index("wide"))


def gather_parts(piece):
    own = gather_blocks(piece, wide_masks())
    beside = swap(own, 2)
    return [own, beside, swap(own, 1), swap(beside, 1)]


def quarter_rows(array):
    count = array.shape[0] // lax.axis_size("narrow")
    return lax.dynamic_slice_in_dim(array, lax.axis_index("narrow") * count, count, 0)


def scatter_blocks(keep, send, masks, wide_type):
    for step, mask in enumerate(masks):
        send_type = wide_type if step + 2 >= len(masks) else jnp.bfloat16
        total = keep + swap(send.astype(send_type), mask).astype(jnp.float32)
        half = total.shape[0] // 2
        keep, send = total[:half], total[half:]
    return total


def narrow_rows(piece):
    spot = lax.axis_index("narrow")
    other = swap(piece, 2)
    pair = jnp.where(spot // 2 == 0, jnp.stack([piece, other]), jnp.stack([other, piece]))
    other = swap(pair, 1)
    quad = jnp.where(
        spot % 2 == 0, jnp.stack([pair, other], axis=1), jnp.stack([other, pair], axis=1)
    )
    return quad.reshape(4 * piece.shape[0], piece.shape[1])


def sum_small(blocks):
    masks = wide_masks()
    blocks = blocks + swap(blocks, 1)
    blocks = out_of_order(blocks, masks, lax.axis_size("narrow"), lax.axis_index("wide"))
    for mask in reversed(masks):
        half = blocks.shape[0] // 2
        blocks = blocks[:half] + swap(blocks[half:], mask)
    piece = blocks[0]
    return piece + swap(piece, 2)


def sum_gram(blocks):
    wide_at = lax.axis_index("wide")
    narrow_size = lax.axis_size("narrow")
    masks = wide_masks()
    bits = [(mask // narrow_size).bit_length() - 1 for mask in masks]
    order = list(zip(masks, bits))
    order = list(reversed(order))
    for mask, bit in order:
        side = (wide_at >> bit) % 2
        half = blocks.shape[0] // 2
        keep = lax.dynamic_slice_in_dim(blocks, side * half, half, 0)
        send = lax.dynamic_slice_in_dim(blocks, (1 - side) * half, half, 0)
        blocks = keep + swap(send, mask)
    for mask, bit in reversed(order):
        side = (wide_at >> bit) % 2
        other = swap(blocks, mask)
        blocks = jnp.where(
            side == 0,
            jnp.concatenate([blocks, other], axis=0),
            jnp.concatenate([other, blocks], axis=0),
        )
    return blocks


def row_dot(left_side, right_side):
    return lax.dot_general(
        left_side, right_side, (((1,), (1,)), ((), ())), preferred_element_type=jnp.float32
    )


def split_two(values):
    high = values.astype(jnp.bfloat16)
    return high, (values - high.astype(jnp.float32)).astype(jnp.bfloat16)


def newton_kernel(gram_ref, rows_ref, out_ref, gram_now, other, left, right, rows_left):
    tile = GRAM_TILE
    count = rows_ref.shape[0]
    trace = jnp.zeros((1, 1), jnp.float32)
    diagonal = lax.broadcasted_iota(jnp.int32, (tile, tile), 0) == lax.broadcasted_iota(
        jnp.int32, (tile, tile), 1
    )
    for number, (row, column) in enumerate(GRAM_SPOTS):
        if row == column:
            picked = jnp.where(diagonal, gram_ref[number * tile : (number + 1) * tile, :], 0.0)
            trace = trace + jnp.sum(jnp.sum(picked, axis=0, keepdims=True), axis=1, keepdims=True)
    inverse = 1.0 / (jnp.sqrt(trace) + 1e-07)
    scale = inverse * inverse

    def span(number):
        return slice(number * tile, (number + 1) * tile)

    for number, (row, column) in enumerate(GRAM_SPOTS):
        block = gram_ref[span(number), :] * scale
        gram_now[span(row), span(column)] = block
        if row != column:
            gram_now[span(column), span(row)] = block.T

    def set_left(values):
        high, low = split_two(values)
        left[:, 0:D] = high
        left[:, D : 2 * D] = high
        left[:, 2 * D : 3 * D] = low

    def set_right(values):
        high, low = split_two(values)
        right[0:D, :] = high
        right[D : 2 * D, :] = low
        right[2 * D : 3 * D, :] = high

    def set_rows(values):
        high, low = split_two(values)
        rows_left[:, 0:D] = high
        rows_left[:, D : 2 * D] = high
        rows_left[:, 2 * D : 3 * D] = low

    def product(target, finish):
        for column in range(D // tile):
            rows = (column + 1) * tile
            block = jnp.dot(left[0:rows, :], right[:, span(column)], preferred_element_type=jnp.float32)
            for row in range(column + 1):
                piece = finish(block[span(row), :], row, column)
                target[span(row), span(column)] = piece
                if row != column:
                    target[span(column), span(row)] = piece.T

    def same(block, row, column):
        return block

    def factor(block, row, column):
        block = NEWTON_B * gram_now[span(row), span(column)] + NEWTON_C * block
        if row == column:
            block = block + jnp.where(diagonal, NEWTON_A, 0.0)
        return block

    def set_factor():
        set_left(gram_now[...])
        set_right(gram_now[...])
        product(other, factor)
        set_right(other[...])

    def rows_product():
        return jnp.dot(rows_left[...], right[...], preferred_element_type=jnp.float32)

    set_rows(rows_ref[...] * inverse)

    def body(step, carry):
        set_factor()
        product(other, same)
        set_left(other[...])
        product(gram_now, same)
        set_rows(rows_product())
        return carry

    lax.fori_loop(0, NS_ITERS - 1, body, 0)
    set_factor()
    out_ref[...] = rows_product().astype(out_ref.dtype)


def newton_rows(gram_blocks, rows):
    count = rows.shape[0]
    return pl.pallas_call(
        newton_kernel,
        out_shape=jax.ShapeDtypeStruct((count, D), jnp.bfloat16),
        in_specs=[pl.BlockSpec(memory_space=pltpu.VMEM)] * 2,
        out_specs=pl.BlockSpec(memory_space=pltpu.VMEM),
        scratch_shapes=[
            pltpu.VMEM((D, D), jnp.float32),
            pltpu.VMEM((D, D), jnp.float32),
            pltpu.VMEM((D, 3 * D), jnp.bfloat16),
            pltpu.VMEM((3 * D, D), jnp.bfloat16),
            pltpu.VMEM((count, 3 * D), jnp.bfloat16),
        ],
        compiler_params=pltpu.CompilerParams(vmem_limit_bytes=48 << 20),
        cost_estimate=pl.CostEstimate(flops=60 * D * D * D, bytes_accessed=4 << 20, transcendentals=0),
        name="newton",
    )(gram_blocks, rows)


def pick_rows(parts, spot):
    most = max(part.shape[0] for part in parts)
    padded = [jnp.pad(part, ((0, most - part.shape[0]), (0, 0))) for part in parts]
    picked = padded[-1]
    for number in reversed(range(len(parts) - 1)):
        picked = jnp.where(spot == number, padded[number], picked)
    return picked


def local_gram(rows):
    tiles = [rows[:, at * GRAM_TILE : (at + 1) * GRAM_TILE] for at in range(D // GRAM_TILE)]
    return jnp.concatenate(
        [
            lax.dot_general(
                tiles[row],
                tiles[column],
                (((0,), (0,)), ((), ())),
                precision=lax.Precision.HIGHEST,
                preferred_element_type=jnp.float32,
            )
            for row, column in GRAM_SPOTS
        ],
        axis=0,
    )


def muon_rows(weights, moments, gradients):
    spot = lax.axis_index("narrow")
    moment_next = tuple(
        MUON_MU * moment + (1.0 - MUON_MU) * gradient
        for moment, gradient in zip(moments, gradients)
    )
    updates = tuple(
        (1.0 - MUON_MU) * gradient + MUON_MU * moment
        for moment, gradient in zip(moment_next, gradients)
    )
    rows = pick_rows(updates, spot)
    ortho = newton_rows(sum_gram(local_gram(rows)), rows)
    pair = jnp.stack([ortho, swap(ortho, 2)])
    quad = jnp.concatenate([pair, swap(pair, 1)], axis=0)
    place = np.array([0, 2, 1, 3])
    rows_whole = (3 * D, D, FF, FF)
    updated = []
    for number, weight in enumerate(weights):
        mine = lax.dynamic_index_in_dim(quad, jnp.asarray(place)[spot ^ number], 0, keepdims=False)
        mine = mine[: weight.shape[0]].astype(jnp.float32)
        rate = MUON_RATE * SHAPE_FACTOR * math.sqrt(max(rows_whole[number], D))
        updated.append(weight * (1.0 - MUON_RATE * MUON_DECAY) - rate * mine)
    return tuple(updated), moment_next


def turn(values, cosine, sine_table):
    lane = lax.broadcasted_iota(jnp.int32, values.shape, 1)
    half = HEAD_DIM // 2
    partner = jnp.where(
        lane % HEAD_DIM < half,
        pltpu.roll(values, PAIR - half, 1),
        pltpu.roll(values, half, 1),
    )
    return values * cosine + partner * sine_table


def attend_kernel(
    hot_ref, tq_ref, tk_ref, tv_ref, cos_ref, sin_ref,
    q_ref, k_ref, v_ref, mixed_ref, log_ref,
    q_all, v_turned, mixed_turned, prob_all,
):
    hot = hot_ref[...]
    cosine = cos_ref[...]
    sine_table = sin_ref[...]
    queries = jnp.dot(hot, tq_ref[...], preferred_element_type=jnp.float32)
    queries = turn(queries, cosine, sine_table).astype(jnp.bfloat16) * HEAD_DIM ** (-0.5)
    queries = queries.astype(jnp.bfloat16)
    q_ref[...] = queries
    q_all[0:SEQ_LEN, :] = queries
    q_all[SEQ_LEN:SPAN, :] = jnp.zeros((SPAN - SEQ_LEN, PAIR), jnp.bfloat16)
    keys = jnp.dot(hot, tk_ref[...], preferred_element_type=jnp.float32)
    keys = turn(keys, cosine, sine_table).astype(jnp.bfloat16)
    k_ref[...] = keys
    values = jnp.dot(hot, tv_ref[...], preferred_element_type=jnp.float32)
    v_ref[...] = values.astype(jnp.bfloat16)
    v_turned[...] = values.T.astype(jnp.bfloat16)

    for head in range(2):
        lane = lax.broadcasted_iota(jnp.int32, (SEQ_LEN, PAIR), 1)
        keys_head = jnp.where(lane // HEAD_DIM == head, k_ref[...], jnp.zeros((), jnp.bfloat16))
        values_head = v_turned[head * HEAD_DIM : (head + 1) * HEAD_DIM, :]

        def body(step, carry):
            at = pl.multiple_of(step * STRIP, STRIP)
            scores = row_dot(keys_head, q_all[pl.ds(at, STRIP), :])
            peak = jnp.max(scores, axis=0, keepdims=True)
            powers = jnp.exp(scores - peak)
            total = jnp.sum(powers, axis=0, keepdims=True)
            prob_low = (powers * (1.0 / total)).astype(jnp.bfloat16)
            prob_all[:, pl.ds(at, STRIP)] = prob_low
            log_ref[0, head : head + 1, pl.ds(at, STRIP)] = peak + jnp.log(total)
            return carry

        lax.fori_loop(0, SPAN // STRIP, body, 0)
        mixed_turned[head * HEAD_DIM : (head + 1) * HEAD_DIM, :] = jnp.dot(
            values_head, prob_all[...], preferred_element_type=jnp.float32)
    mixed_ref[...] = mixed_turned[...].T[0:SEQ_LEN, :].astype(jnp.bfloat16)


def attend_call(hot, tables, cosine, sine_table, first, count):
    whole = lambda step: (0, 0)
    source = lambda step: (0, step + first)
    own = lambda step: (0, step)
    rows_low = jax.ShapeDtypeStruct((SEQ_LEN, count * PAIR), jnp.bfloat16)
    return pl.pallas_call(
        attend_kernel,
        grid=(count,),
        in_specs=[
            pl.BlockSpec(hot.shape, whole),
            pl.BlockSpec((hot.shape[1], PAIR), source),
            pl.BlockSpec((hot.shape[1], PAIR), lambda step: (0, step + first + D // PAIR)),
            pl.BlockSpec((hot.shape[1], PAIR), lambda step: (0, step + first + 2 * D // PAIR)),
            pl.BlockSpec((SEQ_LEN, PAIR), whole),
            pl.BlockSpec((SEQ_LEN, PAIR), whole),
        ],
        out_specs=[
            pl.BlockSpec((SEQ_LEN, PAIR), own),
            pl.BlockSpec((SEQ_LEN, PAIR), own),
            pl.BlockSpec((SEQ_LEN, PAIR), own),
            pl.BlockSpec((SEQ_LEN, PAIR), own),
            pl.BlockSpec((1, 2, SPAN), lambda step: (step, 0, 0)),
        ],
        out_shape=[rows_low] * 4 + [jax.ShapeDtypeStruct((count, 2, SPAN), jnp.float32)],
        scratch_shapes=[
            pltpu.VMEM((SPAN, PAIR), jnp.bfloat16),
            pltpu.VMEM((PAIR, SEQ_LEN), jnp.bfloat16),
            pltpu.VMEM((PAIR, SPAN), jnp.float32),
            pltpu.VMEM((SEQ_LEN, SPAN), jnp.bfloat16),
        ],
        compiler_params=pltpu.CompilerParams(vmem_limit_bytes=40 << 20),
        cost_estimate=pl.CostEstimate(
            flops=count * 8 * SPAN * SPAN * 256, bytes_accessed=count * 2 << 20,
            transcendentals=count * 2 * SPAN * SEQ_LEN,
        ),
        name="attend",
    )(hot, tables, tables, tables, cosine, sine_table)


def attend_back_kernel(
    hot_ref, q_ref, k_ref, v_ref, grad_ref, log_ref, cos_ref, sin_ref,
    low_ref, sums_ref,
    q_all, grad_all, k_turned, prob_all, score_all, query_turned, key_sum, value_sum,
):
    rest = jnp.zeros((SPAN - SEQ_LEN, PAIR), jnp.bfloat16)
    q_all[0:SEQ_LEN, :] = q_ref[...]
    q_all[SEQ_LEN:SPAN, :] = rest
    grad_all[0:SEQ_LEN, :] = grad_ref[...]
    grad_all[SEQ_LEN:SPAN, :] = rest
    k_turned[...] = k_ref[...].astype(jnp.float32).T.astype(jnp.bfloat16)
    lane = lax.broadcasted_iota(jnp.int32, (SEQ_LEN, PAIR), 1)
    none = jnp.zeros((), jnp.bfloat16)

    for head in range(2):
        keys_head = jnp.where(lane // HEAD_DIM == head, k_ref[...], none)
        values_head = jnp.where(lane // HEAD_DIM == head, v_ref[...], none)

        def body(step, carry):
            at = pl.multiple_of(step * STRIP, STRIP)
            scores = row_dot(keys_head, q_all[pl.ds(at, STRIP), :])
            prob_rows = jnp.exp(scores - log_ref[0, head : head + 1, pl.ds(at, STRIP)])
            prob_all[:, pl.ds(at, STRIP)] = prob_rows.astype(jnp.bfloat16)
            prob_grad = row_dot(values_head, grad_all[pl.ds(at, STRIP), :])
            delta = jnp.sum(prob_grad * prob_rows, axis=0, keepdims=True)
            score_all[:, pl.ds(at, STRIP)] = (prob_rows * (prob_grad - delta)).astype(jnp.bfloat16)
            return carry

        lax.fori_loop(0, SPAN // STRIP, body, 0)
        value_part = jnp.dot(prob_all[...], grad_all[...], preferred_element_type=jnp.float32)
        key_part = jnp.dot(score_all[...], q_all[...], preferred_element_type=jnp.float32)
        if head == 0:
            value_sum[...] = value_part
            key_sum[...] = key_part
        else:
            value_sum[...] = jnp.where(lane < HEAD_DIM, value_sum[...], value_part)
            key_sum[...] = jnp.where(lane < HEAD_DIM, key_sum[...], key_part)
        query_turned[head * HEAD_DIM : (head + 1) * HEAD_DIM, :] = jnp.dot(
            k_turned[head * HEAD_DIM : (head + 1) * HEAD_DIM, :],
            score_all[...],
            preferred_element_type=jnp.float32,
        ) * HEAD_DIM ** (-0.5)
    cosine = cos_ref[...]
    sine_table = -sin_ref[...]
    hot = hot_ref[...]
    query_low = turn(query_turned[...].T[0:SEQ_LEN, :], cosine, sine_table).astype(jnp.bfloat16)
    key_low = turn(key_sum[...], cosine, sine_table).astype(jnp.bfloat16)
    value_low = value_sum[...].astype(jnp.bfloat16)
    for number, low in enumerate((query_low, key_low, value_low)):
        low_ref[number] = low
        sums_ref[number] = jnp.dot(hot, low, preferred_element_type=jnp.float32)


def attend_back_call(hot_turned, queries, keys, values, gradients, logs, cosine, sine_table, first):
    count = logs.shape[0]
    whole = lambda step: (0, 0)
    own = lambda step: (0, step)
    rows = pl.BlockSpec((SEQ_LEN, PAIR), own)
    whole_rows = pl.BlockSpec((SEQ_LEN, PAIR), whole)
    return pl.pallas_call(
        attend_back_kernel,
        grid=(count,),
        in_specs=[
            pl.BlockSpec(hot_turned.shape, whole),
            rows,
            rows,
            rows,
            pl.BlockSpec((SEQ_LEN, PAIR), lambda step: (0, step + first)),
            pl.BlockSpec((1, 2, SPAN), lambda step: (step, 0, 0)),
            whole_rows,
            whole_rows,
        ],
        out_specs=[
            pl.BlockSpec((3, SEQ_LEN, PAIR), lambda step: (0, 0, step)),
            pl.BlockSpec((3, hot_turned.shape[0], PAIR), lambda step: (0, 0, step)),
        ],
        out_shape=[
            jax.ShapeDtypeStruct((3, SEQ_LEN, count * PAIR), jnp.bfloat16),
            jax.ShapeDtypeStruct((3, hot_turned.shape[0], count * PAIR), jnp.float32),
        ],
        scratch_shapes=[
            pltpu.VMEM((SPAN, PAIR), jnp.bfloat16),
            pltpu.VMEM((SPAN, PAIR), jnp.bfloat16),
            pltpu.VMEM((PAIR, SEQ_LEN), jnp.bfloat16),
            pltpu.VMEM((SEQ_LEN, SPAN), jnp.bfloat16),
            pltpu.VMEM((SEQ_LEN, SPAN), jnp.bfloat16),
            pltpu.VMEM((PAIR, SPAN), jnp.float32),
            pltpu.VMEM((SEQ_LEN, PAIR), jnp.float32),
            pltpu.VMEM((SEQ_LEN, PAIR), jnp.float32),
        ],
        compiler_params=pltpu.CompilerParams(vmem_limit_bytes=48 << 20),
        cost_estimate=pl.CostEstimate(
            flops=count * 20 * SPAN * SPAN * 256, bytes_accessed=count * 3 << 20,
            transcendentals=count * 2 * SPAN * SEQ_LEN,
        ),
        name="attend_back",
    )(hot_turned, queries, keys, values, gradients, logs, cosine, sine_table)


ERF_P = 0.3275911
ERF_A = (0.254829592, -0.284496736, 1.421413741, -1.453152027, 1.061405429)

def normal_parts(values):
    size = jnp.abs(values)
    bell = jnp.exp(values * values * -0.5)
    step = 1.0 / (1.0 + (ERF_P * 0.5**0.5) * size)
    series = ERF_A[4]
    for factor in (ERF_A[3], ERF_A[2], ERF_A[1], ERF_A[0]):
        series = series * step + factor
    tail = (0.5 * series) * step * bell
    return jnp.where(values < 0.0, tail, 1.0 - tail), bell * (1.0 / math.sqrt(2.0 * math.pi))

def feed_kernel(rows_ref, bias_ref, e0, e1, e2, e3, r0, r1, r2, r3, hidden_ref, slope_ref, out_ref, expand_held, reduce_held, pre, sems):
    step = pl.program_id(0)
    @pl.when(step == 0)
    def _():
        for number in range(PARTS):
            pltpu.make_async_copy((e0,e1,e2,e3)[number], expand_held.at[number], sems.at[number]).start()
            pltpu.make_async_copy((r0,r1,r2,r3)[number], reduce_held.at[number], sems.at[PARTS + number]).start()
    pltpu.make_async_copy(e0, expand_held.at[step], sems.at[step]).wait()
    for at in range(0, SEQ_LEN, 304):
        spot = slice(at, at + 304)
        values = row_dot(rows_ref[spot, :], expand_held[step]) + bias_ref[...]
        below, bell = normal_parts(values)
        hidden_ref[spot, :] = (values * below).astype(jnp.bfloat16)
        slope_ref[spot, :] = (below + values * bell).astype(jnp.bfloat16)
    pltpu.make_async_copy(r0, reduce_held.at[step], sems.at[PARTS + step]).wait()
    part = jnp.dot(hidden_ref[...], reduce_held[step], preferred_element_type=jnp.float32)
    @pl.when(step == 0)
    def _():
        out_ref[...] = part
    @pl.when(step > 0)
    def _():
        out_ref[...] += part

def feed_call(rows, bias, expands, reduces):
    whole = lambda step: (0, 0)
    chunk = pl.BlockSpec((SEQ_LEN, D), lambda step: (0, step))
    anywhere = pl.BlockSpec(memory_space=pl.ANY)
    return pl.pallas_call(
        feed_kernel, grid=(PARTS,),
        in_specs=[pl.BlockSpec((SEQ_LEN, D), whole), pl.BlockSpec((1, D), lambda step: (0, step))] + [anywhere] * 8,
        out_specs=[chunk, chunk, pl.BlockSpec((SEQ_LEN, D), whole)],
        out_shape=[jax.ShapeDtypeStruct((SEQ_LEN, FF), jnp.bfloat16)] * 2 + [jax.ShapeDtypeStruct((SEQ_LEN, D), jnp.float32)],
        scratch_shapes=[pltpu.VMEM((PARTS, D, D), jnp.bfloat16), pltpu.VMEM((PARTS, D, D), jnp.bfloat16), pltpu.VMEM((SEQ_LEN, D), jnp.float32), pltpu.SemaphoreType.DMA((2 * PARTS,))],
        compiler_params=pltpu.CompilerParams(vmem_limit_bytes=48 << 20),
        cost_estimate=pl.CostEstimate(flops=4 * SEQ_LEN * D * FF, bytes_accessed=24 << 20, transcendentals=SEQ_LEN * FF),
        name="feed",
    )(rows, bias, *expands, *reduces)

def feed_back_kernel(grad_ref, slope_ref, e0, e1, e2, e3, r0, r1, r2, r3, pre_ref, out_ref, bias_ref, expand_held, reduce_held, sems):
    step = pl.program_id(0)
    @pl.when(step == 0)
    def _():
        for number in range(PARTS):
            pltpu.make_async_copy((r0,r1,r2,r3)[number], reduce_held.at[number], sems.at[PARTS + number]).start()
            pltpu.make_async_copy((e0,e1,e2,e3)[number], expand_held.at[number], sems.at[number]).start()
    pltpu.make_async_copy(r0, reduce_held.at[step], sems.at[PARTS + step]).wait()
    total = jnp.zeros((1, D), jnp.float32)
    for at in range(0, SEQ_LEN, 304):
        spot = slice(at, at + 304)
        grad = row_dot(grad_ref[spot, :], reduce_held[step]) * slope_ref[spot, :].astype(jnp.float32)
        low = grad.astype(jnp.bfloat16)
        pre_ref[spot, :] = low
        total = total + jnp.sum(low.astype(jnp.float32), axis=0, keepdims=True)
    bias_ref[...] = total
    low = pre_ref[...]
    pltpu.make_async_copy(e0, expand_held.at[step], sems.at[step]).wait()
    part = jnp.dot(low, expand_held[step], preferred_element_type=jnp.float32)
    @pl.when(step == 0)
    def _():
        out_ref[...] = part
    @pl.when(step > 0)
    def _():
        out_ref[...] += part

def feed_back_call(grad, slope, expands, reduces):
    whole = lambda step: (0, 0)
    chunk = pl.BlockSpec((SEQ_LEN, D), lambda step: (0, step))
    anywhere = pl.BlockSpec(memory_space=pl.ANY)
    return pl.pallas_call(
        feed_back_kernel, grid=(PARTS,),
        in_specs=[pl.BlockSpec((SEQ_LEN, D), whole), chunk] + [anywhere] * 8,
        out_specs=[chunk, pl.BlockSpec((SEQ_LEN, D), whole), pl.BlockSpec((1, D), lambda step: (0, step))],
        out_shape=[jax.ShapeDtypeStruct((SEQ_LEN, FF), jnp.bfloat16), jax.ShapeDtypeStruct((SEQ_LEN, D), jnp.float32), jax.ShapeDtypeStruct((1, FF), jnp.float32)],
        scratch_shapes=[pltpu.VMEM((PARTS, D, D), jnp.bfloat16), pltpu.VMEM((PARTS, D, D), jnp.bfloat16), pltpu.SemaphoreType.DMA((2 * PARTS,))],
        compiler_params=pltpu.CompilerParams(vmem_limit_bytes=48 << 20),
        cost_estimate=pl.CostEstimate(flops=4 * SEQ_LEN * D * FF, bytes_accessed=24 << 20, transcendentals=0),
        name="feed_back",
    )(grad, slope, *expands, *reduces)


def adam_step(weight, mean_state, square, gradient, step_rate, decay_rate, step_count):
    mean_next = ADAM_BETA1 * mean_state + (1.0 - ADAM_BETA1) * gradient
    square_next = ADAM_BETA2 * square + (1.0 - ADAM_BETA2) * gradient * gradient
    step_float = step_count.astype(jnp.float32)
    mean_hat = mean_next / (1.0 - ADAM_BETA1**step_float)
    square_hat = square_next / (1.0 - ADAM_BETA2**step_float)
    updated = weight - step_rate * (
        mean_hat / (jnp.sqrt(square_hat) + ADAM_EPS) + decay_rate * weight
    )
    return (updated, mean_next, square_next)


def on_device(
    codons,
    offsets,
    positions,
    targets,
    table_weight,
    attend_weight,
    mixing_weight,
    expand_weight,
    reduce_weight,
    vector_params,
    attend_moment,
    mixing_moment,
    expand_moment,
    reduce_moment,
    table_mean,
    table_square,
    vector_mean,
    vector_square,
    step_count,
):
    low_type = jnp.bfloat16
    wide_at = lax.axis_index("wide")
    me = my_index()
    devices = lax.axis_size(BOTH)
    all_masks = wide_masks() + [2, 1]
    small = gather_wide(jnp.concatenate([table_weight, vector_params], axis=0).astype(low_type))
    small = jnp.transpose(small, (1, 0, 2)).reshape(VOCAB + 15, D)
    table_low = small[:VOCAB]
    vector_full = small[VOCAB:].astype(jnp.float32)
    gain_one = vector_full[0]
    bias_one = vector_full[1]
    gain_two = vector_full[2]
    bias_two = vector_full[3]
    gain_last = vector_full[4]
    bias_last = vector_full[5]
    attend_bias = vector_full[6:9].reshape(3 * D)
    mixing_bias = vector_full[9]
    reduce_bias = vector_full[10]
    expand_bias = out_of_order(
        vector_full[11:15].reshape(devices, FF // devices), all_masks, 1, me
    ).reshape(FF)
    embed_scale = math.sqrt(D)
    table_stream = embed_scale * table_low.astype(jnp.float32)
    table_normed = norm_forward(table_stream, gain_one, bias_one)[0].astype(low_type)
    attend_own = attend_weight.astype(low_type)
    table_own = times_trans(table_normed, attend_own)
    table_heads = jnp.transpose(gather_wide(table_own), (1, 0, 2)).reshape(VOCAB, 3 * D)
    table_heads = table_heads + attend_bias

    mixing_low = gather_blocks(quarter_rows(mixing_weight).astype(low_type)[None], all_masks)
    mixing_low = in_order(mixing_low, all_masks, 1, me).reshape(D, D)
    expand_parts = gather_parts(quarter_rows(expand_weight).astype(low_type))
    reduce_parts = gather_parts(quarter_rows(reduce_weight).astype(low_type))
    attend_low = gather_blocks(quarter_rows(attend_weight).astype(low_type)[None], all_masks)
    attend_low = in_order(attend_low, all_masks, 1, me).reshape(3 * D, D)

    seq_count = codons.shape[0]
    row_count = seq_count * SEQ_LEN
    window = jax.vmap(partial(lax.dynamic_slice_in_dim, slice_size=SEQ_LEN))(codons, offsets)
    vocab_ids = jnp.arange(VOCAB, dtype=jnp.int32)
    token_hot = window.reshape(row_count)[:, None] == vocab_ids[None, :]
    token_low = token_hot.astype(low_type)
    target_hot = (targets.reshape(row_count)[:, None] == vocab_ids[None, :]).astype(jnp.float32)
    stream = embed_scale * times_plain(token_low, table_low)
    token_ids = window.reshape(row_count)
    lane_ids = jnp.arange(2 * LANES, dtype=jnp.int32) % LANES
    hot = (token_ids[:, None] == lane_ids[None, :]).astype(low_type)
    hot_turned = (token_ids[None, :] == lane_ids[:LANES, None]).astype(low_type)
    heads_high, heads_low = split_two(table_heads)
    spare = ((0, LANES - VOCAB), (0, 0))
    tables = jnp.concatenate([jnp.pad(heads_high, spare), jnp.pad(heads_low, spare)], axis=0)
    cosine, sine_table = rotary_tables(positions.reshape(row_count))
    cosine = jnp.concatenate([cosine] * 4, axis=1)
    sine_table = jnp.concatenate([-sine_table, sine_table] * 2, axis=1)
    pairs = D // PAIR // ATTEND_CALLS
    attended = [
        attend_call(hot, tables, cosine, sine_table, number * pairs, pairs)
        for number in range(ATTEND_CALLS)
    ]
    mixed_low = jnp.concatenate([parts[3] for parts in attended], axis=1)
    branch = times_trans(mixed_low, mixing_low) + mixing_bias
    middle = stream + branch
    normed_two, normal_two, inverse_two = norm_forward(middle, gain_two, bias_two)
    normed_two_low = normed_two.astype(low_type)
    hidden_low, slope_low, feed_out = feed_call(
        normed_two_low, expand_bias[None, :], expand_parts, reduce_parts
    )
    feed_out = feed_out + reduce_bias
    output = middle + feed_out
    final_norm, normal_last, inverse_last = norm_forward(output, gain_last, bias_last)
    final_low = final_norm.astype(low_type)
    logits = times_trans(final_low, table_low)
    row_peak = jnp.max(logits, axis=-1, keepdims=True)
    shifted = jnp.exp(logits - row_peak)
    prob_rows = shifted / jnp.sum(shifted, axis=-1, keepdims=True)
    prob_sum = jnp.sum(prob_rows, axis=0)
    logit_grad = (prob_rows - target_hot).astype(low_type)
    final_grad = times_plain(logit_grad, table_low)
    table_head = trans_times(logit_grad, final_low)
    output_grad, gain_last_grad, bias_last_grad = norm_backward(
        final_grad, normal_last, inverse_last, gain_last
    )
    feed_low = output_grad.astype(low_type)
    reduce_bias_grad = jnp.sum(feed_low, axis=0, dtype=jnp.float32)
    scatter_masks = list(reversed(all_masks))
    half_ff = FF // 2
    reduce_part = scatter_blocks(
        trans_times(hidden_low[:, :half_ff], feed_low),
        trans_times(hidden_low[:, half_ff:], feed_low),
        scatter_masks,
        jnp.float32,
    )
    reduce_total = narrow_rows(reduce_part)
    pre_grad, normed_two_grad, expand_bias_grad = feed_back_call(
        feed_low, slope_low, expand_parts, reduce_parts
    )
    expand_bias_grad = in_order(
        expand_bias_grad.reshape(devices, FF // devices), all_masks, 1, me
    )
    expand_part = scatter_blocks(
        trans_times(pre_grad[:, :half_ff], normed_two_low),
        trans_times(pre_grad[:, half_ff:], normed_two_low),
        scatter_masks,
        jnp.float32,
    )
    expand_total = narrow_rows(expand_part)
    middle_part, gain_two_grad, bias_two_grad = norm_backward(
        normed_two_grad, normal_two, inverse_two, gain_two
    )
    middle_grad = output_grad + middle_part
    branch_low = middle_grad.astype(low_type)
    mixing_bias_grad = jnp.sum(branch_low, axis=0, dtype=jnp.float32)
    mixing_grad = trans_times(branch_low, mixed_low).reshape(devices, D // devices, D)
    mixing_grad = out_of_order(mixing_grad, all_masks, 1, me)
    mixing_part = scatter_blocks(
        mixing_grad[: devices // 2], mixing_grad[devices // 2 :], scatter_masks, jnp.float32
    )
    mixing_total = narrow_rows(mixing_part[0])
    mixed_grad = times_plain(branch_low, mixing_low).astype(low_type)
    backs = [
        attend_back_call(
            hot_turned,
            *attended[number][:3],
            mixed_grad,
            attended[number][4],
            cosine,
            sine_table,
            number * pairs,
        )
        for number in range(ATTEND_CALLS)
    ]
    token_sums = jnp.concatenate([back[1][:, :VOCAB] for back in backs], axis=2)
    token_sums = jnp.transpose(token_sums, (1, 0, 2)).reshape(VOCAB, 3 * D)
    attend_bias_grad = jnp.sum(token_sums, axis=0)
    projected_low = jnp.concatenate(
        [back[0][number] for number in range(3) for back in backs], axis=1
    )
    wide_size = lax.axis_size("wide")
    token_sums = jnp.transpose(token_sums.reshape(VOCAB, wide_size, 3 * D // wide_size), (1, 0, 2))
    token_sums = sum_small(token_sums)
    attend_total = lax.dot_general(
        token_sums,
        table_normed.astype(jnp.float32),
        (((0,), (0,)), ((), ())),
        precision=lax.Precision.HIGHEST,
        preferred_element_type=jnp.float32,
    )
    normed_one_grad = times_plain(projected_low, attend_low)
    normed_one, normal_one, inverse_one = norm_forward(stream, gain_one, bias_one)
    stream_part, gain_one_grad, bias_one_grad = norm_backward(
        normed_one_grad, normal_one, inverse_one, gain_one
    )
    entry_gradient = middle_grad + stream_part
    table_grad = (
        embed_scale * exact_times(token_hot.astype(jnp.float32).T, entry_gradient) + table_head
    )
    vector_grad = jnp.concatenate(
        [
            jnp.stack(
                [
                    gain_one_grad,
                    bias_one_grad,
                    gain_two_grad,
                    bias_two_grad,
                    gain_last_grad,
                    bias_last_grad,
                ]
            ),
            attend_bias_grad.reshape(3, D),
            mixing_bias_grad[None, :],
            reduce_bias_grad[None, :],
            expand_bias_grad.reshape(4, D),
        ],
        axis=0,
    )
    columns = D // wide_size
    rows_hist = -(-VOCAB // columns)
    hist_part = jnp.pad(prob_sum, (0, rows_hist * columns - VOCAB)).reshape(rows_hist, columns)
    small_grads = jnp.concatenate([table_grad, vector_grad], axis=0)
    small_grads = jnp.transpose(small_grads.reshape(VOCAB + 15, wide_size, columns), (1, 0, 2))
    small_grads = jnp.concatenate(
        [small_grads, jnp.broadcast_to(hist_part, (wide_size, rows_hist, columns))], axis=1
    )
    small_total = sum_small(small_grads)
    table_total = small_total[:VOCAB]
    vector_total = small_total[VOCAB : VOCAB + 15]
    prob_total = small_total[VOCAB + 15 :].reshape(rows_hist * columns)[:VOCAB]
    histogram = prob_total * (VOCAB / (row_count * devices))
    totals = (attend_total, mixing_total, expand_total, reduce_total)
    matrix_new, moment_next = muon_rows(
        (attend_weight, mixing_weight, expand_weight, reduce_weight),
        (attend_moment, mixing_moment, expand_moment, reduce_moment),
        totals,
    )
    table_new, table_mean_next, table_square_next = adam_step(
        table_weight, table_mean, table_square, table_total, TABLE_RATE, TABLE_DECAY, step_count
    )
    vector_new, vector_mean_next, vector_square_next = adam_step(
        vector_params, vector_mean, vector_square, vector_total, VECTOR_RATE, 0.0, step_count
    )
    results = (
        totals
        + (table_total, vector_total)
        + matrix_new
        + moment_next
        + (
            table_new,
            table_mean_next,
            table_square_next,
            vector_new,
            vector_mean_next,
            vector_square_next,
        )
    )
    block_output = output.astype(low_type).reshape(seq_count, SEQ_LEN, D)
    return (block_output, entry_gradient.reshape(seq_count, SEQ_LEN, D)) + results + (histogram,)


def solution(mesh):
    in_specs = (
        P(("wide", "narrow"), None),
        P(("wide", "narrow")),
        P(("wide", "narrow"), None),
        P(("wide", "narrow"), None),
        P(None, "wide"),
        P("wide", None),
        P("wide", None),
        P("wide", None),
        P("wide", None),
        P(None, "wide"),
        P("wide", None),
        P("wide", None),
        P("wide", None),
        P("wide", None),
        P(None, "wide"),
        P(None, "wide"),
        P(None, "wide"),
        P(None, "wide"),
        P(),
    )
    out_specs = (
        P(("wide", "narrow"), None, None),
        P(("wide", "narrow"), None, None),
        P("wide", None),
        P("wide", None),
        P("wide", None),
        P("wide", None),
        P(None, "wide"),
        P(None, "wide"),
        P("wide", None),
        P("wide", None),
        P("wide", None),
        P("wide", None),
        P("wide", None),
        P("wide", None),
        P("wide", None),
        P("wide", None),
        P(None, "wide"),
        P(None, "wide"),
        P(None, "wide"),
        P(None, "wide"),
        P(None, "wide"),
        P(None, "wide"),
        P(),
    )
    return jax.shard_map(
        on_device, mesh=mesh, in_specs=in_specs, out_specs=out_specs, check_vma=False
    )
```

```python
from functools import partial
import math

import jax
import jax.numpy as jnp
import numpy as np
from jax import lax
from jax.experimental import pallas as pl
from jax.experimental.pallas import tpu as pltpu
from jax.sharding import PartitionSpec as P

D = 768
HEADS = 12
HEAD_DIM = 64
FF = 3072
VOCAB = 70
SEQ_LEN = 912
NS_ITERS = 5


NORM_EPS = 1e-05
ROPE_BASE = 10000.0
NEWTON_A = 3.4445
NEWTON_B = -4.775
NEWTON_C = 2.0315
MUON_MU = 0.95
MUON_RATE = 0.3
MUON_DECAY = 0.1
SHAPE_FACTOR = 0.2
ADAM_BETA1 = 0.9
ADAM_BETA2 = 0.95
ADAM_EPS = 1e-08
TABLE_RATE = 0.03
TABLE_DECAY = 0.01
VECTOR_RATE = 0.2


def times_plain(left_side, right_side):
    return jnp.dot(left_side, right_side, preferred_element_type=jnp.float32)


def times_trans(left_side, right_side):
    return lax.dot_general(
        left_side, right_side, (((1,), (1,)), ((), ())), preferred_element_type=jnp.float32
    )


def trans_times(left_side, right_side):
    return lax.dot_general(
        left_side, right_side, (((0,), (0,)), ((), ())), preferred_element_type=jnp.float32
    )


def exact_times(left_side, right_side):
    return jnp.dot(
        left_side, right_side, precision=lax.Precision.HIGHEST, preferred_element_type=jnp.float32
    )


def norm_forward(values, gain_row, bias_row):
    center = values - jnp.mean(values, axis=-1, keepdims=True)
    spread = jnp.mean(center * center, axis=-1, keepdims=True)
    inverse = lax.rsqrt(spread + NORM_EPS)
    normal = center * inverse
    return (normal * gain_row + bias_row, normal, inverse)


def norm_backward(upstream, normal, inverse, gain_row):
    scaled = upstream * gain_row
    inner_part = (
        scaled
        - jnp.mean(scaled, axis=-1, keepdims=True)
        - normal * jnp.mean(scaled * normal, axis=-1, keepdims=True)
    )
    return (inverse * inner_part, jnp.sum(upstream * normal, axis=0), jnp.sum(upstream, axis=0))


def rotary_tables(positions):
    half_dim = HEAD_DIM // 2
    frequency = ROPE_BASE ** (-(jnp.arange(half_dim, dtype=jnp.float32) * 2.0 / HEAD_DIM))
    turned = positions.astype(jnp.float32)[..., None] * frequency
    return (jnp.cos(turned), jnp.sin(turned))


PAIR = 2 * HEAD_DIM
SPAN = 1024
STRIP = 256
PARTS = 4
BLOCK = 96
PART_BLOCKS = D // BLOCK
LANES = 128
ATTEND_CALLS = 3
BACK_CALLS = 6


BOTH = ("wide", "narrow")
GRAM_TILE = 256
GRAM_SPOTS = ((0, 0), (0, 1), (0, 2), (1, 1), (1, 2), (2, 2))


def swap(value, mask):
    total = lax.axis_size(BOTH)
    return lax.ppermute(value, BOTH, [(spot, spot ^ mask) for spot in range(total)])


def my_index():
    return lax.axis_index("wide") * lax.axis_size("narrow") + lax.axis_index("narrow")


def wide_masks():
    narrow_size = lax.axis_size("narrow")
    count = lax.axis_size("wide").bit_length() - 1
    return [narrow_size << bit for bit in reversed(range(count))]


def offsets_of(masks):
    table = [0]
    for mask in masks:
        table = table + [offset ^ mask for offset in table]
    return np.array(table)


def gate(value, others):
    leaves, form = jax.tree.flatten(value)
    held = lax.optimization_barrier(tuple(leaves) + tuple(jax.tree.leaves(others)))
    return jax.tree.unflatten(form, held[: len(leaves)])


def padded_rows(array):
    return jnp.pad(array, ((0, -array.shape[0] % 16), (0, 0)))


def gather_blocks(piece, masks):
    for mask in masks:
        piece = jnp.concatenate([piece, swap(piece, mask)], axis=0)
    return piece


def take_blocks(array, index):
    return jnp.take(array, index, axis=0, mode="clip")


def places_of(masks, unit):
    offsets = offsets_of(masks) // unit
    place = np.zeros_like(offsets)
    place[offsets] = np.arange(offsets.size)
    return place


def in_order(blocks, masks, unit, base):
    place = places_of(masks, unit)
    return take_blocks(blocks, jnp.asarray(place)[jnp.arange(place.size) ^ base])


def out_of_order(blocks, masks, unit, base):
    offsets = offsets_of(masks) // unit
    return take_blocks(blocks, jnp.asarray(offsets) ^ base)


def quarter_rows(array):
    count = array.shape[0] // lax.axis_size("narrow")
    return lax.dynamic_slice_in_dim(array, lax.axis_index("narrow") * count, count, 0)


def side_of(mask):
    return (my_index() // mask) % 2


def split_static(array, axis):
    return lax.index_in_dim(array, 0, axis, False), lax.index_in_dim(array, 1, axis, False)


def split_sided(array, axis, mask):
    side = side_of(mask)
    return (
        lax.dynamic_index_in_dim(array, side, axis, False),
        lax.dynamic_index_in_dim(array, 1 - side, axis, False),
    )


def halves(item, mask):
    array, marks, sided = item
    axis = marks.index(mask)
    keep, send = split_sided(array, axis, mask) if sided else split_static(array, axis)
    return (keep, marks[:axis] + marks[axis + 1 :], sided), send


def hop(items, mask, kind):
    pairs = [halves(item, mask) for item in items]
    rows = [send.astype(kind).reshape(-1, send.shape[-1]) for _, send in pairs]
    flat = jnp.concatenate(rows, axis=0) if len(rows) > 1 else rows[0]
    token = yield flat
    got = gate(swap(flat, mask), token)
    results, at = [], 0
    for ((keep, marks, sided), send), row in zip(pairs, rows):
        part = got[at : at + row.shape[0]].reshape(send.shape).astype(jnp.float32)
        results.append((keep + part, marks, sided))
        at += row.shape[0]
    return results


def finish(steps, token):
    try:
        steps.send(token)
    except StopIteration as stop:
        return stop.value


def finish_hop(steps):
    next(steps)
    return finish(steps, ())


def columns_of(items, start, stop):
    return [(array[..., start:stop], marks, sided) for array, marks, sided in items]


def sum_chain(items, kind):
    masks = wide_masks()
    width = items[0][0].shape[-1]
    ways = [columns_of(items, 0, width // 2), columns_of(items, width // 2, width)]
    for pair in ((masks[-1], 2), (2, masks[-1])):
        steps = [hop(way, mask, jnp.bfloat16) for way, mask in zip(ways, pair)]
        token = yield tuple(next(step) for step in steps)
        ways = [finish(step, token) for step in steps]
    items = [
        (jnp.concatenate([left[0], right[0]], axis=-1), left[1], left[2])
        for left, right in zip(*ways)
    ]
    for mask in reversed(masks[:-1]):
        items = yield from hop(items, mask, kind)
    return [item[0] for item in items]


def drain(chain, token):
    while True:
        try:
            chain.send(token)
        except StopIteration as stop:
            return stop.value


def bits_shape(count, tail):
    return (2,) * (count.bit_length() - 1) + tuple(tail)


def join_narrow(piece):
    spot = lax.axis_index("narrow")
    other = swap(piece, 2)
    pair = jnp.where(spot // 2 == 0, jnp.stack([piece, other]), jnp.stack([other, piece]))
    other = swap(pair, 1)
    quad = jnp.where(
        spot % 2 == 0, jnp.stack([pair, other], axis=1), jnp.stack([other, pair], axis=1)
    )
    return quad.reshape((4,) + piece.shape)


def sum_small(blocks):
    total = blocks + swap(blocks, 1)
    first = total
    total = total.reshape(bits_shape(blocks.shape[0], blocks.shape[1:]))
    masks = wide_masks()
    while masks:
        mask = masks[-1]
        keep, send = split_sided(total, len(masks) - 1, mask)
        total = keep + swap(send, mask)
        masks = masks[:-1]
    return total + swap(total, 2), first


def sum_wide(value):
    for mask in reversed(wide_masks()):
        value = value + swap(value, mask)
    return value


def sum_gram(blocks):
    masks = list(reversed(wide_masks()))
    ways = [masks, [masks[1], masks[0]] + masks[2:]]
    half = blocks.shape[0] // 2
    parts = [blocks[:half], blocks[half:]]
    for step in range(len(masks)):
        for number, way in enumerate(ways):
            part = parts[number]
            split = part.reshape((2, part.shape[0] // 2) + part.shape[1:])
            keep, send = split_sided(split, 0, way[step])
            parts[number] = keep + swap(send, way[step])
    for step in reversed(range(len(masks))):
        for number, way in enumerate(ways):
            part = parts[number]
            other = swap(part, way[step])
            parts[number] = jnp.where(
                side_of(way[step]) == 0,
                jnp.concatenate([part, other], axis=0),
                jnp.concatenate([other, part], axis=0),
            )
    return parts


def row_dot(left_side, right_side):
    return lax.dot_general(
        left_side, right_side, (((1,), (1,)), ((), ())), preferred_element_type=jnp.float32
    )


def split_two(values):
    high = values.astype(jnp.bfloat16)
    return high, (values - high.astype(jnp.float32)).astype(jnp.bfloat16)


def rounded(values):
    return lax.reduce_precision(values, 8, 7)


def newton_kernel(
    low_ref, high_ref, rows_ref, add_left_ref, add_right_ref, out_ref,
    gram_now, other, left, right, rows_left,
):
    tile = GRAM_TILE
    trace = jnp.zeros((1, 1), jnp.float32)
    diagonal = lax.broadcasted_iota(jnp.int32, (tile, tile), 0) == lax.broadcasted_iota(
        jnp.int32, (tile, tile), 1
    )

    def span(number):
        return slice(number * tile, (number + 1) * tile)

    half = len(GRAM_SPOTS) // 2
    for number, (row, column) in enumerate(GRAM_SPOTS):
        source = low_ref if number < half else high_ref
        block = source[span(number % half), :] + lax.dot_general(
            add_left_ref[:, span(row)],
            add_right_ref[:, span(column)],
            (((0,), (0,)), ((), ())),
            preferred_element_type=jnp.float32,
        )
        gram_now[span(row), span(column)] = block
        if row == column:
            picked = jnp.where(diagonal, block, 0.0)
            trace = trace + jnp.sum(jnp.sum(picked, axis=0, keepdims=True), axis=1, keepdims=True)
    inverse = 1.0 / (jnp.sqrt(trace) + 1e-07)
    scale = inverse * inverse
    for row, column in GRAM_SPOTS:
        block = gram_now[span(row), span(column)] * scale
        gram_now[span(row), span(column)] = block
        if row != column:
            gram_now[span(column), span(row)] = block.T

    def set_left(values):
        high, low = split_two(values)
        left[:, 0:D] = high
        left[:, D : 2 * D] = high
        left[:, 2 * D : 3 * D] = low

    def set_right(values):
        high, low = split_two(values)
        right[0:D, :] = high
        right[D : 2 * D, :] = low
        right[2 * D : 3 * D, :] = high

    def set_rows(values):
        high, low = split_two(values)
        rows_left[:, 0:D] = high
        rows_left[:, D : 2 * D] = high
        rows_left[:, 2 * D : 3 * D] = low

    def product(target, finish):
        for column in range(D // tile):
            rows = (column + 1) * tile
            block = jnp.dot(left[0:rows, :], right[:, span(column)], preferred_element_type=jnp.float32)
            for row in range(column + 1):
                piece = finish(block[span(row), :], row, column)
                target[span(row), span(column)] = piece
                if row != column:
                    target[span(column), span(row)] = piece.T

    def same(block, row, column):
        return block

    def factor(block, row, column):
        block = NEWTON_B * gram_now[span(row), span(column)] + NEWTON_C * block
        if row == column:
            block = block + jnp.where(diagonal, NEWTON_A, 0.0)
        return block

    def set_factor():
        set_left(gram_now[...])
        set_right(gram_now[...])
        product(other, factor)
        set_right(other[...])

    def rows_product():
        return jnp.dot(rows_left[...], right[...], preferred_element_type=jnp.float32)

    set_rows(rows_ref[...] * inverse)

    def body(step, carry):
        set_factor()
        product(other, same)
        set_left(other[...])
        product(gram_now, same)
        set_rows(rows_product())
        return carry

    lax.fori_loop(0, NS_ITERS - 1, body, 0)
    set_factor()
    out_ref[...] = rows_product().astype(out_ref.dtype)


def newton_rows(gram_parts, rows, add_left, add_right):
    count = rows.shape[0]
    return pl.pallas_call(
        newton_kernel,
        out_shape=jax.ShapeDtypeStruct((count, D), jnp.bfloat16),
        in_specs=[pl.BlockSpec(memory_space=pltpu.VMEM)] * 5,
        out_specs=pl.BlockSpec(memory_space=pltpu.VMEM),
        scratch_shapes=[
            pltpu.VMEM((D, D), jnp.float32),
            pltpu.VMEM((D, D), jnp.float32),
            pltpu.VMEM((D, 3 * D), jnp.bfloat16),
            pltpu.VMEM((3 * D, D), jnp.bfloat16),
            pltpu.VMEM((count, 3 * D), jnp.bfloat16),
        ],
        compiler_params=pltpu.CompilerParams(vmem_limit_bytes=48 << 20),
        cost_estimate=pl.CostEstimate(flops=60 * D * D * D, bytes_accessed=4 << 20, transcendentals=0),
        name="newton",
    )(*gram_parts, rows, add_left, add_right)


def pick_rows(parts, spot):
    most = max(part.shape[0] for part in parts)
    padded = [jnp.pad(part, ((0, most - part.shape[0]), (0, 0))) for part in parts]
    picked = padded[-1]
    for number in reversed(range(len(parts) - 1)):
        picked = jnp.where(spot == number, padded[number], picked)
    return picked


def local_gram(rows):
    tiles = [rows[:, at * GRAM_TILE : (at + 1) * GRAM_TILE] for at in range(D // GRAM_TILE)]
    return jnp.concatenate(
        [
            lax.dot_general(
                tiles[row],
                tiles[column],
                (((0,), (0,)), ((), ())),
                precision=lax.Precision.HIGHEST,
                preferred_element_type=jnp.float32,
            )
            for row, column in GRAM_SPOTS
        ],
        axis=0,
    )


def pack_kernel(spot_ref, *refs):
    out_ref = refs[-1]
    at = 0
    for ref in refs[:-1]:
        count = ref.shape[0]
        out_ref[at : at + count, :] = ref[...].astype(jnp.bfloat16)
        at += count
        room = -count % 16
        if room:
            out_ref[at : at + room, :] = jnp.zeros((room, D), jnp.bfloat16)
            at += room


def pack_rows(weights, spot):
    units = [weight.shape[0] // lax.axis_size("narrow") for weight in weights]
    total = sum(unit + -unit % 16 for unit in units)
    if any(unit % 8 for unit in units):
        return jnp.concatenate(
            [padded_rows(quarter_rows(weight).astype(jnp.bfloat16)) for weight in weights], axis=0
        )
    return pl.pallas_call(
        pack_kernel,
        grid_spec=pltpu.PrefetchScalarGridSpec(
            num_scalar_prefetch=1,
            grid=(1,),
            in_specs=[pl.BlockSpec((unit, D), lambda step, spot: (spot[0], 0)) for unit in units],
            out_specs=pl.BlockSpec((total, D), lambda step, spot: (0, 0)),
        ),
        out_shape=jax.ShapeDtypeStruct((total, D), jnp.bfloat16),
        name="pack",
    )(spot[None].astype(jnp.int32), *weights)


def sums_kernel(*refs):
    *parts, out_ref, bias_ref, held = refs
    for number, part in enumerate(parts):
        width = part.shape[2]
        for kind in range(3):
            start = kind * D + number * width
            held[:, start : start + width] = part[kind]
    bias_ref[...] = jnp.sum(held[...], axis=0, keepdims=True)
    count, rows, columns = out_ref.shape
    for number in range(count):
        out_ref[number] = held[0:rows, number * columns : (number + 1) * columns]


def sums_blocks(parts, wide_size):
    whole = pl.BlockSpec(memory_space=pltpu.VMEM)
    return pl.pallas_call(
        sums_kernel,
        in_specs=[whole] * len(parts),
        out_specs=[whole, whole],
        out_shape=[
            jax.ShapeDtypeStruct((wide_size, VOCAB, 3 * D // wide_size), jnp.float32),
            jax.ShapeDtypeStruct((1, 3 * D), jnp.float32),
        ],
        scratch_shapes=[pltpu.VMEM((LANES, 3 * D), jnp.float32)],
        name="token_sums",
    )(*parts)


def update_kernel(rates, spot_ref, pair_ref, other_ref, *refs):
    count = len(rates)
    for number in range(count):
        weight_ref, out_ref = refs[number], refs[count + number]
        rows = weight_ref.shape[0]
        way = spot_ref[0] ^ number
        mine = jnp.where(
            way % 2 == 0, pair_ref[way // 2, 0:rows, :], other_ref[way // 2, 0:rows, :]
        )
        out_ref[...] = (
            weight_ref[...] * (1.0 - MUON_RATE * MUON_DECAY)
            - rates[number] * mine.astype(jnp.float32)
        )


def update_rows(spot, pair, other, weights, rates):
    whole = pl.BlockSpec(memory_space=pltpu.VMEM)
    return pl.pallas_call(
        partial(update_kernel, rates),
        in_specs=[pl.BlockSpec(memory_space=pltpu.SMEM)] + [whole] * (2 + len(weights)),
        out_specs=[whole] * len(weights),
        out_shape=[jax.ShapeDtypeStruct(weight.shape, jnp.float32) for weight in weights],
        compiler_params=pltpu.CompilerParams(vmem_limit_bytes=40 << 20),
        name="update",
    )(spot[None].astype(jnp.int32), pair, other, *weights)


def heads_kernel(place_ref, blocks_ref, bias_ref, out_ref, held):
    count, rows, columns = blocks_ref.shape
    held[...] = jnp.zeros_like(held)
    for number in range(count):
        spot = slice(number * columns, (number + 1) * columns)
        held[0:rows, spot] = blocks_ref[place_ref[number]] + bias_ref[:, spot]
    high, low = split_two(held[...])
    out_ref[0:LANES, :] = high
    out_ref[LANES : 2 * LANES, :] = low


def heads_table(blocks, place, bias):
    return pl.pallas_call(
        heads_kernel,
        grid_spec=pltpu.PrefetchScalarGridSpec(
            num_scalar_prefetch=1,
            grid=(1,),
            in_specs=[
                pl.BlockSpec(blocks.shape, lambda step, place: (0, 0, 0)),
                pl.BlockSpec(bias.shape, lambda step, place: (0, 0)),
            ],
            out_specs=pl.BlockSpec((2 * LANES, 3 * D), lambda step, place: (0, 0)),
            scratch_shapes=[pltpu.VMEM((LANES, 3 * D), jnp.float32)],
        ),
        out_shape=jax.ShapeDtypeStruct((2 * LANES, 3 * D), jnp.bfloat16),
        name="heads_table",
    )(place, blocks, bias)


def turn(values, cosine, sine_table):
    lane = lax.broadcasted_iota(jnp.int32, values.shape, 1)
    half = HEAD_DIM // 2
    partner = jnp.where(
        lane % HEAD_DIM < half,
        pltpu.roll(values, PAIR - half, 1),
        pltpu.roll(values, half, 1),
    )
    return values * cosine + partner * sine_table


def attend_kernel(
    hot_ref, tq_ref, tk_ref, tv_ref, cos_ref, sin_ref,
    q_ref, k_ref, v_ref, mixed_ref, log_ref,
    q_all, v_turned, mixed_turned, prob_all,
):
    hot = hot_ref[...]
    cosine = cos_ref[...]
    sine_table = sin_ref[...]
    queries = jnp.dot(hot, tq_ref[...], preferred_element_type=jnp.float32)
    queries = turn(queries, cosine, sine_table).astype(jnp.bfloat16) * HEAD_DIM ** (-0.5)
    queries = queries.astype(jnp.bfloat16)
    q_ref[...] = queries
    q_all[0:SEQ_LEN, :] = queries
    q_all[SEQ_LEN:SPAN, :] = jnp.zeros((SPAN - SEQ_LEN, PAIR), jnp.bfloat16)
    keys = jnp.dot(hot, tk_ref[...], preferred_element_type=jnp.float32)
    keys = turn(keys, cosine, sine_table).astype(jnp.bfloat16)
    k_ref[...] = keys
    values = jnp.dot(hot, tv_ref[...], preferred_element_type=jnp.float32)
    v_ref[...] = values.astype(jnp.bfloat16)
    v_turned[...] = values.T.astype(jnp.bfloat16)

    def one_head(head, carry):
        lane = lax.broadcasted_iota(jnp.int32, (SEQ_LEN, PAIR), 1)
        keys_head = jnp.where(lane // HEAD_DIM == head, k_ref[...], jnp.zeros((), jnp.bfloat16))
        head_rows = pl.ds(pl.multiple_of(head * HEAD_DIM, HEAD_DIM), HEAD_DIM)
        values_head = v_turned[head_rows, :]

        def body(step, carry):
            at = pl.multiple_of(step * STRIP, STRIP)
            scores = row_dot(keys_head, q_all[pl.ds(at, STRIP), :])
            peak = jnp.max(scores, axis=0, keepdims=True)
            powers = jnp.exp(scores - peak)
            total = jnp.sum(powers, axis=0, keepdims=True)
            prob_low = (powers * (1.0 / total)).astype(jnp.bfloat16)
            prob_all[:, pl.ds(at, STRIP)] = prob_low
            log_ref[0, pl.ds(head, 1), pl.ds(at, STRIP)] = peak + jnp.log(total)
            return carry

        lax.fori_loop(0, SPAN // STRIP, body, 0)
        mixed_turned[head_rows, :] = jnp.dot(
            values_head, prob_all[...], preferred_element_type=jnp.float32
        )
        return carry

    lax.fori_loop(0, 2, one_head, 0)
    mixed_ref[...] = mixed_turned[...].T[0:SEQ_LEN, :].astype(jnp.bfloat16)


def attend_call(hot, tables, cosine, sine_table, first, count):
    whole = lambda step: (0, 0)
    source = lambda step: (0, step + first)
    own = lambda step: (0, step)
    rows_low = jax.ShapeDtypeStruct((SEQ_LEN, count * PAIR), jnp.bfloat16)
    return pl.pallas_call(
        attend_kernel,
        grid=(count,),
        in_specs=[
            pl.BlockSpec(hot.shape, whole),
            pl.BlockSpec((hot.shape[1], PAIR), source),
            pl.BlockSpec((hot.shape[1], PAIR), lambda step: (0, step + first + D // PAIR)),
            pl.BlockSpec((hot.shape[1], PAIR), lambda step: (0, step + first + 2 * D // PAIR)),
            pl.BlockSpec((SEQ_LEN, PAIR), whole),
            pl.BlockSpec((SEQ_LEN, PAIR), whole),
        ],
        out_specs=[
            pl.BlockSpec((SEQ_LEN, PAIR), own),
            pl.BlockSpec((SEQ_LEN, PAIR), own),
            pl.BlockSpec((SEQ_LEN, PAIR), own),
            pl.BlockSpec((SEQ_LEN, PAIR), own),
            pl.BlockSpec((1, 2, SPAN), lambda step: (step, 0, 0)),
        ],
        out_shape=[rows_low] * 4 + [jax.ShapeDtypeStruct((count, 2, SPAN), jnp.float32)],
        scratch_shapes=[
            pltpu.VMEM((SPAN, PAIR), jnp.bfloat16),
            pltpu.VMEM((PAIR, SEQ_LEN), jnp.bfloat16),
            pltpu.VMEM((PAIR, SPAN), jnp.float32),
            pltpu.VMEM((SEQ_LEN, SPAN), jnp.bfloat16),
        ],
        compiler_params=pltpu.CompilerParams(vmem_limit_bytes=40 << 20),
        cost_estimate=pl.CostEstimate(
            flops=count * SPAN * SPAN, bytes_accessed=1 << 16,
            transcendentals=0,
        ),
        name="attend",
    )(hot, tables, tables, tables, cosine, sine_table)


def attend_back_kernel(
    hot_ref, q_ref, k_ref, v_ref, grad_ref, log_ref, cos_ref, sin_ref,
    low_ref, sums_ref,
    q_all, grad_all, k_turned, prob_all, score_all, query_turned, key_sum, value_sum,
):
    rest = jnp.zeros((SPAN - SEQ_LEN, PAIR), jnp.bfloat16)
    q_all[0:SEQ_LEN, :] = q_ref[...]
    q_all[SEQ_LEN:SPAN, :] = rest
    grad_all[0:SEQ_LEN, :] = grad_ref[...]
    grad_all[SEQ_LEN:SPAN, :] = rest
    k_turned[...] = k_ref[...].astype(jnp.float32).T.astype(jnp.bfloat16)
    lane = lax.broadcasted_iota(jnp.int32, (SEQ_LEN, PAIR), 1)
    none = jnp.zeros((), jnp.bfloat16)

    def one_head(head, carry):
        head_rows = pl.ds(pl.multiple_of(head * HEAD_DIM, HEAD_DIM), HEAD_DIM)
        keys_head = jnp.where(lane // HEAD_DIM == head, k_ref[...], none)
        values_head = jnp.where(lane // HEAD_DIM == head, v_ref[...], none)

        def body(step, carry):
            at = pl.multiple_of(step * STRIP, STRIP)
            scores = row_dot(keys_head, q_all[pl.ds(at, STRIP), :])
            prob_rows = jnp.exp(scores - log_ref[0, pl.ds(head, 1), pl.ds(at, STRIP)])
            prob_all[:, pl.ds(at, STRIP)] = prob_rows.astype(jnp.bfloat16)
            prob_grad = row_dot(values_head, grad_all[pl.ds(at, STRIP), :])
            delta = jnp.sum(prob_grad * prob_rows, axis=0, keepdims=True)
            score_all[:, pl.ds(at, STRIP)] = (prob_rows * (prob_grad - delta)).astype(jnp.bfloat16)
            return carry

        lax.fori_loop(0, SPAN // STRIP, body, 0)
        value_part = jnp.dot(prob_all[...], grad_all[...], preferred_element_type=jnp.float32)
        key_part = jnp.dot(score_all[...], q_all[...], preferred_element_type=jnp.float32)
        value_sum[...] = jnp.where(lane // HEAD_DIM == head, value_part, value_sum[...])
        key_sum[...] = jnp.where(lane // HEAD_DIM == head, key_part, key_sum[...])
        query_turned[head_rows, :] = (
            jnp.dot(k_turned[head_rows, :], score_all[...], preferred_element_type=jnp.float32)
            * HEAD_DIM ** (-0.5)
        )
        return carry

    lax.fori_loop(0, 2, one_head, 0)
    cosine = cos_ref[...]
    sine_table = -sin_ref[...]
    hot = hot_ref[...]
    query_low = turn(query_turned[...].T[0:SEQ_LEN, :], cosine, sine_table).astype(jnp.bfloat16)
    key_low = turn(key_sum[...], cosine, sine_table).astype(jnp.bfloat16)
    value_low = value_sum[...].astype(jnp.bfloat16)
    for number, low in enumerate((query_low, key_low, value_low)):
        low_ref[number] = low
        sums_ref[number] = jnp.dot(hot, low, preferred_element_type=jnp.float32)


def attend_back_call(
    hot_turned, queries, keys, values, gradients, logs, cosine, sine_table, first, inside, count
):
    whole = lambda step: (0, 0)
    rows = pl.BlockSpec((SEQ_LEN, PAIR), lambda step: (0, step + inside))
    whole_rows = pl.BlockSpec((SEQ_LEN, PAIR), whole)
    return pl.pallas_call(
        attend_back_kernel,
        grid=(count,),
        in_specs=[
            pl.BlockSpec(hot_turned.shape, whole),
            rows,
            rows,
            rows,
            pl.BlockSpec((SEQ_LEN, PAIR), lambda step: (0, step + first)),
            pl.BlockSpec((1, 2, SPAN), lambda step: (step + inside, 0, 0)),
            whole_rows,
            whole_rows,
        ],
        out_specs=[
            pl.BlockSpec((3, SEQ_LEN, PAIR), lambda step: (0, 0, step)),
            pl.BlockSpec((3, hot_turned.shape[0], PAIR), lambda step: (0, 0, step)),
        ],
        out_shape=[
            jax.ShapeDtypeStruct((3, SEQ_LEN, count * PAIR), jnp.bfloat16),
            jax.ShapeDtypeStruct((3, hot_turned.shape[0], count * PAIR), jnp.float32),
        ],
        scratch_shapes=[
            pltpu.VMEM((SPAN, PAIR), jnp.bfloat16),
            pltpu.VMEM((SPAN, PAIR), jnp.bfloat16),
            pltpu.VMEM((PAIR, SEQ_LEN), jnp.bfloat16),
            pltpu.VMEM((SEQ_LEN, SPAN), jnp.bfloat16),
            pltpu.VMEM((SEQ_LEN, SPAN), jnp.bfloat16),
            pltpu.VMEM((PAIR, SPAN), jnp.float32),
            pltpu.VMEM((SEQ_LEN, PAIR), jnp.float32),
            pltpu.VMEM((SEQ_LEN, PAIR), jnp.float32),
        ],
        compiler_params=pltpu.CompilerParams(vmem_limit_bytes=48 << 20),
        cost_estimate=pl.CostEstimate(
            flops=count * SPAN * SPAN, bytes_accessed=1 << 16,
            transcendentals=0,
        ),
        name="attend_back",
    )(hot_turned, queries, keys, values, gradients, logs, cosine, sine_table)


ERF_P = 0.3275911
ERF_A = (0.254829592, -0.284496736, 1.421413741, -1.453152027, 1.061405429)

def normal_parts(values):
    size = jnp.abs(values)
    bell = jnp.exp(values * values * -0.5)
    step = 1.0 / (1.0 + (ERF_P * 0.5**0.5) * size)
    series = ERF_A[4]
    for factor in (ERF_A[3], ERF_A[2], ERF_A[1], ERF_A[0]):
        series = series * step + factor
    tail = (0.5 * series) * step * bell
    return jnp.where(values < 0.0, tail, 1.0 - tail), bell * (1.0 / math.sqrt(2.0 * math.pi))

def start_parts(place_ref, source_ref, starts, held, sems):
    for part in range(PARTS):
        for number, start in enumerate(starts):

            def body(spot, carry):
                pltpu.make_async_copy(
                    source_ref.at[place_ref[part * PART_BLOCKS + spot], pl.ds(start, BLOCK), :],
                    held[number].at[part, spot],
                    sems.at[number, part],
                ).start()
                return carry

            lax.fori_loop(0, PART_BLOCKS, body, 0)


def wait_part(source_ref, number, held, sems, step):
    pltpu.make_async_copy(
        source_ref.at[pl.ds(0, PART_BLOCKS), pl.ds(0, BLOCK), :],
        held[number].at[step],
        sems.at[number, step],
    ).wait()
    return held[number][step].reshape(D, D)


def feed_kernel(starts, place_ref, rows_ref, bias_ref, source_ref, hidden_ref, slope_ref, out_ref, expand_held, reduce_held, sems):
    held = (expand_held, reduce_held)
    step = pl.program_id(0)
    @pl.when(step == 0)
    def _():
        start_parts(place_ref, source_ref, starts, held, sems)

    expand = wait_part(source_ref, 0, held, sems, step)
    for at in range(0, SEQ_LEN, 304):
        spot = slice(at, at + 304)
        values = row_dot(rows_ref[spot, :], expand) + bias_ref[...]
        below, bell = normal_parts(values)
        hidden_ref[spot, :] = (values * below).astype(jnp.bfloat16)
        slope_ref[spot, :] = (below + values * bell).astype(jnp.bfloat16)
    reduce = wait_part(source_ref, 1, held, sems, step)
    part = jnp.dot(hidden_ref[...], reduce, preferred_element_type=jnp.float32)
    @pl.when(step == 0)
    def _():
        out_ref[...] = part
    @pl.when(step > 0)
    def _():
        out_ref[...] += part

def feed_call(place, rows, bias, source, starts):
    whole = lambda step, place: (0, 0)
    chunk = pl.BlockSpec((SEQ_LEN, D), lambda step, place: (0, step))
    return pl.pallas_call(
        partial(feed_kernel, starts),
        grid_spec=pltpu.PrefetchScalarGridSpec(
            num_scalar_prefetch=1,
            grid=(PARTS,),
            in_specs=[
                pl.BlockSpec((SEQ_LEN, D), whole),
                pl.BlockSpec((1, D), lambda step, place: (0, step)),
                pl.BlockSpec(memory_space=pl.ANY),
            ],
            out_specs=[chunk, chunk, pl.BlockSpec((SEQ_LEN, D), whole)],
            scratch_shapes=[
                pltpu.VMEM((PARTS, PART_BLOCKS, BLOCK, D), jnp.bfloat16),
                pltpu.VMEM((PARTS, PART_BLOCKS, BLOCK, D), jnp.bfloat16),
                pltpu.SemaphoreType.DMA((2, PARTS)),
            ],
        ),
        out_shape=[jax.ShapeDtypeStruct((SEQ_LEN, FF), jnp.bfloat16)] * 2
        + [jax.ShapeDtypeStruct((SEQ_LEN, D), jnp.float32)],
        compiler_params=pltpu.CompilerParams(vmem_limit_bytes=48 << 20),
        cost_estimate=pl.CostEstimate(
            flops=SEQ_LEN * D * FF, bytes_accessed=1 << 16, transcendentals=0
        ),
        name="feed",
    )(place, rows, bias, source)


def feed_back_kernel(starts, place_ref, grad_ref, slope_ref, source_ref, pre_ref, out_ref, bias_ref, expand_held, reduce_held, sems):
    held = (expand_held, reduce_held)
    step = pl.program_id(0)
    @pl.when(step == 0)
    def _():
        start_parts(place_ref, source_ref, starts, held, sems)

    reduce = wait_part(source_ref, 1, held, sems, step)
    total = jnp.zeros((1, D), jnp.float32)
    for at in range(0, SEQ_LEN, 304):
        spot = slice(at, at + 304)
        grad = row_dot(grad_ref[spot, :], reduce) * slope_ref[spot, :].astype(jnp.float32)
        low = grad.astype(jnp.bfloat16)
        pre_ref[spot, :] = low
        total = total + jnp.sum(low.astype(jnp.float32), axis=0, keepdims=True)
    bias_ref[...] = total
    low = pre_ref[...]
    expand = wait_part(source_ref, 0, held, sems, step)
    part = jnp.dot(low, expand, preferred_element_type=jnp.float32)
    @pl.when(step == 0)
    def _():
        out_ref[...] = part
    @pl.when(step > 0)
    def _():
        out_ref[...] += part

def feed_back_call(place, grad, slope, source, starts):
    whole = lambda step, place: (0, 0)
    chunk = pl.BlockSpec((SEQ_LEN, D), lambda step, place: (0, step))
    return pl.pallas_call(
        partial(feed_back_kernel, starts),
        grid_spec=pltpu.PrefetchScalarGridSpec(
            num_scalar_prefetch=1,
            grid=(PARTS,),
            in_specs=[
                pl.BlockSpec((SEQ_LEN, D), whole),
                chunk,
                pl.BlockSpec(memory_space=pl.ANY),
            ],
            out_specs=[
                chunk,
                pl.BlockSpec((SEQ_LEN, D), whole),
                pl.BlockSpec((1, D), lambda step, place: (0, step)),
            ],
            scratch_shapes=[
                pltpu.VMEM((PARTS, PART_BLOCKS, BLOCK, D), jnp.bfloat16),
                pltpu.VMEM((PARTS, PART_BLOCKS, BLOCK, D), jnp.bfloat16),
                pltpu.SemaphoreType.DMA((2, PARTS)),
            ],
        ),
        out_shape=[
            jax.ShapeDtypeStruct((SEQ_LEN, FF), jnp.bfloat16),
            jax.ShapeDtypeStruct((SEQ_LEN, D), jnp.float32),
            jax.ShapeDtypeStruct((1, FF), jnp.float32),
        ],
        compiler_params=pltpu.CompilerParams(vmem_limit_bytes=48 << 20),
        cost_estimate=pl.CostEstimate(
            flops=SEQ_LEN * D * FF, bytes_accessed=1 << 16, transcendentals=0
        ),
        name="feed_back",
    )(place, grad, slope, source)


def adam_step(weight, mean_state, square, gradient, step_rate, decay_rate, step_count):
    mean_next = ADAM_BETA1 * mean_state + (1.0 - ADAM_BETA1) * gradient
    square_next = ADAM_BETA2 * square + (1.0 - ADAM_BETA2) * gradient * gradient
    step_float = step_count.astype(jnp.float32)
    mean_hat = mean_next / (1.0 - ADAM_BETA1**step_float)
    square_hat = square_next / (1.0 - ADAM_BETA2**step_float)
    updated = weight - step_rate * (
        mean_hat / (jnp.sqrt(square_hat) + ADAM_EPS) + decay_rate * weight
    )
    return (updated, mean_next, square_next)


def on_device(
    codons,
    offsets,
    positions,
    targets,
    table_weight,
    attend_weight,
    mixing_weight,
    expand_weight,
    reduce_weight,
    vector_params,
    attend_moment,
    mixing_moment,
    expand_moment,
    reduce_moment,
    table_mean,
    table_square,
    vector_mean,
    vector_square,
    step_count,
):
    low_type = jnp.bfloat16
    wide_at = lax.axis_index("wide")
    me = my_index()
    devices = lax.axis_size(BOTH)
    masks = wide_masks()
    narrow_size = lax.axis_size("narrow")
    wide_size = lax.axis_size("wide")
    hidden_masks = masks[:-1] + [2, masks[-1], 1]
    all_masks = masks + [2, 1]
    small = jnp.concatenate([table_weight, vector_params], axis=0).astype(low_type)
    small = gather_blocks(small[None], masks)
    packed = (expand_weight, reduce_weight, attend_weight, mixing_weight)
    units = [weight.shape[0] // narrow_size for weight in packed]
    starts = np.cumsum([0] + [unit + -unit % 16 for unit in units])
    weights_low = lax.all_gather(pack_rows(packed, lax.axis_index("narrow")), BOTH, axis=0)

    def weight_rows(number, unit):
        start = int(starts[number])
        return weights_low[:, start : start + unit].reshape(-1, D)

    codons, positions, targets = gate((codons, positions, targets), small)
    small = in_order(small, masks, narrow_size, wide_at)
    small = jnp.transpose(small, (1, 0, 2)).reshape(VOCAB + 15, D)
    table_low = small[:VOCAB]
    vector_full = small[VOCAB:].astype(jnp.float32)
    gain_one = vector_full[0]
    bias_one = vector_full[1]
    gain_two = vector_full[2]
    bias_two = vector_full[3]
    gain_last = vector_full[4]
    bias_last = vector_full[5]
    attend_bias = vector_full[6:9].reshape(1, 3 * D)
    mixing_bias = vector_full[9]
    reduce_bias = vector_full[10]
    expand_bias = out_of_order(
        vector_full[11:15].reshape(devices, FF // devices), hidden_masks, 1, me
    ).reshape(FF)
    embed_scale = math.sqrt(D)
    table_stream = embed_scale * table_low.astype(jnp.float32)
    table_normed = norm_forward(table_stream, gain_one, bias_one)[0].astype(low_type)
    table_own = times_trans(table_normed, attend_weight.astype(low_type))
    place = jnp.asarray(places_of(masks, narrow_size), jnp.int32)[jnp.arange(wide_size) ^ wide_at]
    tables = heads_table(gather_blocks(table_own[None], masks), place, attend_bias)

    unit = FF // devices
    hidden_place = jnp.asarray(offsets_of(hidden_masks)) ^ me
    if unit == BLOCK:
        feed_place, feed_source, feed_starts = hidden_place, weights_low, tuple(starts[:2])
    else:
        feed_source = jnp.concatenate(
            [
                take_blocks(weights_low[:, start : start + unit], hidden_place).reshape(-1, BLOCK, D)
                for start in (int(starts[0]), int(starts[1]))
            ],
            axis=1,
        )
        feed_place, feed_starts = jnp.arange(FF // BLOCK), (0, BLOCK)
    feed_place = feed_place.astype(jnp.int32)
    feed_starts = tuple(int(start) for start in feed_starts)

    seq_count = codons.shape[0]
    row_count = seq_count * SEQ_LEN
    window = jax.vmap(partial(lax.dynamic_slice_in_dim, slice_size=SEQ_LEN))(codons, offsets)
    vocab_ids = jnp.arange(VOCAB, dtype=jnp.int32)
    token_hot = window.reshape(row_count)[:, None] == vocab_ids[None, :]
    token_low = token_hot.astype(low_type)
    target_hot = (targets.reshape(row_count)[:, None] == vocab_ids[None, :]).astype(jnp.float32)
    stream = embed_scale * times_plain(token_low, table_low)
    token_ids = window.reshape(row_count)
    lane_ids = jnp.arange(2 * LANES, dtype=jnp.int32) % LANES
    hot = (token_ids[:, None] == lane_ids[None, :]).astype(low_type)
    hot_turned = (token_ids[None, :] == lane_ids[:LANES, None]).astype(low_type)
    cosine, sine_table = rotary_tables(positions.reshape(row_count))
    cosine = jnp.concatenate([cosine] * 4, axis=1)
    sine_table = jnp.concatenate([-sine_table, sine_table] * 2, axis=1)
    pairs = D // PAIR // ATTEND_CALLS
    attended = []

    for number in range(ATTEND_CALLS):
        attended.append(
            attend_call(hot, tables, cosine, sine_table, number * pairs, pairs)
        )
    last_mask = masks[-1]
    mixed_low = jnp.concatenate([parts[3] for parts in attended], axis=1)
    mixing_low = weight_rows(3, D // devices)
    branch = times_trans(mixed_low, mixing_low) + mixing_bias
    middle = stream + branch
    normed_two, normal_two, inverse_two = norm_forward(middle, gain_two, bias_two)
    normed_two_low = normed_two.astype(low_type)
    hidden_low, slope_low, feed_out = feed_call(
        feed_place, normed_two_low, expand_bias[None, :], feed_source, feed_starts
    )
    feed_out = feed_out + reduce_bias
    output = middle + feed_out
    final_norm, normal_last, inverse_last = norm_forward(output, gain_last, bias_last)
    final_low = final_norm.astype(low_type)
    logits = times_trans(final_low, table_low)
    row_peak = jnp.max(logits, axis=-1, keepdims=True)
    shifted = jnp.exp(logits - row_peak)
    prob_rows = shifted / jnp.sum(shifted, axis=-1, keepdims=True)
    prob_sum = jnp.sum(prob_rows, axis=0)
    logit_grad = (prob_rows - target_hot).astype(low_type)
    final_grad = times_plain(logit_grad, table_low)
    table_head = trans_times(logit_grad, final_low)
    output_grad, gain_last_grad, bias_last_grad = norm_backward(
        final_grad, normal_last, inverse_last, gain_last
    )
    feed_low = output_grad.astype(low_type)
    reduce_bias_grad = jnp.sum(feed_low, axis=0, dtype=jnp.float32)
    half_ff = FF // 2
    static_marks = [masks[-1], 2] + list(reversed(masks[:-1]))
    static_shape = (2,) * len(static_marks) + (unit, D)

    reduce_send = trans_times(hidden_low[:, half_ff:], feed_low).astype(low_type)
    reduce_sum = trans_times(hidden_low[:, :half_ff], feed_low) + swap(reduce_send, 1)
    reduce_chain = sum_chain([(reduce_sum.reshape(static_shape), static_marks, False)], jnp.float32)
    sent = next(reduce_chain)
    pre_grad, normed_two_grad, expand_bias_grad = feed_back_call(
        feed_place, gate(feed_low, sent), slope_low, feed_source, feed_starts
    )
    sent = reduce_chain.send(pre_grad)
    expand_send = trans_times(
        gate(pre_grad, sent)[:, half_ff:], normed_two_low
    ).astype(low_type)
    expand_sum = trans_times(pre_grad[:, :half_ff], normed_two_low) + swap(expand_send, 1)
    middle_part, gain_two_grad, bias_two_grad = norm_backward(
        normed_two_grad, normal_two, inverse_two, gain_two
    )
    middle_grad = output_grad + middle_part
    branch_low = middle_grad.astype(low_type)
    mixing_bias_grad = jnp.sum(branch_low, axis=0, dtype=jnp.float32)
    mixing_sum = trans_times(branch_low, mixed_low).reshape(
        bits_shape(devices, (D // devices, D))
    )
    (mixing_item,) = finish_hop(hop([(mixing_sum, all_masks, True)], 1, low_type))
    mixed_grad = times_plain(branch_low, mixing_low).astype(low_type)
    expand_chain = sum_chain(
        [(expand_sum.reshape(static_shape), static_marks, False), mixing_item], low_type
    )
    expand_sent = next(expand_chain)
    reduce_sent = reduce_chain.send(expand_sum)

    backs = []
    back_pairs = D // PAIR // BACK_CALLS

    def back_step(waits):
        number = len(backs)
        first = number * back_pairs
        source = attended[first // pairs]
        order = (backs[-1][1],) if backs else ()
        backs.append(
            attend_back_call(
                hot_turned,
                *source[:3],
                gate(mixed_grad, (waits, order)),
                source[4],
                cosine,
                sine_table,
                first,
                first % pairs,
                back_pairs,
            )
        )
        return backs[-1][1]

    back_step((expand_sent, reduce_sent))
    token = back_step(())
    expand_sent = expand_chain.send(token)
    reduce_sent = reduce_chain.send(token)
    token = back_step((expand_sent, reduce_sent))
    expand_sent = expand_chain.send(token)
    token = back_step(expand_sent)
    (reduce_sum,) = drain(reduce_chain, token)
    token = back_step(())
    expand_sent = expand_chain.send(token)
    token = back_step(expand_sent)
    expand_sum, mixing_sum = drain(expand_chain, token)
    token_sums, attend_bias_grad = sums_blocks([back[1] for back in backs], wide_size)
    dense = join_narrow(jnp.concatenate([reduce_sum, expand_sum, mixing_sum], axis=0))
    reduce_total = dense[:, :unit].reshape(-1, D)
    expand_total = dense[:, unit : 2 * unit].reshape(-1, D)
    mixing_total = dense[:, 2 * unit :].reshape(-1, D)
    spot = lax.axis_index("narrow")

    def step_of(moment, gradient):
        moment_next = MUON_MU * moment + (1.0 - MUON_MU) * gradient
        return moment_next, (1.0 - MUON_MU) * gradient + MUON_MU * moment_next

    mixing_next, mixing_step = step_of(mixing_moment, mixing_total)
    expand_next, expand_step = step_of(expand_moment, expand_total)
    reduce_next, reduce_step = step_of(reduce_moment, reduce_total)
    attend_base = (MUON_MU * MUON_MU) * attend_moment
    gram_parts = sum_gram(
        local_gram(pick_rows((attend_base, mixing_step, expand_step, reduce_step), spot))
    )

    token_sums, token_first = sum_small(token_sums)
    attend_total = lax.dot_general(
        token_sums,
        table_normed.astype(jnp.float32),
        (((0,), (0,)), ((), ())),
        precision=lax.Precision.HIGHEST,
        preferred_element_type=jnp.float32,
    )
    attend_next, attend_step = step_of(attend_moment, attend_total)
    gradient_rate = (1.0 - MUON_MU) * (1.0 + MUON_MU)
    crossed = exact_times(
        token_sums, jnp.concatenate([attend_moment, token_sums.T], axis=1)
    )
    crossed = sum_wide(crossed)
    table_wide = table_normed.astype(jnp.float32)
    added = gradient_rate * (
        (MUON_MU * MUON_MU) * crossed[:, :D]
        + (0.5 * gradient_rate) * exact_times(crossed[:, D:], table_wide)
    )
    added = jnp.where(spot == 0, added, 0.0)
    added_high = rounded(added)
    added_low = rounded(added - added_high)
    added_least = added - added_high - added_low
    table_three = [table_normed] * 3
    added_three = [part.astype(low_type) for part in (added_high, added_low, added_least)]
    room = ((0, -(-6 * VOCAB // 16) * 16 - 6 * VOCAB), (0, 0))
    add_left = jnp.pad(jnp.concatenate(added_three + table_three, axis=0), room)
    add_right = jnp.pad(jnp.concatenate(table_three + added_three, axis=0), room)

    lows = gate([back[0] for back in backs], token_first)
    projected_low = jnp.concatenate([low[kind] for kind in range(3) for low in lows], axis=1)
    attend_low = gate(weights_low, token_first)[:, int(starts[2]) : int(starts[2]) + units[2]]
    normed_one_grad = times_plain(projected_low, attend_low.reshape(3 * D, D))
    normed_one, normal_one, inverse_one = norm_forward(stream, gain_one, bias_one)
    stream_part, gain_one_grad, bias_one_grad = norm_backward(
        normed_one_grad, normal_one, inverse_one, gain_one
    )
    entry_gradient = middle_grad + stream_part
    table_grad = (
        embed_scale * exact_times(token_hot.astype(jnp.float32).T, entry_gradient) + table_head
    )
    (
        gain_two_grad,
        bias_two_grad,
        gain_last_grad,
        bias_last_grad,
        mixing_bias_grad,
        reduce_bias_grad,
        expand_bias_grad,
        prob_sum,
    ) = gate(
        (
            gain_two_grad,
            bias_two_grad,
            gain_last_grad,
            bias_last_grad,
            mixing_bias_grad,
            reduce_bias_grad,
            expand_bias_grad,
            prob_sum,
        ),
        token_first,
    )
    expand_bias_grad = in_order(
        expand_bias_grad.reshape(devices, FF // devices), hidden_masks, 1, me
    )
    vector_grad = jnp.concatenate(
        [
            jnp.stack(
                [
                    gain_one_grad,
                    bias_one_grad,
                    gain_two_grad,
                    bias_two_grad,
                    gain_last_grad,
                    bias_last_grad,
                ]
            ),
            attend_bias_grad.reshape(3, D),
            mixing_bias_grad[None, :],
            reduce_bias_grad[None, :],
            expand_bias_grad.reshape(4, D),
        ],
        axis=0,
    )
    columns = D // wide_size
    rows_hist = -(-VOCAB // columns)
    hist_part = jnp.pad(prob_sum, (0, rows_hist * columns - VOCAB)).reshape(rows_hist, columns)
    small_grads = jnp.concatenate([table_grad, vector_grad], axis=0)
    small_grads = jnp.transpose(small_grads.reshape(VOCAB + 15, wide_size, columns), (1, 0, 2))
    small_grads = jnp.concatenate(
        [small_grads, jnp.broadcast_to(hist_part, (wide_size, rows_hist, columns))], axis=1
    )
    small_total, _ = sum_small(small_grads)
    table_total = small_total[:VOCAB]
    vector_total = small_total[VOCAB : VOCAB + 15]
    prob_total = small_total[VOCAB + 15 :].reshape(rows_hist * columns)[:VOCAB]
    histogram = prob_total * (VOCAB / (row_count * devices))
    totals = (attend_total, mixing_total, expand_total, reduce_total)
    moment_next = (attend_next, mixing_next, expand_next, reduce_next)
    rows = pick_rows((attend_step, mixing_step, expand_step, reduce_step), spot)
    rows = gate(rows, small_total)
    ortho = newton_rows(gram_parts, rows, add_left, add_right)
    pair = jnp.stack([ortho, swap(ortho, 2)])
    matrices = (attend_weight, mixing_weight, expand_weight, reduce_weight)
    rates = tuple(
        MUON_RATE * SHAPE_FACTOR * math.sqrt(max(rows, D)) for rows in (3 * D, D, FF, FF)
    )
    matrix_new = tuple(update_rows(spot, pair, swap(pair, 1), matrices, rates))
    table_new, table_mean_next, table_square_next = adam_step(
        table_weight, table_mean, table_square, table_total, TABLE_RATE, TABLE_DECAY, step_count
    )
    vector_new, vector_mean_next, vector_square_next = adam_step(
        vector_params, vector_mean, vector_square, vector_total, VECTOR_RATE, 0.0, step_count
    )
    results = (
        totals
        + (table_total, vector_total)
        + matrix_new
        + moment_next
        + (
            table_new,
            table_mean_next,
            table_square_next,
            vector_new,
            vector_mean_next,
            vector_square_next,
        )
    )
    block_output = output.astype(low_type).reshape(seq_count, SEQ_LEN, D)
    return (block_output, entry_gradient.reshape(seq_count, SEQ_LEN, D)) + results + (histogram,)


def solution(mesh):
    in_specs = (
        P(("wide", "narrow"), None),
        P(("wide", "narrow")),
        P(("wide", "narrow"), None),
        P(("wide", "narrow"), None),
        P(None, "wide"),
        P("wide", None),
        P("wide", None),
        P("wide", None),
        P("wide", None),
        P(None, "wide"),
        P("wide", None),
        P("wide", None),
        P("wide", None),
        P("wide", None),
        P(None, "wide"),
        P(None, "wide"),
        P(None, "wide"),
        P(None, "wide"),
        P(),
    )
    out_specs = (
        P(("wide", "narrow"), None, None),
        P(("wide", "narrow"), None, None),
        P("wide", None),
        P("wide", None),
        P("wide", None),
        P("wide", None),
        P(None, "wide"),
        P(None, "wide"),
        P("wide", None),
        P("wide", None),
        P("wide", None),
        P("wide", None),
        P("wide", None),
        P("wide", None),
        P("wide", None),
        P("wide", None),
        P(None, "wide"),
        P(None, "wide"),
        P(None, "wide"),
        P(None, "wide"),
        P(None, "wide"),
        P(None, "wide"),
        P(),
    )
    return jax.shard_map(
        on_device, mesh=mesh, in_specs=in_specs, out_specs=out_specs, check_vma=False
    )
```

```python
from functools import partial
import math

import jax
import jax.numpy as jnp
import numpy as np
from jax import lax
from jax.experimental import pallas as pl
from jax.experimental.pallas import tpu as pltpu
from jax.sharding import PartitionSpec as P

D = 768
HEADS = 12
HEAD_DIM = 64
FF = 3072
VOCAB = 70
SEQ_LEN = 912
NS_ITERS = 5


NORM_EPS = 1e-05
ROPE_BASE = 10000.0
NEWTON_A = 3.4445
NEWTON_B = -4.775
NEWTON_C = 2.0315
MUON_MU = 0.95
MUON_RATE = 0.3
MUON_DECAY = 0.1
SHAPE_FACTOR = 0.2
ADAM_BETA1 = 0.9
ADAM_BETA2 = 0.95
ADAM_EPS = 1e-08
TABLE_RATE = 0.03
TABLE_DECAY = 0.01
VECTOR_RATE = 0.2


def times_plain(left_side, right_side):
    return jnp.dot(left_side, right_side, preferred_element_type=jnp.float32)


def times_trans(left_side, right_side):
    return lax.dot_general(
        left_side, right_side, (((1,), (1,)), ((), ())), preferred_element_type=jnp.float32
    )


def trans_times(left_side, right_side):
    return lax.dot_general(
        left_side, right_side, (((0,), (0,)), ((), ())), preferred_element_type=jnp.float32
    )


def exact_times(left_side, right_side):
    return jnp.dot(
        left_side, right_side, precision=lax.Precision.HIGHEST, preferred_element_type=jnp.float32
    )


def norm_forward(values, gain_row, bias_row):
    center = values - jnp.mean(values, axis=-1, keepdims=True)
    spread = jnp.mean(center * center, axis=-1, keepdims=True)
    inverse = lax.rsqrt(spread + NORM_EPS)
    normal = center * inverse
    return (normal * gain_row + bias_row, normal, inverse)


def norm_backward(upstream, normal, inverse, gain_row):
    scaled = upstream * gain_row
    inner_part = (
        scaled
        - jnp.mean(scaled, axis=-1, keepdims=True)
        - normal * jnp.mean(scaled * normal, axis=-1, keepdims=True)
    )
    return (inverse * inner_part, jnp.sum(upstream * normal, axis=0), jnp.sum(upstream, axis=0))


def rotary_tables(positions):
    half_dim = HEAD_DIM // 2
    frequency = ROPE_BASE ** (-(jnp.arange(half_dim, dtype=jnp.float32) * 2.0 / HEAD_DIM))
    turned = positions.astype(jnp.float32)[..., None] * frequency
    return (jnp.cos(turned), jnp.sin(turned))


PAIR = 2 * HEAD_DIM
SPAN = 1024
STRIP = 256
PARTS = 4
BLOCK = 96
PART_BLOCKS = D // BLOCK
LANES = 128
ATTEND_CALLS = 3
BACK_CALLS = 6


BOTH = ("wide", "narrow")
GRAM_TILE = 256
GRAM_SPOTS = ((0, 0), (0, 1), (0, 2), (1, 1), (1, 2), (2, 2))


def swap(value, mask):
    total = lax.axis_size(BOTH)
    return lax.ppermute(value, BOTH, [(spot, spot ^ mask) for spot in range(total)])


def my_index():
    return lax.axis_index("wide") * lax.axis_size("narrow") + lax.axis_index("narrow")


def wide_masks():
    narrow_size = lax.axis_size("narrow")
    count = lax.axis_size("wide").bit_length() - 1
    return [narrow_size << bit for bit in reversed(range(count))]


def offsets_of(masks):
    table = [0]
    for mask in masks:
        table = table + [offset ^ mask for offset in table]
    return np.array(table)


def gate(value, others):
    leaves, form = jax.tree.flatten(value)
    held = lax.optimization_barrier(tuple(leaves) + tuple(jax.tree.leaves(others)))
    return jax.tree.unflatten(form, held[: len(leaves)])


def padded_rows(array):
    return jnp.pad(array, ((0, -array.shape[0] % 16), (0, 0)))


def together(values):
    leaves, form = jax.tree.flatten(values)
    return jax.tree.unflatten(form, lax.optimization_barrier(tuple(leaves)))


def gather_blocks(piece, masks):
    for mask in masks:
        piece = jnp.concatenate([piece, swap(piece, mask)], axis=0)
    return piece


def take_blocks(array, index):
    return jnp.take(array, index, axis=0, mode="clip")


def places_of(masks, unit):
    offsets = offsets_of(masks) // unit
    place = np.zeros_like(offsets)
    place[offsets] = np.arange(offsets.size)
    return place


def in_order(blocks, masks, unit, base):
    place = places_of(masks, unit)
    return take_blocks(blocks, jnp.asarray(place)[jnp.arange(place.size) ^ base])


def out_of_order(blocks, masks, unit, base):
    offsets = offsets_of(masks) // unit
    return take_blocks(blocks, jnp.asarray(offsets) ^ base)


def quarter_rows(array):
    count = array.shape[0] // lax.axis_size("narrow")
    return lax.dynamic_slice_in_dim(array, lax.axis_index("narrow") * count, count, 0)


def side_of(mask):
    return (my_index() // mask) % 2


def split_static(array, axis):
    return lax.index_in_dim(array, 0, axis, False), lax.index_in_dim(array, 1, axis, False)


def split_sided(array, axis, mask):
    side = side_of(mask)
    return (
        lax.dynamic_index_in_dim(array, side, axis, False),
        lax.dynamic_index_in_dim(array, 1 - side, axis, False),
    )


def halves(item, mask):
    array, marks, sided = item
    axis = marks.index(mask)
    keep, send = split_sided(array, axis, mask) if sided else split_static(array, axis)
    return (keep, marks[:axis] + marks[axis + 1 :], sided), send


def hop(items, mask, kind):
    pairs = [halves(item, mask) for item in items]
    rows = [send.astype(kind).reshape(-1, send.shape[-1]) for _, send in pairs]
    flat = jnp.concatenate(rows, axis=0) if len(rows) > 1 else rows[0]
    token = yield flat
    got = gate(swap(flat, mask), token)
    results, at = [], 0
    for ((keep, marks, sided), send), row in zip(pairs, rows):
        part = got[at : at + row.shape[0]].reshape(send.shape).astype(jnp.float32)
        results.append((keep + part, marks, sided))
        at += row.shape[0]
    return results


def finish(steps, token):
    try:
        steps.send(token)
    except StopIteration as stop:
        return stop.value


def finish_hop(steps):
    next(steps)
    return finish(steps, ())


def columns_of(items, start, stop):
    return [(array[..., start:stop], marks, sided) for array, marks, sided in items]


def sum_chain(items, kind):
    masks = wide_masks()
    width = items[0][0].shape[-1]
    ways = [columns_of(items, 0, width // 2), columns_of(items, width // 2, width)]
    for pair in ((masks[-1], 2), (2, masks[-1])):
        steps = [hop(way, mask, jnp.bfloat16) for way, mask in zip(ways, pair)]
        token = yield tuple(next(step) for step in steps)
        ways = [finish(step, token) for step in steps]
    items = [
        (jnp.concatenate([left[0], right[0]], axis=-1), left[1], left[2])
        for left, right in zip(*ways)
    ]
    for mask in reversed(masks[:-1]):
        items = yield from hop(items, mask, kind)
    return [item[0] for item in items]


def drain(chain, token):
    while True:
        try:
            chain.send(token)
        except StopIteration as stop:
            return stop.value


def bits_shape(count, tail):
    return (2,) * (count.bit_length() - 1) + tuple(tail)


class Chain:
    def __init__(self, steps):
        self.steps, self.result = steps, None
        self.request = next(steps)

    def give(self, got):
        try:
            self.request = self.steps.send(got)
        except StopIteration as stop:
            self.request, self.result = [], stop.value


def advance(chains, meanwhile=None, needs=()):
    sends, needs = together(([[array for array, _ in chain.request] for chain in chains], needs))
    gots = [
        [swap(array, mask) for array, (_, mask) in zip(send, chain.request)]
        for send, chain in zip(sends, chains)
    ]
    made = meanwhile(needs) if meanwhile else ()
    gots, made = together((gots, made))
    for chain, got in zip(chains, gots):
        chain.give(got)
    return made


def sum_small(blocks):
    (got,) = yield [(blocks, 1)]
    total = (blocks + got).reshape(bits_shape(blocks.shape[0], blocks.shape[1:]))
    masks = wide_masks()
    while masks:
        mask = masks[-1]
        keep, send = split_sided(total, len(masks) - 1, mask)
        (got,) = yield [(send, mask)]
        total = keep + got
        masks = masks[:-1]
    (got,) = yield [(total, 2)]
    return total + got


def sum_wide(value):
    for mask in reversed(wide_masks()):
        (got,) = yield [(value, mask)]
        value = value + got
    return value


def sum_gram(parts):
    masks = list(reversed(wide_masks()))
    ways = [masks, [masks[1], masks[0]] + masks[2:]]
    parts = list(parts)
    for step in range(len(masks)):
        pairs = [
            split_sided(part.reshape((2, part.shape[0] // 2) + part.shape[1:]), 0, way[step])
            for part, way in zip(parts, ways)
        ]
        gots = yield [(send, way[step]) for (_, send), way in zip(pairs, ways)]
        parts = [keep + got for (keep, _), got in zip(pairs, gots)]
    for step in reversed(range(len(masks))):
        gots = yield [(part, way[step]) for part, way in zip(parts, ways)]
        parts = [
            jnp.where(
                side_of(way[step]) == 0,
                jnp.concatenate([part, got], axis=0),
                jnp.concatenate([got, part], axis=0),
            )
            for part, got, way in zip(parts, gots, ways)
        ]
    return parts


def row_dot(left_side, right_side):
    return lax.dot_general(
        left_side, right_side, (((1,), (1,)), ((), ())), preferred_element_type=jnp.float32
    )


def split_two(values):
    high = values.astype(jnp.bfloat16)
    return high, (values - high.astype(jnp.float32)).astype(jnp.bfloat16)


def newton_kernel(
    low_ref, high_ref, rows_ref, added_ref, table_ref, out_ref,
    gram_now, other, left, right, rows_left,
):
    tile = GRAM_TILE
    trace = jnp.zeros((1, 1), jnp.float32)
    diagonal = lax.broadcasted_iota(jnp.int32, (tile, tile), 0) == lax.broadcasted_iota(
        jnp.int32, (tile, tile), 1
    )

    def span(number):
        return slice(number * tile, (number + 1) * tile)

    def turned_dot(left_side, right_side):
        return lax.dot_general(
            left_side,
            right_side,
            (((0,), (0,)), ((), ())),
            preferred_element_type=jnp.float32,
        )

    added_high, added_low = split_two(added_ref[...])
    added_rest = added_ref[...] - added_high.astype(jnp.float32) - added_low.astype(jnp.float32)
    added_parts = (added_high, added_low, added_rest.astype(jnp.bfloat16))
    half = len(GRAM_SPOTS) // 2
    for number, (row, column) in enumerate(GRAM_SPOTS):
        source = low_ref if number < half else high_ref
        block = source[span(number % half), :]
        for part in added_parts:
            block = block + turned_dot(part[:, span(row)], table_ref[:, span(column)])
            block = block + turned_dot(table_ref[:, span(row)], part[:, span(column)])
        gram_now[span(row), span(column)] = block
        if row == column:
            picked = jnp.where(diagonal, block, 0.0)
            trace = trace + jnp.sum(jnp.sum(picked, axis=0, keepdims=True), axis=1, keepdims=True)
    inverse = 1.0 / (jnp.sqrt(trace) + 1e-07)
    scale = inverse * inverse
    for row, column in GRAM_SPOTS:
        block = gram_now[span(row), span(column)] * scale
        gram_now[span(row), span(column)] = block
        if row != column:
            gram_now[span(column), span(row)] = block.T

    def set_left(values):
        high, low = split_two(values)
        left[:, 0:D] = high
        left[:, D : 2 * D] = high
        left[:, 2 * D : 3 * D] = low

    def set_right(values):
        high, low = split_two(values)
        right[0:D, :] = high
        right[D : 2 * D, :] = low
        right[2 * D : 3 * D, :] = high

    def set_rows(values):
        high, low = split_two(values)
        rows_left[:, 0:D] = high
        rows_left[:, D : 2 * D] = high
        rows_left[:, 2 * D : 3 * D] = low

    def product(target, finish):
        for column in range(D // tile):
            rows = (column + 1) * tile
            block = jnp.dot(left[0:rows, :], right[:, span(column)], preferred_element_type=jnp.float32)
            for row in range(column + 1):
                piece = finish(block[span(row), :], row, column)
                target[span(row), span(column)] = piece
                if row != column:
                    target[span(column), span(row)] = piece.T

    def same(block, row, column):
        return block

    def factor(block, row, column):
        block = NEWTON_B * gram_now[span(row), span(column)] + NEWTON_C * block
        if row == column:
            block = block + jnp.where(diagonal, NEWTON_A, 0.0)
        return block

    def set_factor():
        set_left(gram_now[...])
        set_right(gram_now[...])
        product(other, factor)
        set_right(other[...])

    def rows_product():
        return jnp.dot(rows_left[...], right[...], preferred_element_type=jnp.float32)

    set_rows(rows_ref[...] * inverse)

    def body(step, carry):
        set_factor()
        product(other, same)
        set_left(other[...])
        product(gram_now, same)
        set_rows(rows_product())
        return carry

    lax.fori_loop(0, NS_ITERS - 1, body, 0)
    set_factor()
    out_ref[...] = rows_product().astype(out_ref.dtype)


def newton_rows(gram_parts, rows, added, table):
    count = rows.shape[0]
    return pl.pallas_call(
        newton_kernel,
        out_shape=jax.ShapeDtypeStruct((count, D), jnp.bfloat16),
        in_specs=[pl.BlockSpec(memory_space=pltpu.VMEM)] * 5,
        out_specs=pl.BlockSpec(memory_space=pltpu.VMEM),
        scratch_shapes=[
            pltpu.VMEM((D, D), jnp.float32),
            pltpu.VMEM((D, D), jnp.float32),
            pltpu.VMEM((D, 3 * D), jnp.bfloat16),
            pltpu.VMEM((3 * D, D), jnp.bfloat16),
            pltpu.VMEM((count, 3 * D), jnp.bfloat16),
        ],
        compiler_params=pltpu.CompilerParams(vmem_limit_bytes=48 << 20),
        cost_estimate=pl.CostEstimate(flops=60 * D * D * D, bytes_accessed=4 << 20, transcendentals=0),
        name="newton",
    )(*gram_parts, rows, added, table)


def pack_kernel(spot_ref, *refs):
    out_ref = refs[-1]
    at = 0
    for ref in refs[:-1]:
        count = ref.shape[0]
        out_ref[at : at + count, :] = ref[...].astype(jnp.bfloat16)
        at += count
        room = -count % 16
        if room:
            out_ref[at : at + room, :] = jnp.zeros((room, D), jnp.bfloat16)
            at += room


def pack_rows(weights, spot):
    units = [weight.shape[0] // lax.axis_size("narrow") for weight in weights]
    total = sum(unit + -unit % 16 for unit in units)
    if any(unit % 8 for unit in units):
        return jnp.concatenate(
            [padded_rows(quarter_rows(weight).astype(jnp.bfloat16)) for weight in weights], axis=0
        )
    return pl.pallas_call(
        pack_kernel,
        grid_spec=pltpu.PrefetchScalarGridSpec(
            num_scalar_prefetch=1,
            grid=(1,),
            in_specs=[pl.BlockSpec((unit, D), lambda step, spot: (spot[0], 0)) for unit in units],
            out_specs=pl.BlockSpec((total, D), lambda step, spot: (0, 0)),
        ),
        out_shape=jax.ShapeDtypeStruct((total, D), jnp.bfloat16),
        name="pack",
    )(spot[None].astype(jnp.int32), *weights)


def entry_kernel(scale, *refs):
    (hot_ref, table_ref, gain_ref, middle_ref, weight_ref), refs = refs[:5], refs[5:]
    *low_refs, entry_ref, sums_ref, table_sum_ref = refs
    step = pl.program_id(0)
    hot = hot_ref[:, 0:LANES]
    stream = scale * jnp.dot(hot, table_ref[...], preferred_element_type=jnp.float32)
    grads = None
    for kind in range(3):
        low = jnp.concatenate([ref[kind] for ref in low_refs], axis=1)
        part = jnp.dot(
            low, weight_ref[kind * D : (kind + 1) * D, :], preferred_element_type=jnp.float32
        )
        grads = part if grads is None else grads + part
    center = stream - jnp.mean(stream, axis=-1, keepdims=True)
    inverse = lax.rsqrt(jnp.mean(center * center, axis=-1, keepdims=True) + NORM_EPS)
    normal = center * inverse
    scaled = grads * gain_ref[...]
    inner = (
        scaled
        - jnp.mean(scaled, axis=-1, keepdims=True)
        - normal * jnp.mean(scaled * normal, axis=-1, keepdims=True)
    )
    entry = middle_ref[...] + inverse * inner
    entry_ref[...] = entry
    sums = jnp.concatenate(
        [
            jnp.sum(grads * normal, axis=0, keepdims=True),
            jnp.sum(grads, axis=0, keepdims=True),
        ],
        axis=0,
    )
    high = entry.astype(jnp.bfloat16)
    rest = entry - high.astype(jnp.float32)
    middle = rest.astype(jnp.bfloat16)
    low = (rest - middle.astype(jnp.float32)).astype(jnp.bfloat16)
    table_sum = None
    for part in (high, middle, low):
        part = lax.dot_general(
            hot, part, (((0,), (0,)), ((), ())), preferred_element_type=jnp.float32
        )
        table_sum = part if table_sum is None else table_sum + part

    @pl.when(step == 0)
    def _():
        sums_ref[...] = sums
        table_sum_ref[...] = scale * table_sum

    @pl.when(step > 0)
    def _():
        sums_ref[...] += sums
        table_sum_ref[...] += scale * table_sum


def entry_call(scale, hot, table, gain, middle_grad, weight, lows):
    rows = SEQ_LEN // 3
    whole = lambda step: (0, 0)
    own = lambda step: (step, 0)
    return pl.pallas_call(
        partial(entry_kernel, scale),
        grid=(3,),
        in_specs=[
            pl.BlockSpec((rows, hot.shape[1]), own),
            pl.BlockSpec(table.shape, whole),
            pl.BlockSpec(gain.shape, whole),
            pl.BlockSpec((rows, D), own),
            pl.BlockSpec(weight.shape, whole),
        ]
        + [pl.BlockSpec((3, rows, low.shape[2]), lambda step: (0, step, 0)) for low in lows],
        out_specs=[
            pl.BlockSpec((rows, D), own),
            pl.BlockSpec((2, D), whole),
            pl.BlockSpec((LANES, D), whole),
        ],
        out_shape=[
            jax.ShapeDtypeStruct((SEQ_LEN, D), jnp.float32),
            jax.ShapeDtypeStruct((2, D), jnp.float32),
            jax.ShapeDtypeStruct((LANES, D), jnp.float32),
        ],
        compiler_params=pltpu.CompilerParams(vmem_limit_bytes=48 << 20),
        cost_estimate=pl.CostEstimate(flops=1 << 20, bytes_accessed=1 << 16, transcendentals=0),
        name="entry",
    )(hot, table, gain, middle_grad, weight, *lows)


def small_kernel(parts, spot_rows, table_sum_ref, head_ref, hist_ref, *refs):
    part_refs, refs = refs[:parts], refs[parts:]
    *row_refs, out_ref, sums, held = refs
    for number, part in enumerate(part_refs):
        width = part.shape[2]
        for kind in range(3):
            start = kind * D + number * width
            sums[:, start : start + width] = part[kind]
    held[0:VOCAB, :] = table_sum_ref[0:VOCAB, :] + head_ref[...]
    bias = jnp.sum(sums[...], axis=0, keepdims=True)
    for kind in range(3):
        held[VOCAB + 6 + kind : VOCAB + 7 + kind, :] = bias[:, kind * D : (kind + 1) * D]
    for ref, at in zip(row_refs, spot_rows):
        for row in range(ref.shape[0]):
            for part in range(ref.shape[1] // D):
                held[at : at + 1, :] = ref[row : row + 1, part * D : (part + 1) * D]
                at += 1
    count, rows, columns = out_ref.shape
    narrow = D // count
    wide = columns - narrow
    base = held.shape[0]
    for number in range(count):
        out_ref[number, 0:VOCAB, 0:wide] = sums[0:VOCAB, number * wide : (number + 1) * wide]
        out_ref[number, VOCAB:rows, 0:wide] = jnp.zeros((rows - VOCAB, wide), jnp.float32)
        out_ref[number, 0:base, wide:columns] = held[:, number * narrow : (number + 1) * narrow]
        out_ref[number, base:rows, wide:columns] = hist_ref[...]


def small_blocks(parts, table_sum, head, hist, rows, wide_size):
    whole = pl.BlockSpec(memory_space=pltpu.VMEM)
    total = VOCAB + 15 + hist.shape[0]
    arrays = [array for array, _ in rows]
    return pl.pallas_call(
        partial(small_kernel, len(parts), tuple(VOCAB + place for _, place in rows)),
        in_specs=[whole] * (3 + len(parts) + len(rows)),
        out_specs=whole,
        out_shape=jax.ShapeDtypeStruct((wide_size, total, 4 * D // wide_size), jnp.float32),
        scratch_shapes=[
            pltpu.VMEM((LANES, 3 * D), jnp.float32),
            pltpu.VMEM((VOCAB + 15, D), jnp.float32),
        ],
        cost_estimate=pl.CostEstimate(flops=1 << 20, bytes_accessed=1 << 16, transcendentals=0),
        name="small_grads",
    )(table_sum, head, hist, *parts, *arrays)


def dense_kernel(units, spot_ref, own_ref, beside_ref, core_ref, cross_ref, *refs):
    base_ref, *refs = refs
    count = len(units)
    moment_refs, refs = refs[:count], refs[count:]
    total_refs, next_refs, refs = refs[:count], refs[count : 2 * count], refs[2 * count :]
    rows_ref, low_ref, high_ref, left, right = refs
    spot = spot_ref[0]
    for device in range(4):
        way = spot ^ device
        for kind, source in enumerate((own_ref, core_ref, beside_ref, cross_ref)):

            @pl.when(way == kind)
            def _():
                at = 0
                for total_ref, unit in zip(total_refs, units):
                    total_ref[device * unit : (device + 1) * unit, :] = source[at : at + unit, :]
                    at += unit

    rows_ref[...] = jnp.zeros_like(rows_ref)

    @pl.when(spot == 0)
    def _():
        rows_ref[0 : base_ref.shape[0], :] = (MUON_MU * MUON_MU) * base_ref[...]

    for number in range(count):
        gradient = total_refs[number][...]
        moment_next = MUON_MU * moment_refs[number][...] + (1.0 - MUON_MU) * gradient
        next_refs[number][...] = moment_next
        place = count - number

        @pl.when(spot == place)
        def _():
            rows_ref[0 : gradient.shape[0], :] = (
                1.0 - MUON_MU
            ) * gradient + MUON_MU * moment_next

    high, low = split_two(rows_ref[...])
    depth = rows_ref.shape[0]
    right[0:depth, :] = high
    right[depth : 2 * depth, :] = low
    right[2 * depth : 3 * depth, :] = high
    turned_high, turned_low = split_two(rows_ref[...].T)
    left[:, 0:depth] = turned_high
    left[:, depth : 2 * depth] = turned_high
    left[:, 2 * depth : 3 * depth] = turned_low
    half = len(GRAM_SPOTS) // 2
    for number, (row, column) in enumerate(GRAM_SPOTS):
        target = low_ref if number < half else high_ref
        at = (number % half) * GRAM_TILE
        target[at : at + GRAM_TILE, :] = jnp.dot(
            left[row * GRAM_TILE : (row + 1) * GRAM_TILE, :],
            right[:, column * GRAM_TILE : (column + 1) * GRAM_TILE],
            preferred_element_type=jnp.float32,
        )


def dense_step(spot, units, pieces, base, moments):
    whole = pl.BlockSpec(memory_space=pltpu.VMEM)
    most = max(moment.shape[0] for moment in moments)
    shapes = [jax.ShapeDtypeStruct(moment.shape, jnp.float32) for moment in moments]
    half = jax.ShapeDtypeStruct((len(GRAM_SPOTS) // 2 * GRAM_TILE, GRAM_TILE), jnp.float32)
    results = pl.pallas_call(
        partial(dense_kernel, units),
        in_specs=[pl.BlockSpec(memory_space=pltpu.SMEM)] + [whole] * (5 + len(moments)),
        out_specs=[whole] * (2 * len(moments) + 3),
        out_shape=shapes + shapes + [jax.ShapeDtypeStruct((most, D), jnp.float32), half, half],
        scratch_shapes=[
            pltpu.VMEM((D, 3 * most), jnp.bfloat16),
            pltpu.VMEM((3 * most, D), jnp.bfloat16),
        ],
        compiler_params=pltpu.CompilerParams(vmem_limit_bytes=48 << 20),
        cost_estimate=pl.CostEstimate(flops=1 << 20, bytes_accessed=1 << 16, transcendentals=0),
        name="dense_step",
    )(spot[None].astype(jnp.int32), *pieces, base, *moments)
    count = len(moments)
    return results[:count], results[count : 2 * count], results[2 * count], results[2 * count + 1 :]


def update_kernel(rates, spot_ref, *refs):
    count = len(rates)
    sources, refs = refs[:4], refs[4:]
    for number in range(count):
        weight_ref, out_ref = refs[number], refs[count + number]
        rows = weight_ref.shape[0]
        way = spot_ref[0] ^ number
        for kind, source in enumerate(sources):

            @pl.when(way == kind)
            def _():
                out_ref[...] = weight_ref[...] * (1.0 - MUON_RATE * MUON_DECAY) - rates[
                    number
                ] * source[0:rows, :].astype(jnp.float32)


def update_rows(spot, orthos, weights, rates):
    whole = pl.BlockSpec(memory_space=pltpu.VMEM)
    return pl.pallas_call(
        partial(update_kernel, rates),
        in_specs=[pl.BlockSpec(memory_space=pltpu.SMEM)] + [whole] * (4 + len(weights)),
        out_specs=[whole] * len(weights),
        out_shape=[jax.ShapeDtypeStruct(weight.shape, jnp.float32) for weight in weights],
        compiler_params=pltpu.CompilerParams(vmem_limit_bytes=40 << 20),
        cost_estimate=pl.CostEstimate(flops=1 << 20, bytes_accessed=1 << 16, transcendentals=0),
        name="update",
    )(spot[None].astype(jnp.int32), *orthos, *weights)


def heads_kernel(place_ref, blocks_ref, bias_ref, out_ref, held):
    count, rows, columns = blocks_ref.shape
    held[rows : held.shape[0], :] = jnp.zeros((held.shape[0] - rows, 3 * D), jnp.float32)
    for number in range(count):
        spot = slice(number * columns, (number + 1) * columns)
        held[0:rows, spot] = blocks_ref[place_ref[number]] + bias_ref[:, spot]
    high, low = split_two(held[...])
    some = held.shape[0]
    none = jnp.zeros((LANES - some, 3 * D), jnp.bfloat16)
    out_ref[0:some, :] = high
    out_ref[some:LANES, :] = none
    out_ref[LANES : LANES + some, :] = low
    out_ref[LANES + some : 2 * LANES, :] = none


def heads_table(blocks, place, bias):
    return pl.pallas_call(
        heads_kernel,
        grid_spec=pltpu.PrefetchScalarGridSpec(
            num_scalar_prefetch=1,
            grid=(1,),
            in_specs=[
                pl.BlockSpec(blocks.shape, lambda step, place: (0, 0, 0)),
                pl.BlockSpec(bias.shape, lambda step, place: (0, 0)),
            ],
            out_specs=pl.BlockSpec((2 * LANES, 3 * D), lambda step, place: (0, 0)),
            scratch_shapes=[pltpu.VMEM((VOCAB + -VOCAB % 16, 3 * D), jnp.float32)],
        ),
        out_shape=jax.ShapeDtypeStruct((2 * LANES, 3 * D), jnp.bfloat16),
        name="heads_table",
    )(place, blocks, bias)


def turn(values, cosine, sine_table):
    lane = lax.broadcasted_iota(jnp.int32, values.shape, 1)
    half = HEAD_DIM // 2
    partner = jnp.where(
        lane % HEAD_DIM < half,
        pltpu.roll(values, PAIR - half, 1),
        pltpu.roll(values, half, 1),
    )
    return values * cosine + partner * sine_table


def attend_kernel(
    hot_ref, tq_ref, tk_ref, tv_ref, cos_ref, sin_ref,
    q_ref, k_ref, v_ref, mixed_ref, log_ref,
    q_all, v_turned, mixed_turned, prob_all,
):
    hot = hot_ref[...]
    cosine = cos_ref[...]
    sine_table = sin_ref[...]
    queries = jnp.dot(hot, tq_ref[...], preferred_element_type=jnp.float32)
    queries = turn(queries, cosine, sine_table).astype(jnp.bfloat16) * HEAD_DIM ** (-0.5)
    queries = queries.astype(jnp.bfloat16)
    q_ref[...] = queries
    q_all[0:SEQ_LEN, :] = queries
    q_all[SEQ_LEN:SPAN, :] = jnp.zeros((SPAN - SEQ_LEN, PAIR), jnp.bfloat16)
    keys = jnp.dot(hot, tk_ref[...], preferred_element_type=jnp.float32)
    keys = turn(keys, cosine, sine_table).astype(jnp.bfloat16)
    k_ref[...] = keys
    values = jnp.dot(hot, tv_ref[...], preferred_element_type=jnp.float32)
    v_ref[...] = values.astype(jnp.bfloat16)
    v_turned[...] = values.T.astype(jnp.bfloat16)

    def one_head(head, carry):
        lane = lax.broadcasted_iota(jnp.int32, (SEQ_LEN, PAIR), 1)
        keys_head = jnp.where(lane // HEAD_DIM == head, k_ref[...], jnp.zeros((), jnp.bfloat16))
        head_rows = pl.ds(pl.multiple_of(head * HEAD_DIM, HEAD_DIM), HEAD_DIM)
        values_head = v_turned[head_rows, :]

        def body(step, carry):
            at = pl.multiple_of(step * STRIP, STRIP)
            scores = row_dot(keys_head, q_all[pl.ds(at, STRIP), :])
            peak = jnp.max(scores, axis=0, keepdims=True)
            powers = jnp.exp(scores - peak)
            total = jnp.sum(powers, axis=0, keepdims=True)
            prob_low = (powers * (1.0 / total)).astype(jnp.bfloat16)
            prob_all[:, pl.ds(at, STRIP)] = prob_low
            log_ref[0, pl.ds(head, 1), pl.ds(at, STRIP)] = peak + jnp.log(total)
            return carry

        lax.fori_loop(0, SPAN // STRIP, body, 0)
        mixed_turned[head_rows, :] = jnp.dot(
            values_head, prob_all[...], preferred_element_type=jnp.float32
        )
        return carry

    lax.fori_loop(0, 2, one_head, 0)
    mixed_ref[...] = mixed_turned[...].T[0:SEQ_LEN, :].astype(jnp.bfloat16)


def attend_call(hot, tables, cosine, sine_table, first, count):
    whole = lambda step: (0, 0)
    source = lambda step: (0, step + first)
    own = lambda step: (0, step)
    rows_low = jax.ShapeDtypeStruct((SEQ_LEN, count * PAIR), jnp.bfloat16)
    return pl.pallas_call(
        attend_kernel,
        grid=(count,),
        in_specs=[
            pl.BlockSpec(hot.shape, whole),
            pl.BlockSpec((hot.shape[1], PAIR), source),
            pl.BlockSpec((hot.shape[1], PAIR), lambda step: (0, step + first + D // PAIR)),
            pl.BlockSpec((hot.shape[1], PAIR), lambda step: (0, step + first + 2 * D // PAIR)),
            pl.BlockSpec((SEQ_LEN, PAIR), whole),
            pl.BlockSpec((SEQ_LEN, PAIR), whole),
        ],
        out_specs=[
            pl.BlockSpec((SEQ_LEN, PAIR), own),
            pl.BlockSpec((SEQ_LEN, PAIR), own),
            pl.BlockSpec((SEQ_LEN, PAIR), own),
            pl.BlockSpec((SEQ_LEN, PAIR), own),
            pl.BlockSpec((1, 2, SPAN), lambda step: (step, 0, 0)),
        ],
        out_shape=[rows_low] * 4 + [jax.ShapeDtypeStruct((count, 2, SPAN), jnp.float32)],
        scratch_shapes=[
            pltpu.VMEM((SPAN, PAIR), jnp.bfloat16),
            pltpu.VMEM((PAIR, SEQ_LEN), jnp.bfloat16),
            pltpu.VMEM((PAIR, SPAN), jnp.float32),
            pltpu.VMEM((SEQ_LEN, SPAN), jnp.bfloat16),
        ],
        compiler_params=pltpu.CompilerParams(vmem_limit_bytes=40 << 20),
        cost_estimate=pl.CostEstimate(
            flops=count * SPAN * SPAN, bytes_accessed=1 << 16,
            transcendentals=0,
        ),
        name="attend",
    )(hot, tables, tables, tables, cosine, sine_table)


def attend_back_kernel(
    hot_ref, q_ref, k_ref, v_ref, grad_ref, log_ref, cos_ref, sin_ref,
    low_ref, sums_ref,
    q_all, grad_all, k_turned, prob_all, score_all, query_turned, key_sum, value_sum,
):
    rest = jnp.zeros((SPAN - SEQ_LEN, PAIR), jnp.bfloat16)
    q_all[0:SEQ_LEN, :] = q_ref[...]
    q_all[SEQ_LEN:SPAN, :] = rest
    grad_all[0:SEQ_LEN, :] = grad_ref[...]
    grad_all[SEQ_LEN:SPAN, :] = rest
    k_turned[...] = k_ref[...].astype(jnp.float32).T.astype(jnp.bfloat16)
    lane = lax.broadcasted_iota(jnp.int32, (SEQ_LEN, PAIR), 1)
    none = jnp.zeros((), jnp.bfloat16)

    def one_head(head, carry):
        head_rows = pl.ds(pl.multiple_of(head * HEAD_DIM, HEAD_DIM), HEAD_DIM)
        keys_head = jnp.where(lane // HEAD_DIM == head, k_ref[...], none)
        values_head = jnp.where(lane // HEAD_DIM == head, v_ref[...], none)

        def body(step, carry):
            at = pl.multiple_of(step * STRIP, STRIP)
            scores = row_dot(keys_head, q_all[pl.ds(at, STRIP), :])
            prob_rows = jnp.exp(scores - log_ref[0, pl.ds(head, 1), pl.ds(at, STRIP)])
            prob_all[:, pl.ds(at, STRIP)] = prob_rows.astype(jnp.bfloat16)
            prob_grad = row_dot(values_head, grad_all[pl.ds(at, STRIP), :])
            delta = jnp.sum(prob_grad * prob_rows, axis=0, keepdims=True)
            score_all[:, pl.ds(at, STRIP)] = (prob_rows * (prob_grad - delta)).astype(jnp.bfloat16)
            return carry

        lax.fori_loop(0, SPAN // STRIP, body, 0)
        value_part = jnp.dot(prob_all[...], grad_all[...], preferred_element_type=jnp.float32)
        key_part = jnp.dot(score_all[...], q_all[...], preferred_element_type=jnp.float32)
        value_sum[...] = jnp.where(lane // HEAD_DIM == head, value_part, value_sum[...])
        key_sum[...] = jnp.where(lane // HEAD_DIM == head, key_part, key_sum[...])
        query_turned[head_rows, :] = (
            jnp.dot(k_turned[head_rows, :], score_all[...], preferred_element_type=jnp.float32)
            * HEAD_DIM ** (-0.5)
        )
        return carry

    lax.fori_loop(0, 2, one_head, 0)
    cosine = cos_ref[...]
    sine_table = -sin_ref[...]
    hot = hot_ref[...]
    query_low = turn(query_turned[...].T[0:SEQ_LEN, :], cosine, sine_table).astype(jnp.bfloat16)
    key_low = turn(key_sum[...], cosine, sine_table).astype(jnp.bfloat16)
    value_low = value_sum[...].astype(jnp.bfloat16)
    for number, low in enumerate((query_low, key_low, value_low)):
        low_ref[number] = low
        sums_ref[number] = jnp.dot(hot, low, preferred_element_type=jnp.float32)


def attend_back_call(
    hot_turned, queries, keys, values, gradients, logs, cosine, sine_table, first, inside, count
):
    whole = lambda step: (0, 0)
    rows = pl.BlockSpec((SEQ_LEN, PAIR), lambda step: (0, step + inside))
    whole_rows = pl.BlockSpec((SEQ_LEN, PAIR), whole)
    return pl.pallas_call(
        attend_back_kernel,
        grid=(count,),
        in_specs=[
            pl.BlockSpec(hot_turned.shape, whole),
            rows,
            rows,
            rows,
            pl.BlockSpec((SEQ_LEN, PAIR), lambda step: (0, step + first)),
            pl.BlockSpec((1, 2, SPAN), lambda step: (step + inside, 0, 0)),
            whole_rows,
            whole_rows,
        ],
        out_specs=[
            pl.BlockSpec((3, SEQ_LEN, PAIR), lambda step: (0, 0, step)),
            pl.BlockSpec((3, hot_turned.shape[0], PAIR), lambda step: (0, 0, step)),
        ],
        out_shape=[
            jax.ShapeDtypeStruct((3, SEQ_LEN, count * PAIR), jnp.bfloat16),
            jax.ShapeDtypeStruct((3, hot_turned.shape[0], count * PAIR), jnp.float32),
        ],
        scratch_shapes=[
            pltpu.VMEM((SPAN, PAIR), jnp.bfloat16),
            pltpu.VMEM((SPAN, PAIR), jnp.bfloat16),
            pltpu.VMEM((PAIR, SEQ_LEN), jnp.bfloat16),
            pltpu.VMEM((SEQ_LEN, SPAN), jnp.bfloat16),
            pltpu.VMEM((SEQ_LEN, SPAN), jnp.bfloat16),
            pltpu.VMEM((PAIR, SPAN), jnp.float32),
            pltpu.VMEM((SEQ_LEN, PAIR), jnp.float32),
            pltpu.VMEM((SEQ_LEN, PAIR), jnp.float32),
        ],
        compiler_params=pltpu.CompilerParams(vmem_limit_bytes=48 << 20),
        cost_estimate=pl.CostEstimate(
            flops=count * SPAN * SPAN, bytes_accessed=1 << 16,
            transcendentals=0,
        ),
        name="attend_back",
    )(hot_turned, queries, keys, values, gradients, logs, cosine, sine_table)


ERF_P = 0.3275911
ERF_A = (0.254829592, -0.284496736, 1.421413741, -1.453152027, 1.061405429)

def normal_parts(values):
    size = jnp.abs(values)
    bell = jnp.exp(values * values * -0.5)
    step = 1.0 / (1.0 + (ERF_P * 0.5**0.5) * size)
    series = ERF_A[4]
    for factor in (ERF_A[3], ERF_A[2], ERF_A[1], ERF_A[0]):
        series = series * step + factor
    tail = (0.5 * series) * step * bell
    return jnp.where(values < 0.0, tail, 1.0 - tail), bell * (1.0 / math.sqrt(2.0 * math.pi))

def start_parts(place_ref, source_ref, starts, held, sems):
    for part in range(PARTS):
        for number, start in enumerate(starts):

            def body(spot, carry):
                pltpu.make_async_copy(
                    source_ref.at[place_ref[part * PART_BLOCKS + spot], pl.ds(start, BLOCK), :],
                    held[number].at[part, spot],
                    sems.at[number, part],
                ).start()
                return carry

            lax.fori_loop(0, PART_BLOCKS, body, 0)


def wait_part(source_ref, number, held, sems, step):
    pltpu.make_async_copy(
        source_ref.at[pl.ds(0, PART_BLOCKS), pl.ds(0, BLOCK), :],
        held[number].at[step],
        sems.at[number, step],
    ).wait()
    return held[number][step].reshape(D, D)


def feed_kernel(starts, place_ref, rows_ref, bias_ref, source_ref, hidden_ref, slope_ref, out_ref, expand_held, reduce_held, sems):
    held = (expand_held, reduce_held)
    step = pl.program_id(0)
    @pl.when(step == 0)
    def _():
        start_parts(place_ref, source_ref, starts, held, sems)

    expand = wait_part(source_ref, 0, held, sems, step)
    for at in range(0, SEQ_LEN, 304):
        spot = slice(at, at + 304)
        values = row_dot(rows_ref[spot, :], expand) + bias_ref[...]
        below, bell = normal_parts(values)
        hidden_ref[spot, :] = (values * below).astype(jnp.bfloat16)
        slope_ref[spot, :] = (below + values * bell).astype(jnp.bfloat16)
    reduce = wait_part(source_ref, 1, held, sems, step)
    part = jnp.dot(hidden_ref[...], reduce, preferred_element_type=jnp.float32)
    @pl.when(step == 0)
    def _():
        out_ref[...] = part
    @pl.when(step > 0)
    def _():
        out_ref[...] += part

def feed_call(place, rows, bias, source, starts):
    whole = lambda step, place: (0, 0)
    chunk = pl.BlockSpec((SEQ_LEN, D), lambda step, place: (0, step))
    return pl.pallas_call(
        partial(feed_kernel, starts),
        grid_spec=pltpu.PrefetchScalarGridSpec(
            num_scalar_prefetch=1,
            grid=(PARTS,),
            in_specs=[
                pl.BlockSpec((SEQ_LEN, D), whole),
                pl.BlockSpec((1, D), lambda step, place: (0, step)),
                pl.BlockSpec(memory_space=pl.ANY),
            ],
            out_specs=[chunk, chunk, pl.BlockSpec((SEQ_LEN, D), whole)],
            scratch_shapes=[
                pltpu.VMEM((PARTS, PART_BLOCKS, BLOCK, D), jnp.bfloat16),
                pltpu.VMEM((PARTS, PART_BLOCKS, BLOCK, D), jnp.bfloat16),
                pltpu.SemaphoreType.DMA((2, PARTS)),
            ],
        ),
        out_shape=[jax.ShapeDtypeStruct((SEQ_LEN, FF), jnp.bfloat16)] * 2
        + [jax.ShapeDtypeStruct((SEQ_LEN, D), jnp.float32)],
        compiler_params=pltpu.CompilerParams(vmem_limit_bytes=48 << 20),
        cost_estimate=pl.CostEstimate(
            flops=SEQ_LEN * D * FF, bytes_accessed=1 << 16, transcendentals=0
        ),
        name="feed",
    )(place, rows, bias, source)


def feed_back_kernel(starts, place_ref, grad_ref, slope_ref, source_ref, pre_ref, out_ref, bias_ref, expand_held, reduce_held, sems):
    held = (expand_held, reduce_held)
    step = pl.program_id(0)
    @pl.when(step == 0)
    def _():
        start_parts(place_ref, source_ref, starts, held, sems)

    reduce = wait_part(source_ref, 1, held, sems, step)
    total = jnp.zeros((1, D), jnp.float32)
    for at in range(0, SEQ_LEN, 304):
        spot = slice(at, at + 304)
        grad = row_dot(grad_ref[spot, :], reduce) * slope_ref[spot, :].astype(jnp.float32)
        low = grad.astype(jnp.bfloat16)
        pre_ref[spot, :] = low
        total = total + jnp.sum(low.astype(jnp.float32), axis=0, keepdims=True)
    bias_ref[...] = total
    low = pre_ref[...]
    expand = wait_part(source_ref, 0, held, sems, step)
    part = jnp.dot(low, expand, preferred_element_type=jnp.float32)
    @pl.when(step == 0)
    def _():
        out_ref[...] = part
    @pl.when(step > 0)
    def _():
        out_ref[...] += part

def feed_back_call(place, grad, slope, source, starts):
    whole = lambda step, place: (0, 0)
    chunk = pl.BlockSpec((SEQ_LEN, D), lambda step, place: (0, step))
    return pl.pallas_call(
        partial(feed_back_kernel, starts),
        grid_spec=pltpu.PrefetchScalarGridSpec(
            num_scalar_prefetch=1,
            grid=(PARTS,),
            in_specs=[
                pl.BlockSpec((SEQ_LEN, D), whole),
                chunk,
                pl.BlockSpec(memory_space=pl.ANY),
            ],
            out_specs=[
                chunk,
                pl.BlockSpec((SEQ_LEN, D), whole),
                pl.BlockSpec((1, D), lambda step, place: (0, step)),
            ],
            scratch_shapes=[
                pltpu.VMEM((PARTS, PART_BLOCKS, BLOCK, D), jnp.bfloat16),
                pltpu.VMEM((PARTS, PART_BLOCKS, BLOCK, D), jnp.bfloat16),
                pltpu.SemaphoreType.DMA((2, PARTS)),
            ],
        ),
        out_shape=[
            jax.ShapeDtypeStruct((SEQ_LEN, FF), jnp.bfloat16),
            jax.ShapeDtypeStruct((SEQ_LEN, D), jnp.float32),
            jax.ShapeDtypeStruct((1, FF), jnp.float32),
        ],
        compiler_params=pltpu.CompilerParams(vmem_limit_bytes=48 << 20),
        cost_estimate=pl.CostEstimate(
            flops=SEQ_LEN * D * FF, bytes_accessed=1 << 16, transcendentals=0
        ),
        name="feed_back",
    )(place, grad, slope, source)


def adam_step(weight, mean_state, square, gradient, step_rate, decay_rate, step_count):
    mean_next = ADAM_BETA1 * mean_state + (1.0 - ADAM_BETA1) * gradient
    square_next = ADAM_BETA2 * square + (1.0 - ADAM_BETA2) * gradient * gradient
    step_float = step_count.astype(jnp.float32)
    mean_hat = mean_next / (1.0 - ADAM_BETA1**step_float)
    square_hat = square_next / (1.0 - ADAM_BETA2**step_float)
    updated = weight - step_rate * (
        mean_hat / (jnp.sqrt(square_hat) + ADAM_EPS) + decay_rate * weight
    )
    return (updated, mean_next, square_next)


def on_device(
    codons,
    offsets,
    positions,
    targets,
    table_weight,
    attend_weight,
    mixing_weight,
    expand_weight,
    reduce_weight,
    vector_params,
    attend_moment,
    mixing_moment,
    expand_moment,
    reduce_moment,
    table_mean,
    table_square,
    vector_mean,
    vector_square,
    step_count,
):
    low_type = jnp.bfloat16
    wide_at = lax.axis_index("wide")
    me = my_index()
    devices = lax.axis_size(BOTH)
    masks = wide_masks()
    narrow_size = lax.axis_size("narrow")
    wide_size = lax.axis_size("wide")
    hidden_masks = masks[:-1] + [2, masks[-1], 1]
    all_masks = masks + [2, 1]
    small = jnp.concatenate([table_weight, vector_params], axis=0).astype(low_type)
    small = gather_blocks(small[None], masks)
    packed = (expand_weight, reduce_weight, mixing_weight, attend_weight)
    units = [weight.shape[0] // narrow_size for weight in packed]
    starts = np.cumsum([0] + [unit + -unit % 16 for unit in units])
    packed_low = pack_rows(packed, lax.axis_index("narrow"))
    weights_low = lax.all_gather(packed_low[: int(starts[3])], BOTH, axis=0)
    attend_own = packed_low[int(starts[3]) : int(starts[3]) + units[3]]

    def weight_rows(number, unit):
        start = int(starts[number])
        return weights_low[:, start : start + unit].reshape(-1, D)

    codons, positions, targets = gate((codons, positions, targets), small)
    small = in_order(small, masks, narrow_size, wide_at)
    small = jnp.transpose(small, (1, 0, 2)).reshape(VOCAB + 15, D)
    table_low = small[:VOCAB]
    vector_full = small[VOCAB:].astype(jnp.float32)
    gain_one = vector_full[0]
    bias_one = vector_full[1]
    gain_two = vector_full[2]
    bias_two = vector_full[3]
    gain_last = vector_full[4]
    bias_last = vector_full[5]
    attend_bias = vector_full[6:9].reshape(1, 3 * D)
    mixing_bias = vector_full[9]
    reduce_bias = vector_full[10]
    expand_bias = out_of_order(
        vector_full[11:15].reshape(devices, FF // devices), hidden_masks, 1, me
    ).reshape(FF)
    embed_scale = math.sqrt(D)
    table_stream = embed_scale * table_low.astype(jnp.float32)
    table_normed = norm_forward(table_stream, gain_one, bias_one)[0].astype(low_type)
    table_own = times_trans(table_normed, attend_own)
    place = jnp.asarray(places_of(all_masks, 1), jnp.int32)[jnp.arange(devices) ^ me]
    tables = heads_table(gather_blocks(table_own[None], all_masks), place, attend_bias)

    unit = FF // devices
    hidden_place = jnp.asarray(offsets_of(hidden_masks)) ^ me
    if unit == BLOCK:
        feed_place, feed_source, feed_starts = hidden_place, weights_low, tuple(starts[:2])
    else:
        feed_source = jnp.concatenate(
            [
                take_blocks(weights_low[:, start : start + unit], hidden_place).reshape(-1, BLOCK, D)
                for start in (int(starts[0]), int(starts[1]))
            ],
            axis=1,
        )
        feed_place, feed_starts = jnp.arange(FF // BLOCK), (0, BLOCK)
    feed_place = feed_place.astype(jnp.int32)
    feed_starts = tuple(int(start) for start in feed_starts)

    seq_count = codons.shape[0]
    row_count = seq_count * SEQ_LEN
    window = jax.vmap(partial(lax.dynamic_slice_in_dim, slice_size=SEQ_LEN))(codons, offsets)
    vocab_ids = jnp.arange(VOCAB, dtype=jnp.int32)
    token_hot = window.reshape(row_count)[:, None] == vocab_ids[None, :]
    token_low = token_hot.astype(low_type)
    target_hot = (targets.reshape(row_count)[:, None] == vocab_ids[None, :]).astype(jnp.float32)
    stream = embed_scale * times_plain(token_low, table_low)
    token_ids = window.reshape(row_count)
    lane_ids = jnp.arange(2 * LANES, dtype=jnp.int32) % LANES
    hot = (token_ids[:, None] == lane_ids[None, :]).astype(low_type)
    hot_turned = (token_ids[None, :] == lane_ids[:LANES, None]).astype(low_type)
    cosine, sine_table = rotary_tables(positions.reshape(row_count))
    cosine = jnp.concatenate([cosine] * 4, axis=1)
    sine_table = jnp.concatenate([-sine_table, sine_table] * 2, axis=1)
    pairs = D // PAIR // ATTEND_CALLS
    attended = []

    for number in range(ATTEND_CALLS):
        attended.append(
            attend_call(hot, tables, cosine, sine_table, number * pairs, pairs)
        )
    last_mask = masks[-1]
    mixed_low = jnp.concatenate([parts[3] for parts in attended], axis=1)
    mixing_low = weight_rows(2, D // devices)
    attend_low = lax.all_gather(gate(attend_own, mixed_low), BOTH, axis=0)
    branch = times_trans(mixed_low, mixing_low) + mixing_bias
    middle = stream + branch
    normed_two, normal_two, inverse_two = norm_forward(middle, gain_two, bias_two)
    normed_two_low = normed_two.astype(low_type)
    hidden_low, slope_low, feed_out = feed_call(
        feed_place, normed_two_low, expand_bias[None, :], feed_source, feed_starts
    )
    feed_out = feed_out + reduce_bias
    output = middle + feed_out
    final_norm, normal_last, inverse_last = norm_forward(output, gain_last, bias_last)
    final_low = final_norm.astype(low_type)
    logits = times_trans(final_low, table_low)
    row_peak = jnp.max(logits, axis=-1, keepdims=True)
    shifted = jnp.exp(logits - row_peak)
    prob_rows = shifted / jnp.sum(shifted, axis=-1, keepdims=True)
    prob_sum = jnp.sum(prob_rows, axis=0)
    logit_grad = (prob_rows - target_hot).astype(low_type)
    final_grad = times_plain(logit_grad, table_low)
    table_head = trans_times(logit_grad, final_low)
    output_grad, gain_last_grad, bias_last_grad = norm_backward(
        final_grad, normal_last, inverse_last, gain_last
    )
    feed_low = output_grad.astype(low_type)
    reduce_bias_grad = jnp.sum(feed_low, axis=0, dtype=jnp.float32)
    half_ff = FF // 2
    static_marks = [masks[-1], 2] + list(reversed(masks[:-1]))
    static_shape = (2,) * len(static_marks) + (unit, D)

    reduce_send = trans_times(hidden_low[:, half_ff:], feed_low).astype(low_type)
    pre_grad, normed_two_grad, expand_bias_grad = feed_back_call(
        feed_place, gate(feed_low, reduce_send), slope_low, feed_source, feed_starts
    )
    reduce_got = gate(swap(reduce_send, 1), pre_grad)
    reduce_sum = trans_times(hidden_low[:, :half_ff], feed_low) + reduce_got
    reduce_chain = sum_chain([(reduce_sum.reshape(static_shape), static_marks, False)], low_type)
    reduce_sent = next(reduce_chain)
    expand_send = trans_times(
        gate(pre_grad, reduce_sent)[:, half_ff:], normed_two_low
    ).astype(low_type)
    expand_sum = trans_times(pre_grad[:, :half_ff], normed_two_low) + swap(expand_send, 1)
    middle_part, gain_two_grad, bias_two_grad = norm_backward(
        normed_two_grad, normal_two, inverse_two, gain_two
    )
    middle_grad = output_grad + middle_part
    branch_low = middle_grad.astype(low_type)
    mixing_bias_grad = jnp.sum(branch_low, axis=0, dtype=jnp.float32)
    mixing_sum = trans_times(branch_low, mixed_low).reshape(
        bits_shape(devices, (D // devices, D))
    )
    (mixing_item,) = finish_hop(hop([(mixing_sum, all_masks, True)], 1, low_type))
    mixed_grad = times_plain(branch_low, mixing_low).astype(low_type)
    expand_chain = sum_chain(
        [(expand_sum.reshape(static_shape), static_marks, False), mixing_item], low_type
    )
    expand_sent = next(expand_chain)

    backs = []
    back_pairs = D // PAIR // BACK_CALLS

    def back_step(waits):
        number = len(backs)
        first = number * back_pairs
        source = attended[first // pairs]
        order = (backs[-1][1],) if backs else ()
        backs.append(
            attend_back_call(
                hot_turned,
                *source[:3],
                gate(mixed_grad, (waits, order)),
                source[4],
                cosine,
                sine_table,
                first,
                first % pairs,
                back_pairs,
            )
        )
        return backs[-1][1]

    mixed_grad, attend_low = lax.optimization_barrier((mixed_grad, attend_low))
    back_step(expand_sent)
    token = back_step(())
    expand_sent = expand_chain.send(token)
    reduce_sent = reduce_chain.send(token)
    token = back_step((expand_sent, reduce_sent))
    expand_sent = expand_chain.send(token)
    reduce_sent = reduce_chain.send(token)
    token = back_step((expand_sent, reduce_sent))
    reduce_sent = reduce_chain.send(token)
    token = back_step(reduce_sent)
    expand_sent = expand_chain.send(token)
    token = back_step(expand_sent)
    (reduce_sum,) = drain(reduce_chain, token)
    expand_sum, mixing_sum = drain(expand_chain, token)
    dense = jnp.concatenate([reduce_sum, expand_sum, mixing_sum], axis=0)
    spot = lax.axis_index("narrow")
    dense, backs = together((dense, backs))

    def one_chain(value, mask):
        (got,) = yield [(value, mask)]
        return got

    columns = D // wide_size
    rows_hist = -(-VOCAB // columns)

    def make_small(backs):
        entry_gradient, one_sums, table_sum = entry_call(
            embed_scale,
            hot,
            jnp.pad(table_low, ((0, LANES - VOCAB), (0, 0))),
            gain_one[None, :],
            middle_grad,
            attend_low.reshape(3 * D, D),
            [back[0] for back in backs],
        )
        hist_part = jnp.pad(prob_sum, (0, rows_hist * columns - VOCAB)).reshape(rows_hist, columns)
        expand_ordered = in_order(
            expand_bias_grad.reshape(devices, FF // devices), hidden_masks, 1, me
        )
        small_grads = small_blocks(
            [back[1] for back in backs],
            table_sum,
            table_head,
            hist_part,
            (
                (one_sums, 0),
                (gain_two_grad[None, :], 2),
                (bias_two_grad[None, :], 3),
                (gain_last_grad[None, :], 4),
                (bias_last_grad[None, :], 5),
                (mixing_bias_grad[None, :], 9),
                (reduce_bias_grad[None, :], 10),
                (expand_ordered.reshape(1, FF), 11),
            ),
            wide_size,
        )
        return entry_gradient, small_grads

    beside_chain = Chain(one_chain(dense, 2))
    entry_gradient, small_grads = advance([beside_chain], make_small, backs)
    beside = beside_chain.result
    cores = [Chain(one_chain(dense, 1)), Chain(one_chain(beside, 1))]
    small_chain = Chain(sum_small(small_grads))
    advance(cores + [small_chain])
    pieces = (dense, beside, cores[0].result, cores[1].result)

    def make_dense(pieces):
        return dense_step(
            spot,
            (unit, unit, D // devices),
            pieces,
            attend_moment,
            (reduce_moment, expand_moment, mixing_moment),
        )

    dense_totals, dense_next, dense_rows, gram_own = advance([small_chain], make_dense, pieces)
    reduce_total, expand_total, mixing_total = dense_totals
    reduce_next, expand_next, mixing_next = dense_next

    def step_of(moment, gradient):
        moment_next = MUON_MU * moment + (1.0 - MUON_MU) * gradient
        return moment_next, (1.0 - MUON_MU) * gradient + MUON_MU * moment_next

    gram_chain = Chain(sum_gram(gram_own))
    while small_chain.request:
        advance([chain for chain in (gram_chain, small_chain) if chain.request])
    small_total = small_chain.result
    token_sums = small_total[:VOCAB, : 3 * D // wide_size]
    small_total = small_total[:, 3 * D // wide_size :]
    attend_total = lax.dot_general(
        token_sums,
        table_normed.astype(jnp.float32),
        (((0,), (0,)), ((), ())),
        precision=lax.Precision.HIGHEST,
        preferred_element_type=jnp.float32,
    )
    attend_next, attend_step = step_of(attend_moment, attend_total)
    gradient_rate = (1.0 - MUON_MU) * (1.0 + MUON_MU)
    crossed = exact_times(
        token_sums, jnp.concatenate([attend_moment, token_sums.T], axis=1)
    )
    crossed_chain = Chain(sum_wide(crossed))
    while crossed_chain.request:
        advance([chain for chain in (gram_chain, crossed_chain) if chain.request])
    while gram_chain.request:
        advance([gram_chain])
    crossed = crossed_chain.result
    gram_parts = gram_chain.result
    table_wide = table_normed.astype(jnp.float32)
    added = gradient_rate * (
        (MUON_MU * MUON_MU) * crossed[:, :D]
        + (0.5 * gradient_rate) * exact_times(crossed[:, D:], table_wide)
    )
    added = jnp.where(spot == 0, added, 0.0)
    table_total = small_total[:VOCAB]
    vector_total = small_total[VOCAB : VOCAB + 15]
    prob_total = small_total[VOCAB + 15 :].reshape(rows_hist * columns)[:VOCAB]
    histogram = prob_total * (VOCAB / (row_count * devices))
    totals = (attend_total, mixing_total, expand_total, reduce_total)
    moment_next = (attend_next, mixing_next, expand_next, reduce_next)
    most = dense_rows.shape[0]
    attend_rows = jnp.pad(attend_step, ((0, most - attend_step.shape[0]), (0, 0)))
    rows = jnp.where(spot == 0, attend_rows, dense_rows)
    ortho = newton_rows(gram_parts, rows, added, table_normed)
    ortho, table_total, vector_total = together((ortho, table_total, vector_total))
    across = swap(ortho, 2)
    table_new, table_mean_next, table_square_next = adam_step(
        table_weight, table_mean, table_square, table_total, TABLE_RATE, TABLE_DECAY, step_count
    )
    vector_new, vector_mean_next, vector_square_next = adam_step(
        vector_params, vector_mean, vector_square, vector_total, VECTOR_RATE, 0.0, step_count
    )
    across, adam_results = together(
        (
            across,
            (
                table_new,
                table_mean_next,
                table_square_next,
                vector_new,
                vector_mean_next,
                vector_square_next,
            ),
        )
    )
    orthos = (ortho, swap(ortho, 1), across, swap(across, 1))
    matrices = (attend_weight, mixing_weight, expand_weight, reduce_weight)
    rates = tuple(
        MUON_RATE * SHAPE_FACTOR * math.sqrt(max(rows, D)) for rows in (3 * D, D, FF, FF)
    )
    matrix_new = tuple(update_rows(spot, orthos, matrices, rates))
    results = (
        totals
        + (table_total, vector_total)
        + matrix_new
        + moment_next
        + (
            *adam_results,
        )
    )
    block_output = output.astype(low_type).reshape(seq_count, SEQ_LEN, D)
    return (block_output, entry_gradient.reshape(seq_count, SEQ_LEN, D)) + results + (histogram,)


def solution(mesh):
    in_specs = (
        P(("wide", "narrow"), None),
        P(("wide", "narrow")),
        P(("wide", "narrow"), None),
        P(("wide", "narrow"), None),
        P(None, "wide"),
        P("wide", None),
        P("wide", None),
        P("wide", None),
        P("wide", None),
        P(None, "wide"),
        P("wide", None),
        P("wide", None),
        P("wide", None),
        P("wide", None),
        P(None, "wide"),
        P(None, "wide"),
        P(None, "wide"),
        P(None, "wide"),
        P(),
    )
    out_specs = (
        P(("wide", "narrow"), None, None),
        P(("wide", "narrow"), None, None),
        P("wide", None),
        P("wide", None),
        P("wide", None),
        P("wide", None),
        P(None, "wide"),
        P(None, "wide"),
        P("wide", None),
        P("wide", None),
        P("wide", None),
        P("wide", None),
        P("wide", None),
        P("wide", None),
        P("wide", None),
        P("wide", None),
        P(None, "wide"),
        P(None, "wide"),
        P(None, "wide"),
        P(None, "wide"),
        P(None, "wide"),
        P(None, "wide"),
        P(),
    )
    return jax.shard_map(
        on_device, mesh=mesh, in_specs=in_specs, out_specs=out_specs, check_vma=False
    )
```

```python
from functools import partial
import math

import jax
import jax.numpy as jnp
import numpy as np
from jax import lax
from jax.experimental import pallas as pl
from jax.experimental.pallas import tpu as pltpu
from jax.sharding import PartitionSpec as P

D = 768
HEADS = 12
HEAD_DIM = 64
FF = 3072
VOCAB = 70
SEQ_LEN = 912
NS_ITERS = 5


NORM_EPS = 1e-05
ROPE_BASE = 10000.0
NEWTON_A = 3.4445
NEWTON_B = -4.775
NEWTON_C = 2.0315
MUON_MU = 0.95
MUON_RATE = 0.3
MUON_DECAY = 0.1
SHAPE_FACTOR = 0.2
ADAM_BETA1 = 0.9
ADAM_BETA2 = 0.95
ADAM_EPS = 1e-08
TABLE_RATE = 0.03
TABLE_DECAY = 0.01
VECTOR_RATE = 0.2


def times_plain(left_side, right_side):
    return jnp.dot(left_side, right_side, preferred_element_type=jnp.float32)


def times_trans(left_side, right_side):
    return lax.dot_general(
        left_side, right_side, (((1,), (1,)), ((), ())), preferred_element_type=jnp.float32
    )


def trans_times(left_side, right_side):
    return lax.dot_general(
        left_side, right_side, (((0,), (0,)), ((), ())), preferred_element_type=jnp.float32
    )


def exact_times(left_side, right_side):
    return jnp.dot(
        left_side, right_side, precision=lax.Precision.HIGHEST, preferred_element_type=jnp.float32
    )


def norm_forward(values, gain_row, bias_row):
    center = values - jnp.mean(values, axis=-1, keepdims=True)
    spread = jnp.mean(center * center, axis=-1, keepdims=True)
    inverse = lax.rsqrt(spread + NORM_EPS)
    normal = center * inverse
    return (normal * gain_row + bias_row, normal, inverse)


def norm_backward(upstream, normal, inverse, gain_row):
    scaled = upstream * gain_row
    inner_part = (
        scaled
        - jnp.mean(scaled, axis=-1, keepdims=True)
        - normal * jnp.mean(scaled * normal, axis=-1, keepdims=True)
    )
    return (inverse * inner_part, jnp.sum(upstream * normal, axis=0), jnp.sum(upstream, axis=0))


def rotary_tables(positions):
    half_dim = HEAD_DIM // 2
    frequency = ROPE_BASE ** (-(jnp.arange(half_dim, dtype=jnp.float32) * 2.0 / HEAD_DIM))
    turned = positions.astype(jnp.float32)[..., None] * frequency
    return (jnp.cos(turned), jnp.sin(turned))


PAIR = 2 * HEAD_DIM
SPAN = 1024
STRIP = 256
PARTS = 4
BLOCK = 96
PART_BLOCKS = D // BLOCK
LANES = 128
ATTEND_CALLS = 3
BACK_CALLS = 6


BOTH = ("wide", "narrow")
GRAM_TILE = 256
GRAM_SPOTS = ((0, 0), (0, 1), (0, 2), (1, 1), (1, 2), (2, 2))


def swap(value, mask):
    total = lax.axis_size(BOTH)
    return lax.ppermute(value, BOTH, [(spot, spot ^ mask) for spot in range(total)])


def my_index():
    return lax.axis_index("wide") * lax.axis_size("narrow") + lax.axis_index("narrow")


def wide_masks():
    narrow_size = lax.axis_size("narrow")
    count = lax.axis_size("wide").bit_length() - 1
    return [narrow_size << bit for bit in reversed(range(count))]


def offsets_of(masks):
    table = [0]
    for mask in masks:
        table = table + [offset ^ mask for offset in table]
    return np.array(table)


def gate(value, others):
    leaves, form = jax.tree.flatten(value)
    held = lax.optimization_barrier(tuple(leaves) + tuple(jax.tree.leaves(others)))
    return jax.tree.unflatten(form, held[: len(leaves)])


def padded_rows(array):
    return jnp.pad(array, ((0, -array.shape[0] % 16), (0, 0)))


def together(values):
    leaves, form = jax.tree.flatten(values)
    return jax.tree.unflatten(form, lax.optimization_barrier(tuple(leaves)))


def gather_blocks(piece, masks):
    for mask in masks:
        piece = jnp.concatenate([piece, swap(piece, mask)], axis=0)
    return piece


def take_blocks(array, index):
    return jnp.take(array, index, axis=0, mode="clip")


def places_of(masks, unit):
    offsets = offsets_of(masks) // unit
    place = np.zeros_like(offsets)
    place[offsets] = np.arange(offsets.size)
    return place


def in_order(blocks, masks, unit, base):
    place = places_of(masks, unit)
    return take_blocks(blocks, jnp.asarray(place)[jnp.arange(place.size) ^ base])


def out_of_order(blocks, masks, unit, base):
    offsets = offsets_of(masks) // unit
    return take_blocks(blocks, jnp.asarray(offsets) ^ base)


def quarter_rows(array):
    count = array.shape[0] // lax.axis_size("narrow")
    return lax.dynamic_slice_in_dim(array, lax.axis_index("narrow") * count, count, 0)


def side_of(mask):
    return (my_index() // mask) % 2


def split_static(array, axis):
    return lax.index_in_dim(array, 0, axis, False), lax.index_in_dim(array, 1, axis, False)


def split_sided(array, axis, mask):
    side = side_of(mask)
    return (
        lax.dynamic_index_in_dim(array, side, axis, False),
        lax.dynamic_index_in_dim(array, 1 - side, axis, False),
    )


def halves(item, mask):
    array, marks, sided = item
    axis = marks.index(mask)
    keep, send = split_sided(array, axis, mask) if sided else split_static(array, axis)
    return (keep, marks[:axis] + marks[axis + 1 :], sided), send


def hop(items, mask, kind):
    pairs = [halves(item, mask) for item in items]
    rows = [send.astype(kind).reshape(-1, send.shape[-1]) for _, send in pairs]
    flat = jnp.concatenate(rows, axis=0) if len(rows) > 1 else rows[0]
    token = yield flat
    got = gate(swap(flat, mask), token)
    results, at = [], 0
    for ((keep, marks, sided), send), row in zip(pairs, rows):
        part = got[at : at + row.shape[0]].reshape(send.shape).astype(jnp.float32)
        results.append((keep + part, marks, sided))
        at += row.shape[0]
    return results


def finish(steps, token):
    try:
        steps.send(token)
    except StopIteration as stop:
        return stop.value


def finish_hop(steps):
    next(steps)
    return finish(steps, ())


def columns_of(items, start, stop):
    return [(array[..., start:stop], marks, sided) for array, marks, sided in items]


def sum_chain(items, kind):
    masks = wide_masks()
    width = items[0][0].shape[-1]
    ways = [columns_of(items, 0, width // 2), columns_of(items, width // 2, width)]
    for pair in ((masks[-1], 2), (2, masks[-1])):
        steps = [hop(way, mask, jnp.bfloat16) for way, mask in zip(ways, pair)]
        token = yield tuple(next(step) for step in steps)
        ways = [finish(step, token) for step in steps]
    items = [
        (jnp.concatenate([left[0], right[0]], axis=-1), left[1], left[2])
        for left, right in zip(*ways)
    ]
    for mask in reversed(masks[:-1]):
        items = yield from hop(items, mask, kind)
    return [item[0] for item in items]


def drain(chain, token):
    while True:
        try:
            chain.send(token)
        except StopIteration as stop:
            return stop.value


def bits_shape(count, tail):
    return (2,) * (count.bit_length() - 1) + tuple(tail)


class Chain:
    def __init__(self, steps):
        self.steps, self.result = steps, None
        self.request = next(steps)

    def give(self, got):
        try:
            self.request = self.steps.send(got)
        except StopIteration as stop:
            self.request, self.result = [], stop.value


def advance(chains, meanwhile=None, needs=()):
    sends, needs = together(([[array for array, _ in chain.request] for chain in chains], needs))
    gots = [
        [swap(array, mask) for array, (_, mask) in zip(send, chain.request)]
        for send, chain in zip(sends, chains)
    ]
    made = meanwhile(needs) if meanwhile else ()
    gots, made = together((gots, made))
    for chain, got in zip(chains, gots):
        chain.give(got)
    return made


def sum_small(blocks):
    (got,) = yield [(blocks, 1)]
    total = (blocks + got).reshape(bits_shape(blocks.shape[0], blocks.shape[1:]))
    masks = wide_masks()
    while masks:
        mask = masks[-1]
        keep, send = split_sided(total, len(masks) - 1, mask)
        (got,) = yield [(send, mask)]
        total = keep + got
        masks = masks[:-1]
    (got,) = yield [(total, 2)]
    return total + got


def sum_wide(value):
    for mask in reversed(wide_masks()):
        (got,) = yield [(value, mask)]
        value = value + got
    return value


def sum_gram(parts):
    masks = list(reversed(wide_masks()))
    ways = [masks, [masks[1], masks[0]] + masks[2:]]
    parts = list(parts)
    for step in range(len(masks)):
        pairs = [
            split_sided(part.reshape((2, part.shape[0] // 2) + part.shape[1:]), 0, way[step])
            for part, way in zip(parts, ways)
        ]
        gots = yield [(send, way[step]) for (_, send), way in zip(pairs, ways)]
        parts = [keep + got for (keep, _), got in zip(pairs, gots)]
    for step in reversed(range(len(masks))):
        gots = yield [(part, way[step]) for part, way in zip(parts, ways)]
        parts = [
            jnp.where(
                side_of(way[step]) == 0,
                jnp.concatenate([part, got], axis=0),
                jnp.concatenate([got, part], axis=0),
            )
            for part, got, way in zip(parts, gots, ways)
        ]
    return parts


def row_dot(left_side, right_side):
    return lax.dot_general(
        left_side, right_side, (((1,), (1,)), ((), ())), preferred_element_type=jnp.float32
    )


def split_two(values):
    high = values.astype(jnp.bfloat16)
    return high, (values - high.astype(jnp.float32)).astype(jnp.bfloat16)


def newton_kernel(
    low_ref, high_ref, rows_ref, added_ref, table_ref, out_ref,
    gram_now, other, left, right, rows_left,
):
    tile = GRAM_TILE
    trace = jnp.zeros((1, 1), jnp.float32)
    diagonal = lax.broadcasted_iota(jnp.int32, (tile, tile), 0) == lax.broadcasted_iota(
        jnp.int32, (tile, tile), 1
    )

    def span(number):
        return slice(number * tile, (number + 1) * tile)

    def turned_dot(left_side, right_side):
        return lax.dot_general(
            left_side,
            right_side,
            (((0,), (0,)), ((), ())),
            preferred_element_type=jnp.float32,
        )

    added_high, added_low = split_two(added_ref[...])
    added_rest = added_ref[...] - added_high.astype(jnp.float32) - added_low.astype(jnp.float32)
    added_parts = (added_high, added_low, added_rest.astype(jnp.bfloat16))
    half = len(GRAM_SPOTS) // 2
    for number, (row, column) in enumerate(GRAM_SPOTS):
        source = low_ref if number < half else high_ref
        block = source[span(number % half), :]
        for part in added_parts:
            block = block + turned_dot(part[:, span(row)], table_ref[:, span(column)])
            block = block + turned_dot(table_ref[:, span(row)], part[:, span(column)])
        gram_now[span(row), span(column)] = block
        if row == column:
            picked = jnp.where(diagonal, block, 0.0)
            trace = trace + jnp.sum(jnp.sum(picked, axis=0, keepdims=True), axis=1, keepdims=True)
    inverse = 1.0 / (jnp.sqrt(trace) + 1e-07)
    scale = inverse * inverse
    for row, column in GRAM_SPOTS:
        block = gram_now[span(row), span(column)] * scale
        gram_now[span(row), span(column)] = block
        if row != column:
            gram_now[span(column), span(row)] = block.T

    def set_left(values):
        high, low = split_two(values)
        left[:, 0:D] = high
        left[:, D : 2 * D] = high
        left[:, 2 * D : 3 * D] = low

    def set_right(values):
        high, low = split_two(values)
        right[0:D, :] = high
        right[D : 2 * D, :] = low
        right[2 * D : 3 * D, :] = high

    def set_rows(values):
        high, low = split_two(values)
        rows_left[:, 0:D] = high
        rows_left[:, D : 2 * D] = high
        rows_left[:, 2 * D : 3 * D] = low

    def product(target, finish):
        for column in range(D // tile):
            rows = (column + 1) * tile
            block = jnp.dot(left[0:rows, :], right[:, span(column)], preferred_element_type=jnp.float32)
            for row in range(column + 1):
                piece = finish(block[span(row), :], row, column)
                target[span(row), span(column)] = piece
                if row != column:
                    target[span(column), span(row)] = piece.T

    def same(block, row, column):
        return block

    def factor(block, row, column):
        block = NEWTON_B * gram_now[span(row), span(column)] + NEWTON_C * block
        if row == column:
            block = block + jnp.where(diagonal, NEWTON_A, 0.0)
        return block

    def set_factor():
        set_left(gram_now[...])
        set_right(gram_now[...])
        product(other, factor)
        set_right(other[...])

    def rows_product():
        return jnp.dot(rows_left[...], right[...], preferred_element_type=jnp.float32)

    set_rows(rows_ref[...] * inverse)

    def body(step, carry):
        set_factor()
        product(other, same)
        set_left(other[...])
        product(gram_now, same)
        set_rows(rows_product())
        return carry

    lax.fori_loop(0, NS_ITERS - 1, body, 0)
    set_factor()
    out_ref[...] = rows_product().astype(out_ref.dtype)


def newton_rows(gram_parts, rows, added, table):
    count = rows.shape[0]
    return pl.pallas_call(
        newton_kernel,
        out_shape=jax.ShapeDtypeStruct((count, D), jnp.bfloat16),
        in_specs=[pl.BlockSpec(memory_space=pltpu.VMEM)] * 5,
        out_specs=pl.BlockSpec(memory_space=pltpu.VMEM),
        scratch_shapes=[
            pltpu.VMEM((D, D), jnp.float32),
            pltpu.VMEM((D, D), jnp.float32),
            pltpu.VMEM((D, 3 * D), jnp.bfloat16),
            pltpu.VMEM((3 * D, D), jnp.bfloat16),
            pltpu.VMEM((count, 3 * D), jnp.bfloat16),
        ],
        compiler_params=pltpu.CompilerParams(vmem_limit_bytes=48 << 20),
        cost_estimate=pl.CostEstimate(flops=60 * D * D * D, bytes_accessed=4 << 20, transcendentals=0),
        name="newton",
    )(*gram_parts, rows, added, table)


def pack_kernel(spot_ref, *refs):
    out_ref = refs[-1]
    at = 0
    for ref in refs[:-1]:
        count = ref.shape[0]
        out_ref[at : at + count, :] = ref[...].astype(jnp.bfloat16)
        at += count
        room = -count % 16
        if room:
            out_ref[at : at + room, :] = jnp.zeros((room, D), jnp.bfloat16)
            at += room


def pack_rows(weights, spot):
    units = [weight.shape[0] // lax.axis_size("narrow") for weight in weights]
    total = sum(unit + -unit % 16 for unit in units)
    if any(unit % 8 for unit in units):
        return jnp.concatenate(
            [padded_rows(quarter_rows(weight).astype(jnp.bfloat16)) for weight in weights], axis=0
        )
    return pl.pallas_call(
        pack_kernel,
        grid_spec=pltpu.PrefetchScalarGridSpec(
            num_scalar_prefetch=1,
            grid=(1,),
            in_specs=[pl.BlockSpec((unit, D), lambda step, spot: (spot[0], 0)) for unit in units],
            out_specs=pl.BlockSpec((total, D), lambda step, spot: (0, 0)),
        ),
        out_shape=jax.ShapeDtypeStruct((total, D), jnp.bfloat16),
        name="pack",
    )(spot[None].astype(jnp.int32), *weights)


def entry_kernel(scale, *refs):
    (hot_ref, table_ref, gain_ref, middle_ref, weight_ref), refs = refs[:5], refs[5:]
    *low_refs, entry_ref, sums_ref, table_sum_ref = refs
    step = pl.program_id(0)
    hot = hot_ref[:, 0:LANES]
    stream = scale * jnp.dot(hot, table_ref[...], preferred_element_type=jnp.float32)
    grads = None
    for kind in range(3):
        low = jnp.concatenate([ref[kind] for ref in low_refs], axis=1)
        part = jnp.dot(
            low, weight_ref[kind * D : (kind + 1) * D, :], preferred_element_type=jnp.float32
        )
        grads = part if grads is None else grads + part
    center = stream - jnp.mean(stream, axis=-1, keepdims=True)
    inverse = lax.rsqrt(jnp.mean(center * center, axis=-1, keepdims=True) + NORM_EPS)
    normal = center * inverse
    scaled = grads * gain_ref[...]
    inner = (
        scaled
        - jnp.mean(scaled, axis=-1, keepdims=True)
        - normal * jnp.mean(scaled * normal, axis=-1, keepdims=True)
    )
    entry = middle_ref[...] + inverse * inner
    entry_ref[...] = entry
    sums = jnp.concatenate(
        [
            jnp.sum(grads * normal, axis=0, keepdims=True),
            jnp.sum(grads, axis=0, keepdims=True),
        ],
        axis=0,
    )
    high = entry.astype(jnp.bfloat16)
    rest = entry - high.astype(jnp.float32)
    middle = rest.astype(jnp.bfloat16)
    low = (rest - middle.astype(jnp.float32)).astype(jnp.bfloat16)
    table_sum = None
    for part in (high, middle, low):
        part = lax.dot_general(
            hot, part, (((0,), (0,)), ((), ())), preferred_element_type=jnp.float32
        )
        table_sum = part if table_sum is None else table_sum + part

    @pl.when(step == 0)
    def _():
        sums_ref[...] = sums
        table_sum_ref[...] = scale * table_sum

    @pl.when(step > 0)
    def _():
        sums_ref[...] += sums
        table_sum_ref[...] += scale * table_sum


def entry_call(scale, hot, table, gain, middle_grad, weight, lows):
    rows = SEQ_LEN // 3
    whole = lambda step: (0, 0)
    own = lambda step: (step, 0)
    return pl.pallas_call(
        partial(entry_kernel, scale),
        grid=(3,),
        in_specs=[
            pl.BlockSpec((rows, hot.shape[1]), own),
            pl.BlockSpec(table.shape, whole),
            pl.BlockSpec(gain.shape, whole),
            pl.BlockSpec((rows, D), own),
            pl.BlockSpec(weight.shape, whole),
        ]
        + [pl.BlockSpec((3, rows, low.shape[2]), lambda step: (0, step, 0)) for low in lows],
        out_specs=[
            pl.BlockSpec((rows, D), own),
            pl.BlockSpec((2, D), whole),
            pl.BlockSpec((LANES, D), whole),
        ],
        out_shape=[
            jax.ShapeDtypeStruct((SEQ_LEN, D), jnp.float32),
            jax.ShapeDtypeStruct((2, D), jnp.float32),
            jax.ShapeDtypeStruct((LANES, D), jnp.float32),
        ],
        compiler_params=pltpu.CompilerParams(vmem_limit_bytes=48 << 20),
        cost_estimate=pl.CostEstimate(flops=1 << 20, bytes_accessed=1 << 16, transcendentals=0),
        name="entry",
    )(hot, table, gain, middle_grad, weight, *lows)


def small_kernel(parts, spot_rows, table_sum_ref, head_ref, hist_ref, *refs):
    part_refs, refs = refs[:parts], refs[parts:]
    *row_refs, out_ref, sums, held = refs
    for number, part in enumerate(part_refs):
        width = part.shape[2]
        for kind in range(3):
            start = kind * D + number * width
            sums[:, start : start + width] = part[kind]
    held[0:VOCAB, :] = table_sum_ref[0:VOCAB, :] + head_ref[...]
    bias = jnp.sum(sums[...], axis=0, keepdims=True)
    for kind in range(3):
        held[VOCAB + 6 + kind : VOCAB + 7 + kind, :] = bias[:, kind * D : (kind + 1) * D]
    for ref, at in zip(row_refs, spot_rows):
        for row in range(ref.shape[0]):
            for part in range(ref.shape[1] // D):
                held[at : at + 1, :] = ref[row : row + 1, part * D : (part + 1) * D]
                at += 1
    count, rows, columns = out_ref.shape
    narrow = D // count
    wide = columns - narrow
    base = held.shape[0]
    for number in range(count):
        out_ref[number, 0:VOCAB, 0:wide] = sums[0:VOCAB, number * wide : (number + 1) * wide]
        out_ref[number, VOCAB:rows, 0:wide] = jnp.zeros((rows - VOCAB, wide), jnp.float32)
        out_ref[number, 0:base, wide:columns] = held[:, number * narrow : (number + 1) * narrow]
        out_ref[number, base:rows, wide:columns] = hist_ref[...]


def small_blocks(parts, table_sum, head, hist, rows, wide_size):
    whole = pl.BlockSpec(memory_space=pltpu.VMEM)
    total = VOCAB + 15 + hist.shape[0]
    arrays = [array for array, _ in rows]
    return pl.pallas_call(
        partial(small_kernel, len(parts), tuple(VOCAB + place for _, place in rows)),
        in_specs=[whole] * (3 + len(parts) + len(rows)),
        out_specs=whole,
        out_shape=jax.ShapeDtypeStruct((wide_size, total, 4 * D // wide_size), jnp.float32),
        scratch_shapes=[
            pltpu.VMEM((LANES, 3 * D), jnp.float32),
            pltpu.VMEM((VOCAB + 15, D), jnp.float32),
        ],
        cost_estimate=pl.CostEstimate(flops=1 << 20, bytes_accessed=1 << 16, transcendentals=0),
        name="small_grads",
    )(table_sum, head, hist, *parts, *arrays)


def dense_kernel(units, spot_ref, own_ref, beside_ref, core_ref, cross_ref, *refs):
    base_ref, *refs = refs
    count = len(units)
    moment_refs, refs = refs[:count], refs[count:]
    total_refs, next_refs, refs = refs[:count], refs[count : 2 * count], refs[2 * count :]
    rows_ref, low_ref, high_ref, left, right = refs
    spot = spot_ref[0]
    for device in range(4):
        way = spot ^ device
        for kind, source in enumerate((own_ref, core_ref, beside_ref, cross_ref)):

            @pl.when(way == kind)
            def _():
                at = 0
                for total_ref, unit in zip(total_refs, units):
                    total_ref[device * unit : (device + 1) * unit, :] = source[at : at + unit, :]
                    at += unit

    rows_ref[...] = jnp.zeros_like(rows_ref)

    @pl.when(spot == 0)
    def _():
        rows_ref[0 : base_ref.shape[0], :] = (MUON_MU * MUON_MU) * base_ref[...]

    for number in range(count):
        gradient = total_refs[number][...]
        moment_next = MUON_MU * moment_refs[number][...] + (1.0 - MUON_MU) * gradient
        next_refs[number][...] = moment_next
        place = count - number

        @pl.when(spot == place)
        def _():
            rows_ref[0 : gradient.shape[0], :] = (
                1.0 - MUON_MU
            ) * gradient + MUON_MU * moment_next

    high, low = split_two(rows_ref[...])
    depth = rows_ref.shape[0]
    right[0:depth, :] = high
    right[depth : 2 * depth, :] = low
    right[2 * depth : 3 * depth, :] = high
    turned_high, turned_low = split_two(rows_ref[...].T)
    left[:, 0:depth] = turned_high
    left[:, depth : 2 * depth] = turned_high
    left[:, 2 * depth : 3 * depth] = turned_low
    half = len(GRAM_SPOTS) // 2
    for number, (row, column) in enumerate(GRAM_SPOTS):
        target = low_ref if number < half else high_ref
        at = (number % half) * GRAM_TILE
        target[at : at + GRAM_TILE, :] = jnp.dot(
            left[row * GRAM_TILE : (row + 1) * GRAM_TILE, :],
            right[:, column * GRAM_TILE : (column + 1) * GRAM_TILE],
            preferred_element_type=jnp.float32,
        )


def dense_step(spot, units, pieces, base, moments):
    whole = pl.BlockSpec(memory_space=pltpu.VMEM)
    most = max(moment.shape[0] for moment in moments)
    shapes = [jax.ShapeDtypeStruct(moment.shape, jnp.float32) for moment in moments]
    half = jax.ShapeDtypeStruct((len(GRAM_SPOTS) // 2 * GRAM_TILE, GRAM_TILE), jnp.float32)
    results = pl.pallas_call(
        partial(dense_kernel, units),
        in_specs=[pl.BlockSpec(memory_space=pltpu.SMEM)] + [whole] * (5 + len(moments)),
        out_specs=[whole] * (2 * len(moments) + 3),
        out_shape=shapes + shapes + [jax.ShapeDtypeStruct((most, D), jnp.float32), half, half],
        scratch_shapes=[
            pltpu.VMEM((D, 3 * most), jnp.bfloat16),
            pltpu.VMEM((3 * most, D), jnp.bfloat16),
        ],
        compiler_params=pltpu.CompilerParams(vmem_limit_bytes=48 << 20),
        cost_estimate=pl.CostEstimate(flops=1 << 20, bytes_accessed=1 << 16, transcendentals=0),
        name="dense_step",
    )(spot[None].astype(jnp.int32), *pieces, base, *moments)
    count = len(moments)
    return results[:count], results[count : 2 * count], results[2 * count], results[2 * count + 1 :]


def update_kernel(rates, spot_ref, *refs):
    count = len(rates)
    sources, refs = refs[:4], refs[4:]
    for number in range(count):
        weight_ref, out_ref = refs[number], refs[count + number]
        rows = weight_ref.shape[0]
        way = spot_ref[0] ^ number
        for kind, source in enumerate(sources):

            @pl.when(way == kind)
            def _():
                out_ref[...] = weight_ref[...] * (1.0 - MUON_RATE * MUON_DECAY) - rates[
                    number
                ] * source[0:rows, :].astype(jnp.float32)


def update_rows(spot, orthos, weights, rates):
    whole = pl.BlockSpec(memory_space=pltpu.VMEM)
    return pl.pallas_call(
        partial(update_kernel, rates),
        in_specs=[pl.BlockSpec(memory_space=pltpu.SMEM)] + [whole] * (4 + len(weights)),
        out_specs=[whole] * len(weights),
        out_shape=[jax.ShapeDtypeStruct(weight.shape, jnp.float32) for weight in weights],
        compiler_params=pltpu.CompilerParams(vmem_limit_bytes=40 << 20),
        cost_estimate=pl.CostEstimate(flops=1 << 20, bytes_accessed=1 << 16, transcendentals=0),
        name="update",
    )(spot[None].astype(jnp.int32), *orthos, *weights)


def heads_kernel(place_ref, blocks_ref, bias_ref, out_ref, held):
    count, rows, columns = blocks_ref.shape
    held[rows : held.shape[0], :] = jnp.zeros((held.shape[0] - rows, 3 * D), jnp.float32)
    for number in range(count):
        spot = slice(number * columns, (number + 1) * columns)
        held[0:rows, spot] = blocks_ref[place_ref[number]] + bias_ref[:, spot]
    high, low = split_two(held[...])
    some = held.shape[0]
    none = jnp.zeros((LANES - some, 3 * D), jnp.bfloat16)
    out_ref[0:some, :] = high
    out_ref[some:LANES, :] = none
    out_ref[LANES : LANES + some, :] = low
    out_ref[LANES + some : 2 * LANES, :] = none


def heads_table(blocks, place, bias):
    return pl.pallas_call(
        heads_kernel,
        grid_spec=pltpu.PrefetchScalarGridSpec(
            num_scalar_prefetch=1,
            grid=(1,),
            in_specs=[
                pl.BlockSpec(blocks.shape, lambda step, place: (0, 0, 0)),
                pl.BlockSpec(bias.shape, lambda step, place: (0, 0)),
            ],
            out_specs=pl.BlockSpec((2 * LANES, 3 * D), lambda step, place: (0, 0)),
            scratch_shapes=[pltpu.VMEM((VOCAB + -VOCAB % 16, 3 * D), jnp.float32)],
        ),
        out_shape=jax.ShapeDtypeStruct((2 * LANES, 3 * D), jnp.bfloat16),
        name="heads_table",
    )(place, blocks, bias)


def turn(values, cosine, sine_table):
    lane = lax.broadcasted_iota(jnp.int32, values.shape, 1)
    half = HEAD_DIM // 2
    partner = jnp.where(
        lane % HEAD_DIM < half,
        pltpu.roll(values, PAIR - half, 1),
        pltpu.roll(values, half, 1),
    )
    return values * cosine + partner * sine_table


def attend_kernel(
    hot_ref, tq_ref, tk_ref, tv_ref, cos_ref, sin_ref,
    q_ref, k_ref, v_ref, mixed_ref, log_ref,
    q_all, v_turned, mixed_turned, prob_all,
):
    hot = hot_ref[...]
    cosine = cos_ref[...]
    sine_table = sin_ref[...]
    queries = jnp.dot(hot, tq_ref[...], preferred_element_type=jnp.float32)
    queries = turn(queries, cosine, sine_table).astype(jnp.bfloat16) * HEAD_DIM ** (-0.5)
    queries = queries.astype(jnp.bfloat16)
    q_ref[...] = queries
    q_all[0:SEQ_LEN, :] = queries
    q_all[SEQ_LEN:SPAN, :] = jnp.zeros((SPAN - SEQ_LEN, PAIR), jnp.bfloat16)
    keys = jnp.dot(hot, tk_ref[...], preferred_element_type=jnp.float32)
    keys = turn(keys, cosine, sine_table).astype(jnp.bfloat16)
    k_ref[...] = keys
    values = jnp.dot(hot, tv_ref[...], preferred_element_type=jnp.float32)
    v_ref[...] = values.astype(jnp.bfloat16)
    v_turned[...] = values.T.astype(jnp.bfloat16)

    def one_head(head, carry):
        lane = lax.broadcasted_iota(jnp.int32, (SEQ_LEN, PAIR), 1)
        keys_head = jnp.where(lane // HEAD_DIM == head, k_ref[...], jnp.zeros((), jnp.bfloat16))
        head_rows = pl.ds(pl.multiple_of(head * HEAD_DIM, HEAD_DIM), HEAD_DIM)
        values_head = v_turned[head_rows, :]

        def body(step, carry):
            at = pl.multiple_of(step * STRIP, STRIP)
            scores = row_dot(keys_head, q_all[pl.ds(at, STRIP), :])
            peak = jnp.max(scores, axis=0, keepdims=True)
            powers = jnp.exp(scores - peak)
            total = jnp.sum(powers, axis=0, keepdims=True)
            prob_low = (powers * (1.0 / total)).astype(jnp.bfloat16)
            prob_all[:, pl.ds(at, STRIP)] = prob_low
            log_ref[0, pl.ds(head, 1), pl.ds(at, STRIP)] = peak + jnp.log(total)
            return carry

        lax.fori_loop(0, SPAN // STRIP, body, 0, unroll=SPAN // STRIP)
        mixed_turned[head_rows, :] = jnp.dot(
            values_head, prob_all[...], preferred_element_type=jnp.float32
        )
        return carry

    lax.fori_loop(0, 2, one_head, 0, unroll=2)
    mixed_ref[...] = mixed_turned[...].T[0:SEQ_LEN, :].astype(jnp.bfloat16)


def attend_call(hot, tables, cosine, sine_table, first, count):
    whole = lambda step: (0, 0)
    source = lambda step: (0, step + first)
    own = lambda step: (0, step)
    rows_low = jax.ShapeDtypeStruct((SEQ_LEN, count * PAIR), jnp.bfloat16)
    return pl.pallas_call(
        attend_kernel,
        grid=(count,),
        in_specs=[
            pl.BlockSpec(hot.shape, whole),
            pl.BlockSpec((hot.shape[1], PAIR), source),
            pl.BlockSpec((hot.shape[1], PAIR), lambda step: (0, step + first + D // PAIR)),
            pl.BlockSpec((hot.shape[1], PAIR), lambda step: (0, step + first + 2 * D // PAIR)),
            pl.BlockSpec((SEQ_LEN, PAIR), whole),
            pl.BlockSpec((SEQ_LEN, PAIR), whole),
        ],
        out_specs=[
            pl.BlockSpec((SEQ_LEN, PAIR), own),
            pl.BlockSpec((SEQ_LEN, PAIR), own),
            pl.BlockSpec((SEQ_LEN, PAIR), own),
            pl.BlockSpec((SEQ_LEN, PAIR), own),
            pl.BlockSpec((1, 2, SPAN), lambda step: (step, 0, 0)),
        ],
        out_shape=[rows_low] * 4 + [jax.ShapeDtypeStruct((count, 2, SPAN), jnp.float32)],
        scratch_shapes=[
            pltpu.VMEM((SPAN, PAIR), jnp.bfloat16),
            pltpu.VMEM((PAIR, SEQ_LEN), jnp.bfloat16),
            pltpu.VMEM((PAIR, SPAN), jnp.float32),
            pltpu.VMEM((SEQ_LEN, SPAN), jnp.bfloat16),
        ],
        compiler_params=pltpu.CompilerParams(vmem_limit_bytes=40 << 20),
        cost_estimate=pl.CostEstimate(
            flops=count * SPAN * SPAN, bytes_accessed=1 << 16,
            transcendentals=0,
        ),
        name="attend",
    )(hot, tables, tables, tables, cosine, sine_table)


def attend_back_kernel(
    hot_ref, q_ref, k_ref, v_ref, grad_ref, log_ref, cos_ref, sin_ref,
    low_ref, sums_ref,
    q_all, grad_all, k_turned, prob_all, score_all, query_turned, key_sum, value_sum,
):
    rest = jnp.zeros((SPAN - SEQ_LEN, PAIR), jnp.bfloat16)
    q_all[0:SEQ_LEN, :] = q_ref[...]
    q_all[SEQ_LEN:SPAN, :] = rest
    grad_all[0:SEQ_LEN, :] = grad_ref[...]
    grad_all[SEQ_LEN:SPAN, :] = rest
    k_turned[...] = k_ref[...].astype(jnp.float32).T.astype(jnp.bfloat16)
    lane = lax.broadcasted_iota(jnp.int32, (SEQ_LEN, PAIR), 1)
    none = jnp.zeros((), jnp.bfloat16)

    def one_head(head, carry):
        head_rows = pl.ds(pl.multiple_of(head * HEAD_DIM, HEAD_DIM), HEAD_DIM)
        keys_head = jnp.where(lane // HEAD_DIM == head, k_ref[...], none)
        values_head = jnp.where(lane // HEAD_DIM == head, v_ref[...], none)

        def body(step, carry):
            at = pl.multiple_of(step * STRIP, STRIP)
            scores = row_dot(keys_head, q_all[pl.ds(at, STRIP), :])
            prob_rows = jnp.exp(scores - log_ref[0, pl.ds(head, 1), pl.ds(at, STRIP)])
            prob_all[:, pl.ds(at, STRIP)] = prob_rows.astype(jnp.bfloat16)
            prob_grad = row_dot(values_head, grad_all[pl.ds(at, STRIP), :])
            delta = jnp.sum(prob_grad * prob_rows, axis=0, keepdims=True)
            score_all[:, pl.ds(at, STRIP)] = (prob_rows * (prob_grad - delta)).astype(jnp.bfloat16)
            return carry

        lax.fori_loop(0, SPAN // STRIP, body, 0, unroll=SPAN // STRIP)
        value_part = jnp.dot(prob_all[...], grad_all[...], preferred_element_type=jnp.float32)
        key_part = jnp.dot(score_all[...], q_all[...], preferred_element_type=jnp.float32)
        value_sum[...] = jnp.where(lane // HEAD_DIM == head, value_part, value_sum[...])
        key_sum[...] = jnp.where(lane // HEAD_DIM == head, key_part, key_sum[...])
        query_turned[head_rows, :] = (
            jnp.dot(k_turned[head_rows, :], score_all[...], preferred_element_type=jnp.float32)
            * HEAD_DIM ** (-0.5)
        )
        return carry

    lax.fori_loop(0, 2, one_head, 0, unroll=2)
    cosine = cos_ref[...]
    sine_table = -sin_ref[...]
    hot = hot_ref[...]
    query_low = turn(query_turned[...].T[0:SEQ_LEN, :], cosine, sine_table).astype(jnp.bfloat16)
    key_low = turn(key_sum[...], cosine, sine_table).astype(jnp.bfloat16)
    value_low = value_sum[...].astype(jnp.bfloat16)
    for number, low in enumerate((query_low, key_low, value_low)):
        low_ref[number] = low
        sums_ref[number] = jnp.dot(hot, low, preferred_element_type=jnp.float32)


def attend_back_call(
    hot_turned, queries, keys, values, gradients, logs, cosine, sine_table, first, inside, count
):
    whole = lambda step: (0, 0)
    rows = pl.BlockSpec((SEQ_LEN, PAIR), lambda step: (0, step + inside))
    whole_rows = pl.BlockSpec((SEQ_LEN, PAIR), whole)
    return pl.pallas_call(
        attend_back_kernel,
        grid=(count,),
        in_specs=[
            pl.BlockSpec(hot_turned.shape, whole),
            rows,
            rows,
            rows,
            pl.BlockSpec((SEQ_LEN, PAIR), lambda step: (0, step + first)),
            pl.BlockSpec((1, 2, SPAN), lambda step: (step + inside, 0, 0)),
            whole_rows,
            whole_rows,
        ],
        out_specs=[
            pl.BlockSpec((3, SEQ_LEN, PAIR), lambda step: (0, 0, step)),
            pl.BlockSpec((3, hot_turned.shape[0], PAIR), lambda step: (0, 0, step)),
        ],
        out_shape=[
            jax.ShapeDtypeStruct((3, SEQ_LEN, count * PAIR), jnp.bfloat16),
            jax.ShapeDtypeStruct((3, hot_turned.shape[0], count * PAIR), jnp.float32),
        ],
        scratch_shapes=[
            pltpu.VMEM((SPAN, PAIR), jnp.bfloat16),
            pltpu.VMEM((SPAN, PAIR), jnp.bfloat16),
            pltpu.VMEM((PAIR, SEQ_LEN), jnp.bfloat16),
            pltpu.VMEM((SEQ_LEN, SPAN), jnp.bfloat16),
            pltpu.VMEM((SEQ_LEN, SPAN), jnp.bfloat16),
            pltpu.VMEM((PAIR, SPAN), jnp.float32),
            pltpu.VMEM((SEQ_LEN, PAIR), jnp.float32),
            pltpu.VMEM((SEQ_LEN, PAIR), jnp.float32),
        ],
        compiler_params=pltpu.CompilerParams(vmem_limit_bytes=48 << 20),
        cost_estimate=pl.CostEstimate(
            flops=count * SPAN * SPAN, bytes_accessed=1 << 16,
            transcendentals=0,
        ),
        name="attend_back",
    )(hot_turned, queries, keys, values, gradients, logs, cosine, sine_table)


ERF_P = 0.3275911
ERF_A = (0.254829592, -0.284496736, 1.421413741, -1.453152027, 1.061405429)

def normal_parts(values):
    size = jnp.abs(values)
    bell = jnp.exp(values * values * -0.5)
    step = 1.0 / (1.0 + (ERF_P * 0.5**0.5) * size)
    series = ERF_A[4]
    for factor in (ERF_A[3], ERF_A[2], ERF_A[1], ERF_A[0]):
        series = series * step + factor
    tail = (0.5 * series) * step * bell
    return jnp.where(values < 0.0, tail, 1.0 - tail), bell * (1.0 / math.sqrt(2.0 * math.pi))

def start_parts(place_ref, source_ref, starts, held, sems):
    for part in range(PARTS):
        for number, start in enumerate(starts):

            def body(spot, carry):
                pltpu.make_async_copy(
                    source_ref.at[place_ref[part * PART_BLOCKS + spot], pl.ds(start, BLOCK), :],
                    held[number].at[part, spot],
                    sems.at[number, part],
                ).start()
                return carry

            lax.fori_loop(0, PART_BLOCKS, body, 0)


def wait_part(source_ref, number, held, sems, step):
    pltpu.make_async_copy(
        source_ref.at[pl.ds(0, PART_BLOCKS), pl.ds(0, BLOCK), :],
        held[number].at[step],
        sems.at[number, step],
    ).wait()
    return held[number][step].reshape(D, D)


def feed_kernel(starts, place_ref, rows_ref, bias_ref, source_ref, hidden_ref, slope_ref, out_ref, expand_held, reduce_held, sems):
    held = (expand_held, reduce_held)
    step = pl.program_id(0)
    @pl.when(step == 0)
    def _():
        start_parts(place_ref, source_ref, starts, held, sems)

    expand = wait_part(source_ref, 0, held, sems, step)
    for at in range(0, SEQ_LEN, 304):
        spot = slice(at, at + 304)
        values = row_dot(rows_ref[spot, :], expand) + bias_ref[...]
        below, bell = normal_parts(values)
        hidden_ref[spot, :] = (values * below).astype(jnp.bfloat16)
        slope_ref[spot, :] = (below + values * bell).astype(jnp.bfloat16)
    reduce = wait_part(source_ref, 1, held, sems, step)
    part = jnp.dot(hidden_ref[...], reduce, preferred_element_type=jnp.float32)
    @pl.when(step == 0)
    def _():
        out_ref[...] = part
    @pl.when(step > 0)
    def _():
        out_ref[...] += part

def feed_call(place, rows, bias, source, starts):
    whole = lambda step, place: (0, 0)
    chunk = pl.BlockSpec((SEQ_LEN, D), lambda step, place: (0, step))
    return pl.pallas_call(
        partial(feed_kernel, starts),
        grid_spec=pltpu.PrefetchScalarGridSpec(
            num_scalar_prefetch=1,
            grid=(PARTS,),
            in_specs=[
                pl.BlockSpec((SEQ_LEN, D), whole),
                pl.BlockSpec((1, D), lambda step, place: (0, step)),
                pl.BlockSpec(memory_space=pl.ANY),
            ],
            out_specs=[chunk, chunk, pl.BlockSpec((SEQ_LEN, D), whole)],
            scratch_shapes=[
                pltpu.VMEM((PARTS, PART_BLOCKS, BLOCK, D), jnp.bfloat16),
                pltpu.VMEM((PARTS, PART_BLOCKS, BLOCK, D), jnp.bfloat16),
                pltpu.SemaphoreType.DMA((2, PARTS)),
            ],
        ),
        out_shape=[jax.ShapeDtypeStruct((SEQ_LEN, FF), jnp.bfloat16)] * 2
        + [jax.ShapeDtypeStruct((SEQ_LEN, D), jnp.float32)],
        compiler_params=pltpu.CompilerParams(vmem_limit_bytes=48 << 20),
        cost_estimate=pl.CostEstimate(
            flops=SEQ_LEN * D * FF, bytes_accessed=1 << 16, transcendentals=0
        ),
        name="feed",
    )(place, rows, bias, source)


def feed_back_kernel(starts, place_ref, grad_ref, slope_ref, source_ref, pre_ref, out_ref, bias_ref, expand_held, reduce_held, sems):
    held = (expand_held, reduce_held)
    step = pl.program_id(0)
    @pl.when(step == 0)
    def _():
        start_parts(place_ref, source_ref, starts, held, sems)

    reduce = wait_part(source_ref, 1, held, sems, step)
    total = jnp.zeros((1, D), jnp.float32)
    for at in range(0, SEQ_LEN, 304):
        spot = slice(at, at + 304)
        grad = row_dot(grad_ref[spot, :], reduce) * slope_ref[spot, :].astype(jnp.float32)
        low = grad.astype(jnp.bfloat16)
        pre_ref[spot, :] = low
        total = total + jnp.sum(low.astype(jnp.float32), axis=0, keepdims=True)
    bias_ref[...] = total
    low = pre_ref[...]
    expand = wait_part(source_ref, 0, held, sems, step)
    part = jnp.dot(low, expand, preferred_element_type=jnp.float32)
    @pl.when(step == 0)
    def _():
        out_ref[...] = part
    @pl.when(step > 0)
    def _():
        out_ref[...] += part

def feed_back_call(place, grad, slope, source, starts):
    whole = lambda step, place: (0, 0)
    chunk = pl.BlockSpec((SEQ_LEN, D), lambda step, place: (0, step))
    return pl.pallas_call(
        partial(feed_back_kernel, starts),
        grid_spec=pltpu.PrefetchScalarGridSpec(
            num_scalar_prefetch=1,
            grid=(PARTS,),
            in_specs=[
                pl.BlockSpec((SEQ_LEN, D), whole),
                chunk,
                pl.BlockSpec(memory_space=pl.ANY),
            ],
            out_specs=[
                chunk,
                pl.BlockSpec((SEQ_LEN, D), whole),
                pl.BlockSpec((1, D), lambda step, place: (0, step)),
            ],
            scratch_shapes=[
                pltpu.VMEM((PARTS, PART_BLOCKS, BLOCK, D), jnp.bfloat16),
                pltpu.VMEM((PARTS, PART_BLOCKS, BLOCK, D), jnp.bfloat16),
                pltpu.SemaphoreType.DMA((2, PARTS)),
            ],
        ),
        out_shape=[
            jax.ShapeDtypeStruct((SEQ_LEN, FF), jnp.bfloat16),
            jax.ShapeDtypeStruct((SEQ_LEN, D), jnp.float32),
            jax.ShapeDtypeStruct((1, FF), jnp.float32),
        ],
        compiler_params=pltpu.CompilerParams(vmem_limit_bytes=48 << 20),
        cost_estimate=pl.CostEstimate(
            flops=SEQ_LEN * D * FF, bytes_accessed=1 << 16, transcendentals=0
        ),
        name="feed_back",
    )(place, grad, slope, source)


def adam_step(weight, mean_state, square, gradient, step_rate, decay_rate, step_count):
    mean_next = ADAM_BETA1 * mean_state + (1.0 - ADAM_BETA1) * gradient
    square_next = ADAM_BETA2 * square + (1.0 - ADAM_BETA2) * gradient * gradient
    step_float = step_count.astype(jnp.float32)
    mean_hat = mean_next / (1.0 - ADAM_BETA1**step_float)
    square_hat = square_next / (1.0 - ADAM_BETA2**step_float)
    updated = weight - step_rate * (
        mean_hat / (jnp.sqrt(square_hat) + ADAM_EPS) + decay_rate * weight
    )
    return (updated, mean_next, square_next)


def on_device(
    codons,
    offsets,
    positions,
    targets,
    table_weight,
    attend_weight,
    mixing_weight,
    expand_weight,
    reduce_weight,
    vector_params,
    attend_moment,
    mixing_moment,
    expand_moment,
    reduce_moment,
    table_mean,
    table_square,
    vector_mean,
    vector_square,
    step_count,
):
    low_type = jnp.bfloat16
    wide_at = lax.axis_index("wide")
    me = my_index()
    devices = lax.axis_size(BOTH)
    masks = wide_masks()
    narrow_size = lax.axis_size("narrow")
    wide_size = lax.axis_size("wide")
    hidden_masks = masks[:-1] + [2, masks[-1], 1]
    all_masks = masks + [2, 1]
    small = jnp.concatenate([table_weight, vector_params], axis=0).astype(low_type)
    small = gather_blocks(small[None], masks)
    packed = (expand_weight, reduce_weight, mixing_weight, attend_weight)
    units = [weight.shape[0] // narrow_size for weight in packed]
    starts = np.cumsum([0] + [unit + -unit % 16 for unit in units])
    packed_low = pack_rows(packed, lax.axis_index("narrow"))
    weights_low = lax.all_gather(packed_low[: int(starts[3])], BOTH, axis=0)
    attend_own = packed_low[int(starts[3]) : int(starts[3]) + units[3]]

    def weight_rows(number, unit):
        start = int(starts[number])
        return weights_low[:, start : start + unit].reshape(-1, D)

    codons, positions, targets = gate((codons, positions, targets), small)
    small = in_order(small, masks, narrow_size, wide_at)
    small = jnp.transpose(small, (1, 0, 2)).reshape(VOCAB + 15, D)
    table_low = small[:VOCAB]
    vector_full = small[VOCAB:].astype(jnp.float32)
    gain_one = vector_full[0]
    bias_one = vector_full[1]
    gain_two = vector_full[2]
    bias_two = vector_full[3]
    gain_last = vector_full[4]
    bias_last = vector_full[5]
    attend_bias = vector_full[6:9].reshape(1, 3 * D)
    mixing_bias = vector_full[9]
    reduce_bias = vector_full[10]
    expand_bias = out_of_order(
        vector_full[11:15].reshape(devices, FF // devices), hidden_masks, 1, me
    ).reshape(FF)
    embed_scale = math.sqrt(D)
    table_stream = embed_scale * table_low.astype(jnp.float32)
    table_normed = norm_forward(table_stream, gain_one, bias_one)[0].astype(low_type)
    table_own = times_trans(table_normed, attend_own)
    place = jnp.asarray(places_of(all_masks, 1), jnp.int32)[jnp.arange(devices) ^ me]
    tables = heads_table(gather_blocks(table_own[None], all_masks), place, attend_bias)

    unit = FF // devices
    hidden_place = jnp.asarray(offsets_of(hidden_masks)) ^ me
    if unit == BLOCK:
        feed_place, feed_source, feed_starts = hidden_place, weights_low, tuple(starts[:2])
    else:
        feed_source = jnp.concatenate(
            [
                take_blocks(weights_low[:, start : start + unit], hidden_place).reshape(-1, BLOCK, D)
                for start in (int(starts[0]), int(starts[1]))
            ],
            axis=1,
        )
        feed_place, feed_starts = jnp.arange(FF // BLOCK), (0, BLOCK)
    feed_place = feed_place.astype(jnp.int32)
    feed_starts = tuple(int(start) for start in feed_starts)

    seq_count = codons.shape[0]
    row_count = seq_count * SEQ_LEN
    window = jax.vmap(partial(lax.dynamic_slice_in_dim, slice_size=SEQ_LEN))(codons, offsets)
    vocab_ids = jnp.arange(VOCAB, dtype=jnp.int32)
    token_hot = window.reshape(row_count)[:, None] == vocab_ids[None, :]
    token_low = token_hot.astype(low_type)
    target_hot = (targets.reshape(row_count)[:, None] == vocab_ids[None, :]).astype(jnp.float32)
    stream = embed_scale * times_plain(token_low, table_low)
    token_ids = window.reshape(row_count)
    lane_ids = jnp.arange(2 * LANES, dtype=jnp.int32) % LANES
    hot = (token_ids[:, None] == lane_ids[None, :]).astype(low_type)
    hot_turned = (token_ids[None, :] == lane_ids[:LANES, None]).astype(low_type)
    cosine, sine_table = rotary_tables(positions.reshape(row_count))
    cosine = jnp.concatenate([cosine] * 4, axis=1)
    sine_table = jnp.concatenate([-sine_table, sine_table] * 2, axis=1)
    pairs = D // PAIR // ATTEND_CALLS
    attended = []

    for number in range(ATTEND_CALLS):
        attended.append(
            attend_call(hot, tables, cosine, sine_table, number * pairs, pairs)
        )
    last_mask = masks[-1]
    mixed_low = jnp.concatenate([parts[3] for parts in attended], axis=1)
    mixing_low = weight_rows(2, D // devices)
    attend_low = lax.all_gather(gate(attend_own, mixed_low), BOTH, axis=0)
    branch = times_trans(mixed_low, mixing_low) + mixing_bias
    middle = stream + branch
    normed_two, normal_two, inverse_two = norm_forward(middle, gain_two, bias_two)
    normed_two_low = normed_two.astype(low_type)
    hidden_low, slope_low, feed_out = feed_call(
        feed_place, normed_two_low, expand_bias[None, :], feed_source, feed_starts
    )
    feed_out = feed_out + reduce_bias
    output = middle + feed_out
    final_norm, normal_last, inverse_last = norm_forward(output, gain_last, bias_last)
    final_low = final_norm.astype(low_type)
    logits = times_trans(final_low, table_low)
    row_peak = jnp.max(logits, axis=-1, keepdims=True)
    shifted = jnp.exp(logits - row_peak)
    prob_rows = shifted / jnp.sum(shifted, axis=-1, keepdims=True)
    prob_sum = jnp.sum(prob_rows, axis=0)
    logit_grad = (prob_rows - target_hot).astype(low_type)
    final_grad = times_plain(logit_grad, table_low)
    table_head = trans_times(logit_grad, final_low)
    output_grad, gain_last_grad, bias_last_grad = norm_backward(
        final_grad, normal_last, inverse_last, gain_last
    )
    feed_low = output_grad.astype(low_type)
    reduce_bias_grad = jnp.sum(feed_low, axis=0, dtype=jnp.float32)
    half_ff = FF // 2
    static_marks = [masks[-1], 2] + list(reversed(masks[:-1]))
    static_shape = (2,) * len(static_marks) + (unit, D)

    reduce_send = trans_times(hidden_low[:, half_ff:], feed_low).astype(low_type)
    pre_grad, normed_two_grad, expand_bias_grad = feed_back_call(
        feed_place, gate(feed_low, reduce_send), slope_low, feed_source, feed_starts
    )
    reduce_got = gate(swap(reduce_send, 1), pre_grad)
    reduce_sum = trans_times(hidden_low[:, :half_ff], feed_low) + reduce_got
    reduce_chain = sum_chain([(reduce_sum.reshape(static_shape), static_marks, False)], low_type)
    reduce_sent = next(reduce_chain)
    expand_send = trans_times(
        gate(pre_grad, reduce_sent)[:, half_ff:], normed_two_low
    ).astype(low_type)
    expand_sum = trans_times(pre_grad[:, :half_ff], normed_two_low) + swap(expand_send, 1)
    middle_part, gain_two_grad, bias_two_grad = norm_backward(
        normed_two_grad, normal_two, inverse_two, gain_two
    )
    middle_grad = output_grad + middle_part
    branch_low = middle_grad.astype(low_type)
    mixing_bias_grad = jnp.sum(branch_low, axis=0, dtype=jnp.float32)
    mixing_sum = trans_times(branch_low, mixed_low).reshape(
        bits_shape(devices, (D // devices, D))
    )
    (mixing_item,) = finish_hop(hop([(mixing_sum, all_masks, True)], 1, low_type))
    mixed_grad = times_plain(branch_low, mixing_low).astype(low_type)
    expand_chain = sum_chain(
        [(expand_sum.reshape(static_shape), static_marks, False), mixing_item], low_type
    )
    expand_sent = next(expand_chain)

    backs = []
    back_pairs = D // PAIR // BACK_CALLS

    def back_step(waits):
        number = len(backs)
        first = number * back_pairs
        source = attended[first // pairs]
        order = (backs[-1][1],) if backs else ()
        backs.append(
            attend_back_call(
                hot_turned,
                *source[:3],
                gate(mixed_grad, (waits, order)),
                source[4],
                cosine,
                sine_table,
                first,
                first % pairs,
                back_pairs,
            )
        )
        return backs[-1][1]

    mixed_grad, attend_low = lax.optimization_barrier((mixed_grad, attend_low))
    back_step(expand_sent)
    token = back_step(())
    expand_sent = expand_chain.send(token)
    reduce_sent = reduce_chain.send(token)
    token = back_step((expand_sent, reduce_sent))
    expand_sent = expand_chain.send(token)
    reduce_sent = reduce_chain.send(token)
    token = back_step((expand_sent, reduce_sent))
    reduce_sent = reduce_chain.send(token)
    token = back_step(reduce_sent)
    expand_sent = expand_chain.send(token)
    token = back_step(expand_sent)
    (reduce_sum,) = drain(reduce_chain, token)
    expand_sum, mixing_sum = drain(expand_chain, token)
    dense = jnp.concatenate([reduce_sum, expand_sum, mixing_sum], axis=0)
    spot = lax.axis_index("narrow")
    dense, backs = together((dense, backs))

    def one_chain(value, mask):
        (got,) = yield [(value, mask)]
        return got

    columns = D // wide_size
    rows_hist = -(-VOCAB // columns)

    def make_small(backs):
        entry_gradient, one_sums, table_sum = entry_call(
            embed_scale,
            hot,
            jnp.pad(table_low, ((0, LANES - VOCAB), (0, 0))),
            gain_one[None, :],
            middle_grad,
            attend_low.reshape(3 * D, D),
            [back[0] for back in backs],
        )
        hist_part = jnp.pad(prob_sum, (0, rows_hist * columns - VOCAB)).reshape(rows_hist, columns)
        expand_ordered = in_order(
            expand_bias_grad.reshape(devices, FF // devices), hidden_masks, 1, me
        )
        small_grads = small_blocks(
            [back[1] for back in backs],
            table_sum,
            table_head,
            hist_part,
            (
                (one_sums, 0),
                (gain_two_grad[None, :], 2),
                (bias_two_grad[None, :], 3),
                (gain_last_grad[None, :], 4),
                (bias_last_grad[None, :], 5),
                (mixing_bias_grad[None, :], 9),
                (reduce_bias_grad[None, :], 10),
                (expand_ordered.reshape(1, FF), 11),
            ),
            wide_size,
        )
        return entry_gradient, small_grads

    beside_chain = Chain(one_chain(dense, 2))
    entry_gradient, small_grads = advance([beside_chain], make_small, backs)
    beside = beside_chain.result
    cores = [Chain(one_chain(dense, 1)), Chain(one_chain(beside, 1))]
    small_chain = Chain(sum_small(small_grads))
    advance(cores + [small_chain])
    pieces = (dense, beside, cores[0].result, cores[1].result)

    def make_dense(pieces):
        return dense_step(
            spot,
            (unit, unit, D // devices),
            pieces,
            attend_moment,
            (reduce_moment, expand_moment, mixing_moment),
        )

    dense_totals, dense_next, dense_rows, gram_own = advance([small_chain], make_dense, pieces)
    reduce_total, expand_total, mixing_total = dense_totals
    reduce_next, expand_next, mixing_next = dense_next

    def step_of(moment, gradient):
        moment_next = MUON_MU * moment + (1.0 - MUON_MU) * gradient
        return moment_next, (1.0 - MUON_MU) * gradient + MUON_MU * moment_next

    gram_chain = Chain(sum_gram(gram_own))
    while small_chain.request:
        advance([chain for chain in (gram_chain, small_chain) if chain.request])
    small_total = small_chain.result
    token_sums = small_total[:VOCAB, : 3 * D // wide_size]
    small_total = small_total[:, 3 * D // wide_size :]
    attend_total = lax.dot_general(
        token_sums,
        table_normed.astype(jnp.float32),
        (((0,), (0,)), ((), ())),
        precision=lax.Precision.HIGHEST,
        preferred_element_type=jnp.float32,
    )
    attend_next, attend_step = step_of(attend_moment, attend_total)
    gradient_rate = (1.0 - MUON_MU) * (1.0 + MUON_MU)
    crossed = exact_times(
        token_sums, jnp.concatenate([attend_moment, token_sums.T], axis=1)
    )
    crossed_chain = Chain(sum_wide(crossed))
    while crossed_chain.request:
        advance([chain for chain in (gram_chain, crossed_chain) if chain.request])
    while gram_chain.request:
        advance([gram_chain])
    crossed = crossed_chain.result
    gram_parts = gram_chain.result
    table_wide = table_normed.astype(jnp.float32)
    added = gradient_rate * (
        (MUON_MU * MUON_MU) * crossed[:, :D]
        + (0.5 * gradient_rate) * exact_times(crossed[:, D:], table_wide)
    )
    added = jnp.where(spot == 0, added, 0.0)
    table_total = small_total[:VOCAB]
    vector_total = small_total[VOCAB : VOCAB + 15]
    prob_total = small_total[VOCAB + 15 :].reshape(rows_hist * columns)[:VOCAB]
    histogram = prob_total * (VOCAB / (row_count * devices))
    totals = (attend_total, mixing_total, expand_total, reduce_total)
    moment_next = (attend_next, mixing_next, expand_next, reduce_next)
    most = dense_rows.shape[0]
    attend_rows = jnp.pad(attend_step, ((0, most - attend_step.shape[0]), (0, 0)))
    rows = jnp.where(spot == 0, attend_rows, dense_rows)
    ortho = newton_rows(gram_parts, rows, added, table_normed)
    ortho, table_total, vector_total = together((ortho, table_total, vector_total))
    across = swap(ortho, 2)
    table_new, table_mean_next, table_square_next = adam_step(
        table_weight, table_mean, table_square, table_total, TABLE_RATE, TABLE_DECAY, step_count
    )
    vector_new, vector_mean_next, vector_square_next = adam_step(
        vector_params, vector_mean, vector_square, vector_total, VECTOR_RATE, 0.0, step_count
    )
    across, adam_results = together(
        (
            across,
            (
                table_new,
                table_mean_next,
                table_square_next,
                vector_new,
                vector_mean_next,
                vector_square_next,
            ),
        )
    )
    orthos = (ortho, swap(ortho, 1), across, swap(across, 1))
    matrices = (attend_weight, mixing_weight, expand_weight, reduce_weight)
    rates = tuple(
        MUON_RATE * SHAPE_FACTOR * math.sqrt(max(rows, D)) for rows in (3 * D, D, FF, FF)
    )
    matrix_new = tuple(update_rows(spot, orthos, matrices, rates))
    results = (
        totals
        + (table_total, vector_total)
        + matrix_new
        + moment_next
        + (
            *adam_results,
        )
    )
    block_output = output.astype(low_type).reshape(seq_count, SEQ_LEN, D)
    return (block_output, entry_gradient.reshape(seq_count, SEQ_LEN, D)) + results + (histogram,)


def solution(mesh):
    in_specs = (
        P(("wide", "narrow"), None),
        P(("wide", "narrow")),
        P(("wide", "narrow"), None),
        P(("wide", "narrow"), None),
        P(None, "wide"),
        P("wide", None),
        P("wide", None),
        P("wide", None),
        P("wide", None),
        P(None, "wide"),
        P("wide", None),
        P("wide", None),
        P("wide", None),
        P("wide", None),
        P(None, "wide"),
        P(None, "wide"),
        P(None, "wide"),
        P(None, "wide"),
        P(),
    )
    out_specs = (
        P(("wide", "narrow"), None, None),
        P(("wide", "narrow"), None, None),
        P("wide", None),
        P("wide", None),
        P("wide", None),
        P("wide", None),
        P(None, "wide"),
        P(None, "wide"),
        P("wide", None),
        P("wide", None),
        P("wide", None),
        P("wide", None),
        P("wide", None),
        P("wide", None),
        P("wide", None),
        P("wide", None),
        P(None, "wide"),
        P(None, "wide"),
        P(None, "wide"),
        P(None, "wide"),
        P(None, "wide"),
        P(None, "wide"),
        P(),
    )
    return jax.shard_map(
        on_device, mesh=mesh, in_specs=in_specs, out_specs=out_specs, check_vma=False
    )
```

```python
from functools import partial
import math

import jax
import jax.numpy as jnp
import numpy as np
from jax import lax
from jax.experimental import pallas as pl
from jax.experimental.pallas import tpu as pltpu
from jax.sharding import PartitionSpec as P

D = 768
HEADS = 12
HEAD_DIM = 64
FF = 3072
VOCAB = 70
SEQ_LEN = 912
NS_ITERS = 5


NORM_EPS = 1e-05
ROPE_BASE = 10000.0
NEWTON_A = 3.4445
NEWTON_B = -4.775
NEWTON_C = 2.0315
MUON_MU = 0.95
MUON_RATE = 0.3
MUON_DECAY = 0.1
SHAPE_FACTOR = 0.2
ADAM_BETA1 = 0.9
ADAM_BETA2 = 0.95
ADAM_EPS = 1e-08
TABLE_RATE = 0.03
TABLE_DECAY = 0.01
VECTOR_RATE = 0.2


def times_plain(left_side, right_side):
    return jnp.dot(left_side, right_side, preferred_element_type=jnp.float32)


def times_trans(left_side, right_side):
    return lax.dot_general(
        left_side, right_side, (((1,), (1,)), ((), ())), preferred_element_type=jnp.float32
    )


def trans_times(left_side, right_side):
    return lax.dot_general(
        left_side, right_side, (((0,), (0,)), ((), ())), preferred_element_type=jnp.float32
    )


def exact_times(left_side, right_side):
    return jnp.dot(
        left_side, right_side, precision=lax.Precision.HIGHEST, preferred_element_type=jnp.float32
    )


def norm_forward(values, gain_row, bias_row):
    center = values - jnp.mean(values, axis=-1, keepdims=True)
    spread = jnp.mean(center * center, axis=-1, keepdims=True)
    inverse = lax.rsqrt(spread + NORM_EPS)
    normal = center * inverse
    return (normal * gain_row + bias_row, normal, inverse)


def norm_backward(upstream, normal, inverse, gain_row):
    scaled = upstream * gain_row
    inner_part = (
        scaled
        - jnp.mean(scaled, axis=-1, keepdims=True)
        - normal * jnp.mean(scaled * normal, axis=-1, keepdims=True)
    )
    return (inverse * inner_part, jnp.sum(upstream * normal, axis=0), jnp.sum(upstream, axis=0))


def rotary_tables(positions):
    half_dim = HEAD_DIM // 2
    frequency = ROPE_BASE ** (-(jnp.arange(half_dim, dtype=jnp.float32) * 2.0 / HEAD_DIM))
    turned = positions.astype(jnp.float32)[..., None] * frequency
    return (jnp.cos(turned), jnp.sin(turned))


PAIR = 2 * HEAD_DIM
SPAN = 1024
STRIP = 256
PARTS = 4
FEED_STRIP = 304
BLOCK = 96
PART_BLOCKS = D // BLOCK
LANES = 128
ATTEND_CALLS = 3
BACK_CALLS = 6


BOTH = ("wide", "narrow")
GRAM_TILE = 256
GRAM_SPOTS = ((0, 0), (0, 1), (0, 2), (1, 1), (1, 2), (2, 2))


def swap(value, mask):
    total = lax.axis_size(BOTH)
    return lax.ppermute(value, BOTH, [(spot, spot ^ mask) for spot in range(total)])


def my_index():
    return lax.axis_index("wide") * lax.axis_size("narrow") + lax.axis_index("narrow")


def wide_masks():
    narrow_size = lax.axis_size("narrow")
    count = lax.axis_size("wide").bit_length() - 1
    return [narrow_size << bit for bit in reversed(range(count))]


def offsets_of(masks):
    table = [0]
    for mask in masks:
        table = table + [offset ^ mask for offset in table]
    return np.array(table)


def gate(value, others):
    leaves, form = jax.tree.flatten(value)
    held = lax.optimization_barrier(tuple(leaves) + tuple(jax.tree.leaves(others)))
    return jax.tree.unflatten(form, held[: len(leaves)])


def padded_rows(array):
    return jnp.pad(array, ((0, -array.shape[0] % 16), (0, 0)))


def together(values):
    leaves, form = jax.tree.flatten(values)
    return jax.tree.unflatten(form, lax.optimization_barrier(tuple(leaves)))


def gather_blocks(piece, masks):
    for mask in masks:
        piece = jnp.concatenate([piece, swap(piece, mask)], axis=0)
    return piece


def take_blocks(array, index):
    return jnp.take(array, index, axis=0, mode="clip")


def places_of(masks, unit):
    offsets = offsets_of(masks) // unit
    place = np.zeros_like(offsets)
    place[offsets] = np.arange(offsets.size)
    return place


def in_order(blocks, masks, unit, base):
    place = places_of(masks, unit)
    return take_blocks(blocks, jnp.asarray(place)[jnp.arange(place.size) ^ base])


def out_of_order(blocks, masks, unit, base):
    offsets = offsets_of(masks) // unit
    return take_blocks(blocks, jnp.asarray(offsets) ^ base)


def quarter_rows(array):
    count = array.shape[0] // lax.axis_size("narrow")
    return lax.dynamic_slice_in_dim(array, lax.axis_index("narrow") * count, count, 0)


def side_of(mask):
    return (my_index() // mask) % 2


def split_static(array, axis):
    return lax.index_in_dim(array, 0, axis, False), lax.index_in_dim(array, 1, axis, False)


def split_sided(array, axis, mask):
    side = side_of(mask)
    return (
        lax.dynamic_index_in_dim(array, side, axis, False),
        lax.dynamic_index_in_dim(array, 1 - side, axis, False),
    )


def halves(item, mask):
    array, marks, sided = item
    axis = marks.index(mask)
    keep, send = split_sided(array, axis, mask) if sided else split_static(array, axis)
    return (keep, marks[:axis] + marks[axis + 1 :], sided), send


def hop(items, mask, kind):
    pairs = [halves(item, mask) for item in items]
    rows = [send.astype(kind).reshape(-1, send.shape[-1]) for _, send in pairs]
    flat = jnp.concatenate(rows, axis=0) if len(rows) > 1 else rows[0]
    token = yield flat
    got = gate(swap(flat, mask), token)
    results, at = [], 0
    for ((keep, marks, sided), send), row in zip(pairs, rows):
        part = got[at : at + row.shape[0]].reshape(send.shape).astype(jnp.float32)
        results.append((keep + part, marks, sided))
        at += row.shape[0]
    return results


def finish(steps, token):
    try:
        steps.send(token)
    except StopIteration as stop:
        return stop.value


def finish_hop(steps):
    next(steps)
    return finish(steps, ())


def columns_of(items, start, stop):
    return [(array[..., start:stop], marks, sided) for array, marks, sided in items]


def sum_chain(items, kind):
    masks = wide_masks()
    width = items[0][0].shape[-1]
    ways = [columns_of(items, 0, width // 2), columns_of(items, width // 2, width)]
    for pair in ((masks[-1], 2), (2, masks[-1])):
        steps = [hop(way, mask, jnp.bfloat16) for way, mask in zip(ways, pair)]
        token = yield tuple(next(step) for step in steps)
        ways = [finish(step, token) for step in steps]
    items = [
        (jnp.concatenate([left[0], right[0]], axis=-1), left[1], left[2])
        for left, right in zip(*ways)
    ]
    for mask in reversed(masks[:-1]):
        items = yield from hop(items, mask, kind)
    return [item[0] for item in items]


def drain(chain, token):
    while True:
        try:
            chain.send(token)
        except StopIteration as stop:
            return stop.value


def bits_shape(count, tail):
    return (2,) * (count.bit_length() - 1) + tuple(tail)


class Chain:
    def __init__(self, steps):
        self.steps, self.result = steps, None
        self.request = next(steps)

    def give(self, got):
        try:
            self.request = self.steps.send(got)
        except StopIteration as stop:
            self.request, self.result = [], stop.value


def advance(chains, meanwhile=None, needs=()):
    sends, needs = together(([[array for array, _ in chain.request] for chain in chains], needs))
    gots = [
        [swap(array, mask) for array, (_, mask) in zip(send, chain.request)]
        for send, chain in zip(sends, chains)
    ]
    made = meanwhile(needs) if meanwhile else ()
    gots, made = together((gots, made))
    for chain, got in zip(chains, gots):
        chain.give(got)
    return made


def sum_small(blocks):
    (got,) = yield [(blocks, 1)]
    total = (blocks + got).reshape(bits_shape(blocks.shape[0], blocks.shape[1:]))
    masks = wide_masks()
    while masks:
        mask = masks[-1]
        keep, send = split_sided(total, len(masks) - 1, mask)
        (got,) = yield [(send, mask)]
        total = keep + got
        masks = masks[:-1]
    (got,) = yield [(total, 2)]
    return total + got


def sum_wide(value):
    for mask in reversed(wide_masks()):
        (got,) = yield [(value, mask)]
        value = value + got
    return value


def sum_gram(parts):
    masks = list(reversed(wide_masks()))
    ways = [masks, [masks[1], masks[0]] + masks[2:]]
    parts = list(parts)
    for step in range(len(masks)):
        pairs = [
            split_sided(part.reshape((2, part.shape[0] // 2) + part.shape[1:]), 0, way[step])
            for part, way in zip(parts, ways)
        ]
        gots = yield [(send, way[step]) for (_, send), way in zip(pairs, ways)]
        parts = [keep + got for (keep, _), got in zip(pairs, gots)]
    for step in reversed(range(len(masks))):
        gots = yield [(part, way[step]) for part, way in zip(parts, ways)]
        parts = [
            jnp.where(
                side_of(way[step]) == 0,
                jnp.concatenate([part, got], axis=0),
                jnp.concatenate([got, part], axis=0),
            )
            for part, got, way in zip(parts, gots, ways)
        ]
    return parts


def row_dot(left_side, right_side):
    return lax.dot_general(
        left_side, right_side, (((1,), (1,)), ((), ())), preferred_element_type=jnp.float32
    )


def split_two(values):
    high = values.astype(jnp.bfloat16)
    return high, (values - high.astype(jnp.float32)).astype(jnp.bfloat16)


def newton_kernel(
    low_ref, high_ref, rows_ref, added_ref, table_ref, out_ref,
    gram_now, other, left, right, rows_left,
):
    tile = GRAM_TILE
    trace = jnp.zeros((1, 1), jnp.float32)
    diagonal = lax.broadcasted_iota(jnp.int32, (tile, tile), 0) == lax.broadcasted_iota(
        jnp.int32, (tile, tile), 1
    )

    def span(number):
        return slice(number * tile, (number + 1) * tile)

    def turned_dot(left_side, right_side):
        return lax.dot_general(
            left_side,
            right_side,
            (((0,), (0,)), ((), ())),
            preferred_element_type=jnp.float32,
        )

    added_high, added_low = split_two(added_ref[...])
    added_rest = added_ref[...] - added_high.astype(jnp.float32) - added_low.astype(jnp.float32)
    added_parts = (added_high, added_low, added_rest.astype(jnp.bfloat16))
    half = len(GRAM_SPOTS) // 2
    for number, (row, column) in enumerate(GRAM_SPOTS):
        source = low_ref if number < half else high_ref
        block = source[span(number % half), :]
        for part in added_parts:
            block = block + turned_dot(part[:, span(row)], table_ref[:, span(column)])
            block = block + turned_dot(table_ref[:, span(row)], part[:, span(column)])
        gram_now[span(row), span(column)] = block
        if row == column:
            picked = jnp.where(diagonal, block, 0.0)
            trace = trace + jnp.sum(jnp.sum(picked, axis=0, keepdims=True), axis=1, keepdims=True)
    inverse = 1.0 / (jnp.sqrt(trace) + 1e-07)
    scale = inverse * inverse
    for row, column in GRAM_SPOTS:
        block = gram_now[span(row), span(column)] * scale
        gram_now[span(row), span(column)] = block
        if row != column:
            gram_now[span(column), span(row)] = block.T

    def set_left(values):
        high, low = split_two(values)
        left[:, 0:D] = high
        left[:, D : 2 * D] = high
        left[:, 2 * D : 3 * D] = low

    def set_right(values):
        high, low = split_two(values)
        right[0:D, :] = high
        right[D : 2 * D, :] = low
        right[2 * D : 3 * D, :] = high

    def set_rows(values):
        high, low = split_two(values)
        rows_left[:, 0:D] = high
        rows_left[:, D : 2 * D] = high
        rows_left[:, 2 * D : 3 * D] = low

    def product(target, finish):
        for column in range(D // tile):
            rows = (column + 1) * tile
            block = jnp.dot(left[0:rows, :], right[:, span(column)], preferred_element_type=jnp.float32)
            for row in range(column + 1):
                piece = finish(block[span(row), :], row, column)
                target[span(row), span(column)] = piece
                if row != column:
                    target[span(column), span(row)] = piece.T

    def same(block, row, column):
        return block

    def factor(block, row, column):
        block = NEWTON_B * gram_now[span(row), span(column)] + NEWTON_C * block
        if row == column:
            block = block + jnp.where(diagonal, NEWTON_A, 0.0)
        return block

    def set_factor():
        set_left(gram_now[...])
        set_right(gram_now[...])
        product(other, factor)
        set_right(other[...])

    def rows_product():
        return jnp.dot(rows_left[...], right[...], preferred_element_type=jnp.float32)

    set_rows(rows_ref[...] * inverse)

    def body(step, carry):
        set_factor()
        product(other, same)
        set_left(other[...])
        product(gram_now, same)
        set_rows(rows_product())
        return carry

    lax.fori_loop(0, NS_ITERS - 1, body, 0)
    set_factor()
    out_ref[...] = rows_product().astype(out_ref.dtype)


def newton_rows(gram_parts, rows, added, table):
    count = rows.shape[0]
    return pl.pallas_call(
        newton_kernel,
        out_shape=jax.ShapeDtypeStruct((count, D), jnp.bfloat16),
        in_specs=[pl.BlockSpec(memory_space=pltpu.VMEM)] * 5,
        out_specs=pl.BlockSpec(memory_space=pltpu.VMEM),
        scratch_shapes=[
            pltpu.VMEM((D, D), jnp.float32),
            pltpu.VMEM((D, D), jnp.float32),
            pltpu.VMEM((D, 3 * D), jnp.bfloat16),
            pltpu.VMEM((3 * D, D), jnp.bfloat16),
            pltpu.VMEM((count, 3 * D), jnp.bfloat16),
        ],
        compiler_params=pltpu.CompilerParams(vmem_limit_bytes=48 << 20),
        cost_estimate=pl.CostEstimate(flops=60 * D * D * D, bytes_accessed=4 << 20, transcendentals=0),
        name="newton",
    )(*gram_parts, rows, added, table)


def pack_kernel(spot_ref, *refs):
    *refs, last_ref, out_ref, last_out_ref = refs
    at = 0
    for number, ref in enumerate(refs):
        count = ref.shape[0]
        out_ref[at : at + count, :] = ref[...].astype(jnp.bfloat16)
        at += count + (-count % 16 if number + 1 < len(refs) else 0)
    last_out_ref[...] = last_ref[...].astype(jnp.bfloat16)


def pack_rows(weights, spot):
    units = [weight.shape[0] // lax.axis_size("narrow") for weight in weights]
    if any(unit % 8 for unit in units) or any(unit % 16 for unit in units[:-2]):
        rows = [quarter_rows(weight).astype(jnp.bfloat16) for weight in weights]
        return jnp.concatenate([padded_rows(row) for row in rows[:-2]] + rows[-2:-1], axis=0), rows[-1]
    return pl.pallas_call(
        pack_kernel,
        grid_spec=pltpu.PrefetchScalarGridSpec(
            num_scalar_prefetch=1,
            grid=(1,),
            in_specs=[pl.BlockSpec((unit, D), lambda step, spot: (spot[0], 0)) for unit in units],
            out_specs=[
                pl.BlockSpec((sum(units[:-1]), D), lambda step, spot: (0, 0)),
                pl.BlockSpec((units[-1], D), lambda step, spot: (0, 0)),
            ],
        ),
        out_shape=[
            jax.ShapeDtypeStruct((sum(units[:-1]), D), jnp.bfloat16),
            jax.ShapeDtypeStruct((units[-1], D), jnp.bfloat16),
        ],
        name="pack",
    )(spot[None].astype(jnp.int32), *weights)


def entry_kernel(scale, *refs):
    (hot_ref, table_ref, gain_ref, middle_ref, weight_ref), refs = refs[:5], refs[5:]
    *low_refs, entry_ref, sums_ref, table_sum_ref = refs
    step = pl.program_id(0)
    hot = hot_ref[:, 0:LANES]
    stream = scale * jnp.dot(hot, table_ref[...], preferred_element_type=jnp.float32)
    grads = None
    for kind in range(3):
        low = jnp.concatenate([ref[kind] for ref in low_refs], axis=1)
        part = jnp.dot(
            low, weight_ref[kind * D : (kind + 1) * D, :], preferred_element_type=jnp.float32
        )
        grads = part if grads is None else grads + part
    center = stream - jnp.mean(stream, axis=-1, keepdims=True)
    inverse = lax.rsqrt(jnp.mean(center * center, axis=-1, keepdims=True) + NORM_EPS)
    normal = center * inverse
    scaled = grads * gain_ref[...]
    inner = (
        scaled
        - jnp.mean(scaled, axis=-1, keepdims=True)
        - normal * jnp.mean(scaled * normal, axis=-1, keepdims=True)
    )
    entry = middle_ref[...] + inverse * inner
    entry_ref[...] = entry
    sums = jnp.concatenate(
        [
            jnp.sum(grads * normal, axis=0, keepdims=True),
            jnp.sum(grads, axis=0, keepdims=True),
        ],
        axis=0,
    )
    high = entry.astype(jnp.bfloat16)
    rest = entry - high.astype(jnp.float32)
    middle = rest.astype(jnp.bfloat16)
    low = (rest - middle.astype(jnp.float32)).astype(jnp.bfloat16)
    table_sum = None
    for part in (high, middle, low):
        part = lax.dot_general(
            hot, part, (((0,), (0,)), ((), ())), preferred_element_type=jnp.float32
        )
        table_sum = part if table_sum is None else table_sum + part

    @pl.when(step == 0)
    def _():
        sums_ref[...] = sums
        table_sum_ref[...] = scale * table_sum

    @pl.when(step > 0)
    def _():
        sums_ref[...] += sums
        table_sum_ref[...] += scale * table_sum


def entry_call(scale, hot, table, gain, middle_grad, weight, lows):
    rows = SEQ_LEN // 3
    whole = lambda step: (0, 0)
    own = lambda step: (step, 0)
    return pl.pallas_call(
        partial(entry_kernel, scale),
        grid=(3,),
        in_specs=[
            pl.BlockSpec((rows, hot.shape[1]), own),
            pl.BlockSpec(table.shape, whole),
            pl.BlockSpec(gain.shape, whole),
            pl.BlockSpec((rows, D), own),
            pl.BlockSpec(weight.shape, whole),
        ]
        + [pl.BlockSpec((3, rows, low.shape[2]), lambda step: (0, step, 0)) for low in lows],
        out_specs=[
            pl.BlockSpec((rows, D), own),
            pl.BlockSpec((2, D), whole),
            pl.BlockSpec((LANES, D), whole),
        ],
        out_shape=[
            jax.ShapeDtypeStruct((SEQ_LEN, D), jnp.float32),
            jax.ShapeDtypeStruct((2, D), jnp.float32),
            jax.ShapeDtypeStruct((LANES, D), jnp.float32),
        ],
        compiler_params=pltpu.CompilerParams(vmem_limit_bytes=48 << 20),
        cost_estimate=pl.CostEstimate(flops=1 << 20, bytes_accessed=1 << 16, transcendentals=0),
        name="entry",
    )(hot, table, gain, middle_grad, weight, *lows)


def small_kernel(parts, spot_rows, table_sum_ref, head_ref, hist_ref, *refs):
    part_refs, refs = refs[:parts], refs[parts:]
    *row_refs, out_ref, sums, held = refs
    for number, part in enumerate(part_refs):
        width = part.shape[2]
        for kind in range(3):
            start = kind * D + number * width
            sums[:, start : start + width] = part[kind]
    held[0:VOCAB, :] = table_sum_ref[0:VOCAB, :] + head_ref[...]
    bias = jnp.sum(sums[...], axis=0, keepdims=True)
    for kind in range(3):
        held[VOCAB + 6 + kind : VOCAB + 7 + kind, :] = bias[:, kind * D : (kind + 1) * D]
    for ref, at in zip(row_refs, spot_rows):
        for row in range(ref.shape[0]):
            for part in range(ref.shape[1] // D):
                held[at : at + 1, :] = ref[row : row + 1, part * D : (part + 1) * D]
                at += 1
    count, rows, columns = out_ref.shape
    narrow = D // count
    wide = columns - narrow
    base = held.shape[0]
    for number in range(count):
        out_ref[number, 0:VOCAB, 0:wide] = sums[0:VOCAB, number * wide : (number + 1) * wide]
        out_ref[number, VOCAB:rows, 0:wide] = jnp.zeros((rows - VOCAB, wide), jnp.float32)
        out_ref[number, 0:base, wide:columns] = held[:, number * narrow : (number + 1) * narrow]
        out_ref[number, base:rows, wide:columns] = hist_ref[...]


def small_blocks(parts, table_sum, head, hist, rows, wide_size):
    whole = pl.BlockSpec(memory_space=pltpu.VMEM)
    total = VOCAB + 15 + hist.shape[0]
    arrays = [array for array, _ in rows]
    return pl.pallas_call(
        partial(small_kernel, len(parts), tuple(VOCAB + place for _, place in rows)),
        in_specs=[whole] * (3 + len(parts) + len(rows)),
        out_specs=whole,
        out_shape=jax.ShapeDtypeStruct((wide_size, total, 4 * D // wide_size), jnp.float32),
        scratch_shapes=[
            pltpu.VMEM((LANES, 3 * D), jnp.float32),
            pltpu.VMEM((VOCAB + 15, D), jnp.float32),
        ],
        cost_estimate=pl.CostEstimate(flops=1 << 20, bytes_accessed=1 << 16, transcendentals=0),
        name="small_grads",
    )(table_sum, head, hist, *parts, *arrays)


def dense_kernel(units, spot_ref, own_ref, beside_ref, core_ref, cross_ref, *refs):
    base_ref, *refs = refs
    count = len(units)
    moment_refs, refs = refs[:count], refs[count:]
    total_refs, next_refs, refs = refs[:count], refs[count : 2 * count], refs[2 * count :]
    rows_ref, low_ref, high_ref, left, right = refs
    spot = spot_ref[0]
    for device in range(4):
        way = spot ^ device
        for kind, source in enumerate((own_ref, core_ref, beside_ref, cross_ref)):

            @pl.when(way == kind)
            def _():
                at = 0
                for total_ref, unit in zip(total_refs, units):
                    total_ref[device * unit : (device + 1) * unit, :] = source[at : at + unit, :]
                    at += unit

    rows_ref[...] = jnp.zeros_like(rows_ref)

    @pl.when(spot == 0)
    def _():
        rows_ref[0 : base_ref.shape[0], :] = (MUON_MU * MUON_MU) * base_ref[...]

    for number in range(count):
        gradient = total_refs[number][...]
        moment_next = MUON_MU * moment_refs[number][...] + (1.0 - MUON_MU) * gradient
        next_refs[number][...] = moment_next
        place = count - number

        @pl.when(spot == place)
        def _():
            rows_ref[0 : gradient.shape[0], :] = (
                1.0 - MUON_MU
            ) * gradient + MUON_MU * moment_next

    high, low = split_two(rows_ref[...])
    depth = rows_ref.shape[0]
    right[0:depth, :] = high
    right[depth : 2 * depth, :] = low
    right[2 * depth : 3 * depth, :] = high
    turned_high, turned_low = split_two(rows_ref[...].T)
    left[:, 0:depth] = turned_high
    left[:, depth : 2 * depth] = turned_high
    left[:, 2 * depth : 3 * depth] = turned_low
    half = len(GRAM_SPOTS) // 2
    for number, (row, column) in enumerate(GRAM_SPOTS):
        target = low_ref if number < half else high_ref
        at = (number % half) * GRAM_TILE
        target[at : at + GRAM_TILE, :] = jnp.dot(
            left[row * GRAM_TILE : (row + 1) * GRAM_TILE, :],
            right[:, column * GRAM_TILE : (column + 1) * GRAM_TILE],
            preferred_element_type=jnp.float32,
        )


def dense_step(spot, units, pieces, base, moments):
    whole = pl.BlockSpec(memory_space=pltpu.VMEM)
    most = max(moment.shape[0] for moment in moments)
    shapes = [jax.ShapeDtypeStruct(moment.shape, jnp.float32) for moment in moments]
    half = jax.ShapeDtypeStruct((len(GRAM_SPOTS) // 2 * GRAM_TILE, GRAM_TILE), jnp.float32)
    results = pl.pallas_call(
        partial(dense_kernel, units),
        in_specs=[pl.BlockSpec(memory_space=pltpu.SMEM)] + [whole] * (5 + len(moments)),
        out_specs=[whole] * (2 * len(moments) + 3),
        out_shape=shapes + shapes + [jax.ShapeDtypeStruct((most, D), jnp.float32), half, half],
        scratch_shapes=[
            pltpu.VMEM((D, 3 * most), jnp.bfloat16),
            pltpu.VMEM((3 * most, D), jnp.bfloat16),
        ],
        compiler_params=pltpu.CompilerParams(vmem_limit_bytes=48 << 20),
        cost_estimate=pl.CostEstimate(flops=1 << 20, bytes_accessed=1 << 16, transcendentals=0),
        name="dense_step",
    )(spot[None].astype(jnp.int32), *pieces, base, *moments)
    count = len(moments)
    return results[:count], results[count : 2 * count], results[2 * count], results[2 * count + 1 :]


def update_kernel(rates, spot_ref, *refs):
    count = len(rates)
    sources, refs = refs[:4], refs[4:]
    for number in range(count):
        weight_ref, out_ref = refs[number], refs[count + number]
        rows = weight_ref.shape[0]
        way = spot_ref[0] ^ number
        for kind, source in enumerate(sources):

            @pl.when(way == kind)
            def _():
                out_ref[...] = weight_ref[...] * (1.0 - MUON_RATE * MUON_DECAY) - rates[
                    number
                ] * source[0:rows, :].astype(jnp.float32)


def update_rows(spot, orthos, weights, rates):
    whole = pl.BlockSpec(memory_space=pltpu.VMEM)
    return pl.pallas_call(
        partial(update_kernel, rates),
        in_specs=[pl.BlockSpec(memory_space=pltpu.SMEM)] + [whole] * (4 + len(weights)),
        out_specs=[whole] * len(weights),
        out_shape=[jax.ShapeDtypeStruct(weight.shape, jnp.float32) for weight in weights],
        compiler_params=pltpu.CompilerParams(vmem_limit_bytes=40 << 20),
        cost_estimate=pl.CostEstimate(flops=1 << 20, bytes_accessed=1 << 16, transcendentals=0),
        name="update",
    )(spot[None].astype(jnp.int32), *orthos, *weights)


def heads_kernel(place_ref, blocks_ref, bias_ref, out_ref, held):
    count, rows, columns = blocks_ref.shape
    held[rows : held.shape[0], :] = jnp.zeros((held.shape[0] - rows, 3 * D), jnp.float32)
    for number in range(count):
        spot = slice(number * columns, (number + 1) * columns)
        held[0:rows, spot] = blocks_ref[place_ref[number]] + bias_ref[:, spot]
    high, low = split_two(held[...])
    some = held.shape[0]
    none = jnp.zeros((LANES - some, 3 * D), jnp.bfloat16)
    out_ref[0:some, :] = high
    out_ref[some:LANES, :] = none
    out_ref[LANES : LANES + some, :] = low
    out_ref[LANES + some : 2 * LANES, :] = none


def heads_table(blocks, place, bias):
    return pl.pallas_call(
        heads_kernel,
        grid_spec=pltpu.PrefetchScalarGridSpec(
            num_scalar_prefetch=1,
            grid=(1,),
            in_specs=[
                pl.BlockSpec(blocks.shape, lambda step, place: (0, 0, 0)),
                pl.BlockSpec(bias.shape, lambda step, place: (0, 0)),
            ],
            out_specs=pl.BlockSpec((2 * LANES, 3 * D), lambda step, place: (0, 0)),
            scratch_shapes=[pltpu.VMEM((VOCAB + -VOCAB % 16, 3 * D), jnp.float32)],
        ),
        out_shape=jax.ShapeDtypeStruct((2 * LANES, 3 * D), jnp.bfloat16),
        name="heads_table",
    )(place, blocks, bias)


def turn(values, cosine, sine_table):
    lane = lax.broadcasted_iota(jnp.int32, values.shape, 1)
    half = HEAD_DIM // 2
    partner = jnp.where(
        lane % HEAD_DIM < half,
        pltpu.roll(values, PAIR - half, 1),
        pltpu.roll(values, half, 1),
    )
    return values * cosine + partner * sine_table


def attend_kernel(
    hot_ref, tq_ref, tk_ref, tv_ref, cos_ref, sin_ref,
    q_ref, k_ref, v_ref, mixed_ref, log_ref,
    q_all, v_turned, mixed_turned, prob_all,
):
    hot = hot_ref[...]
    cosine = cos_ref[...]
    sine_table = sin_ref[...]
    queries = jnp.dot(hot, tq_ref[...], preferred_element_type=jnp.float32)
    queries = turn(queries, cosine, sine_table).astype(jnp.bfloat16) * HEAD_DIM ** (-0.5)
    queries = queries.astype(jnp.bfloat16)
    q_ref[...] = queries
    q_all[0:SEQ_LEN, :] = queries
    q_all[SEQ_LEN:SPAN, :] = jnp.zeros((SPAN - SEQ_LEN, PAIR), jnp.bfloat16)
    keys = jnp.dot(hot, tk_ref[...], preferred_element_type=jnp.float32)
    keys = turn(keys, cosine, sine_table).astype(jnp.bfloat16)
    k_ref[...] = keys
    values = jnp.dot(hot, tv_ref[...], preferred_element_type=jnp.float32)
    v_ref[...] = values.astype(jnp.bfloat16)
    v_turned[...] = values.T.astype(jnp.bfloat16)

    def one_head(head, carry):
        lane = lax.broadcasted_iota(jnp.int32, (SEQ_LEN, PAIR), 1)
        keys_head = jnp.where(lane // HEAD_DIM == head, k_ref[...], jnp.zeros((), jnp.bfloat16))
        head_rows = pl.ds(pl.multiple_of(head * HEAD_DIM, HEAD_DIM), HEAD_DIM)
        values_head = v_turned[head_rows, :]

        def body(step, carry):
            at = pl.multiple_of(step * STRIP, STRIP)
            scores = row_dot(keys_head, q_all[pl.ds(at, STRIP), :])
            peak = jnp.max(scores, axis=0, keepdims=True)
            powers = jnp.exp(scores - peak)
            total = jnp.sum(powers, axis=0, keepdims=True)
            prob_low = (powers * (1.0 / total)).astype(jnp.bfloat16)
            prob_all[:, pl.ds(at, STRIP)] = prob_low
            log_ref[0, pl.ds(head, 1), pl.ds(at, STRIP)] = peak + jnp.log(total)
            return carry

        lax.fori_loop(0, SPAN // STRIP, body, 0, unroll=SPAN // STRIP)
        mixed_turned[head_rows, :] = jnp.dot(
            values_head, prob_all[...], preferred_element_type=jnp.float32
        )
        return carry

    lax.fori_loop(0, 2, one_head, 0, unroll=2)
    mixed_ref[...] = mixed_turned[...].T[0:SEQ_LEN, :].astype(jnp.bfloat16)


def attend_call(hot, tables, cosine, sine_table, first, count):
    whole = lambda step: (0, 0)
    source = lambda step: (0, step + first)
    own = lambda step: (0, step)
    rows_low = jax.ShapeDtypeStruct((SEQ_LEN, count * PAIR), jnp.bfloat16)
    return pl.pallas_call(
        attend_kernel,
        grid=(count,),
        in_specs=[
            pl.BlockSpec(hot.shape, whole),
            pl.BlockSpec((hot.shape[1], PAIR), source),
            pl.BlockSpec((hot.shape[1], PAIR), lambda step: (0, step + first + D // PAIR)),
            pl.BlockSpec((hot.shape[1], PAIR), lambda step: (0, step + first + 2 * D // PAIR)),
            pl.BlockSpec((SEQ_LEN, PAIR), whole),
            pl.BlockSpec((SEQ_LEN, PAIR), whole),
        ],
        out_specs=[
            pl.BlockSpec((SEQ_LEN, PAIR), own),
            pl.BlockSpec((SEQ_LEN, PAIR), own),
            pl.BlockSpec((SEQ_LEN, PAIR), own),
            pl.BlockSpec((SEQ_LEN, PAIR), own),
            pl.BlockSpec((1, 2, SPAN), lambda step: (step, 0, 0)),
        ],
        out_shape=[rows_low] * 4 + [jax.ShapeDtypeStruct((count, 2, SPAN), jnp.float32)],
        scratch_shapes=[
            pltpu.VMEM((SPAN, PAIR), jnp.bfloat16),
            pltpu.VMEM((PAIR, SEQ_LEN), jnp.bfloat16),
            pltpu.VMEM((PAIR, SPAN), jnp.float32),
            pltpu.VMEM((SEQ_LEN, SPAN), jnp.bfloat16),
        ],
        compiler_params=pltpu.CompilerParams(vmem_limit_bytes=40 << 20),
        cost_estimate=pl.CostEstimate(
            flops=count * SPAN * SPAN, bytes_accessed=1 << 16,
            transcendentals=0,
        ),
        name="attend",
    )(hot, tables, tables, tables, cosine, sine_table)


def attend_back_kernel(
    hot_ref, q_ref, k_ref, v_ref, grad_ref, log_ref, cos_ref, sin_ref,
    low_ref, sums_ref,
    q_all, grad_all, k_turned, prob_all, score_all, query_turned, key_sum, value_sum,
):
    rest = jnp.zeros((SPAN - SEQ_LEN, PAIR), jnp.bfloat16)
    q_all[0:SEQ_LEN, :] = q_ref[...]
    q_all[SEQ_LEN:SPAN, :] = rest
    grad_all[0:SEQ_LEN, :] = grad_ref[...]
    grad_all[SEQ_LEN:SPAN, :] = rest
    k_turned[...] = k_ref[...].astype(jnp.float32).T.astype(jnp.bfloat16)
    lane = lax.broadcasted_iota(jnp.int32, (SEQ_LEN, PAIR), 1)
    none = jnp.zeros((), jnp.bfloat16)

    def one_head(head, carry):
        head_rows = pl.ds(pl.multiple_of(head * HEAD_DIM, HEAD_DIM), HEAD_DIM)
        keys_head = jnp.where(lane // HEAD_DIM == head, k_ref[...], none)
        values_head = jnp.where(lane // HEAD_DIM == head, v_ref[...], none)

        def body(step, carry):
            at = pl.multiple_of(step * STRIP, STRIP)
            scores = row_dot(keys_head, q_all[pl.ds(at, STRIP), :])
            prob_rows = jnp.exp(scores - log_ref[0, pl.ds(head, 1), pl.ds(at, STRIP)])
            prob_all[:, pl.ds(at, STRIP)] = prob_rows.astype(jnp.bfloat16)
            prob_grad = row_dot(values_head, grad_all[pl.ds(at, STRIP), :])
            delta = jnp.sum(prob_grad * prob_rows, axis=0, keepdims=True)
            score_all[:, pl.ds(at, STRIP)] = (prob_rows * (prob_grad - delta)).astype(jnp.bfloat16)
            return carry

        lax.fori_loop(0, SPAN // STRIP, body, 0, unroll=SPAN // STRIP)
        value_part = jnp.dot(prob_all[...], grad_all[...], preferred_element_type=jnp.float32)
        key_part = jnp.dot(score_all[...], q_all[...], preferred_element_type=jnp.float32)
        value_sum[...] = jnp.where(lane // HEAD_DIM == head, value_part, value_sum[...])
        key_sum[...] = jnp.where(lane // HEAD_DIM == head, key_part, key_sum[...])
        query_turned[head_rows, :] = (
            jnp.dot(k_turned[head_rows, :], score_all[...], preferred_element_type=jnp.float32)
            * HEAD_DIM ** (-0.5)
        )
        return carry

    lax.fori_loop(0, 2, one_head, 0, unroll=2)
    cosine = cos_ref[...]
    sine_table = -sin_ref[...]
    hot = hot_ref[...]
    query_low = turn(query_turned[...].T[0:SEQ_LEN, :], cosine, sine_table).astype(jnp.bfloat16)
    key_low = turn(key_sum[...], cosine, sine_table).astype(jnp.bfloat16)
    value_low = value_sum[...].astype(jnp.bfloat16)
    for number, low in enumerate((query_low, key_low, value_low)):
        low_ref[number] = low
        sums_ref[number] = jnp.dot(hot, low, preferred_element_type=jnp.float32)


def attend_back_call(
    hot_turned, queries, keys, values, gradients, logs, cosine, sine_table, first, inside, count
):
    whole = lambda step: (0, 0)
    rows = pl.BlockSpec((SEQ_LEN, PAIR), lambda step: (0, step + inside))
    whole_rows = pl.BlockSpec((SEQ_LEN, PAIR), whole)
    return pl.pallas_call(
        attend_back_kernel,
        grid=(count,),
        in_specs=[
            pl.BlockSpec(hot_turned.shape, whole),
            rows,
            rows,
            rows,
            pl.BlockSpec((SEQ_LEN, PAIR), lambda step: (0, step + first)),
            pl.BlockSpec((1, 2, SPAN), lambda step: (step + inside, 0, 0)),
            whole_rows,
            whole_rows,
        ],
        out_specs=[
            pl.BlockSpec((3, SEQ_LEN, PAIR), lambda step: (0, 0, step)),
            pl.BlockSpec((3, hot_turned.shape[0], PAIR), lambda step: (0, 0, step)),
        ],
        out_shape=[
            jax.ShapeDtypeStruct((3, SEQ_LEN, count * PAIR), jnp.bfloat16),
            jax.ShapeDtypeStruct((3, hot_turned.shape[0], count * PAIR), jnp.float32),
        ],
        scratch_shapes=[
            pltpu.VMEM((SPAN, PAIR), jnp.bfloat16),
            pltpu.VMEM((SPAN, PAIR), jnp.bfloat16),
            pltpu.VMEM((PAIR, SEQ_LEN), jnp.bfloat16),
            pltpu.VMEM((SEQ_LEN, SPAN), jnp.bfloat16),
            pltpu.VMEM((SEQ_LEN, SPAN), jnp.bfloat16),
            pltpu.VMEM((PAIR, SPAN), jnp.float32),
            pltpu.VMEM((SEQ_LEN, PAIR), jnp.float32),
            pltpu.VMEM((SEQ_LEN, PAIR), jnp.float32),
        ],
        compiler_params=pltpu.CompilerParams(vmem_limit_bytes=48 << 20),
        cost_estimate=pl.CostEstimate(
            flops=count * SPAN * SPAN, bytes_accessed=1 << 16,
            transcendentals=0,
        ),
        name="attend_back",
    )(hot_turned, queries, keys, values, gradients, logs, cosine, sine_table)


ERF_P = 0.3275911
ERF_A = (0.254829592, -0.284496736, 1.421413741, -1.453152027, 1.061405429)

def normal_parts(values):
    size = jnp.abs(values)
    bell = jnp.exp(values * values * -0.5)
    step = 1.0 / (1.0 + (ERF_P * 0.5**0.5) * size)
    series = ERF_A[4]
    for factor in (ERF_A[3], ERF_A[2], ERF_A[1], ERF_A[0]):
        series = series * step + factor
    tail = (0.5 * series) * step * bell
    return jnp.where(values < 0.0, tail, 1.0 - tail), bell * (1.0 / math.sqrt(2.0 * math.pi))

def start_parts(place_ref, source_ref, starts, held, sems):
    for part in range(PARTS):
        for number, start in enumerate(starts):

            def body(spot, carry):
                pltpu.make_async_copy(
                    source_ref.at[place_ref[part * PART_BLOCKS + spot], pl.ds(start, BLOCK), :],
                    held[number].at[part, spot],
                    sems.at[number, part],
                ).start()
                return carry

            lax.fori_loop(0, PART_BLOCKS, body, 0)


def wait_part(source_ref, number, held, sems, step):
    pltpu.make_async_copy(
        source_ref.at[pl.ds(0, PART_BLOCKS), pl.ds(0, BLOCK), :],
        held[number].at[step],
        sems.at[number, step],
    ).wait()
    return held[number][step].reshape(D, D)


def feed_kernel(starts, place_ref, rows_ref, bias_ref, source_ref, hidden_ref, slope_ref, out_ref, expand_held, reduce_held, sems):
    held = (expand_held, reduce_held)
    step = pl.program_id(0)
    @pl.when(step == 0)
    def _():
        start_parts(place_ref, source_ref, starts, held, sems)

    expand = wait_part(source_ref, 0, held, sems, step)
    reduce = wait_part(source_ref, 1, held, sems, step)
    for at in range(0, SEQ_LEN, FEED_STRIP):
        spot = slice(at, at + FEED_STRIP)
        values = row_dot(rows_ref[spot, :], expand) + bias_ref[...]
        below, bell = normal_parts(values)
        hidden = (values * below).astype(jnp.bfloat16)
        hidden_ref[spot, :] = hidden
        slope_ref[spot, :] = (below + values * bell).astype(jnp.bfloat16)
        part = jnp.dot(hidden, reduce, preferred_element_type=jnp.float32)
        out_ref[spot, :] = jnp.where(step == 0, 0.0, out_ref[spot, :]) + part


def feed_call(place, rows, bias, source, starts):
    whole = lambda step, place: (0, 0)
    chunk = pl.BlockSpec((SEQ_LEN, D), lambda step, place: (0, step))
    return pl.pallas_call(
        partial(feed_kernel, starts),
        grid_spec=pltpu.PrefetchScalarGridSpec(
            num_scalar_prefetch=1,
            grid=(PARTS,),
            in_specs=[
                pl.BlockSpec((SEQ_LEN, D), whole),
                pl.BlockSpec((1, D), lambda step, place: (0, step)),
                pl.BlockSpec(memory_space=pl.ANY),
            ],
            out_specs=[chunk, chunk, pl.BlockSpec((SEQ_LEN, D), whole)],
            scratch_shapes=[
                pltpu.VMEM((PARTS, PART_BLOCKS, BLOCK, D), jnp.bfloat16),
                pltpu.VMEM((PARTS, PART_BLOCKS, BLOCK, D), jnp.bfloat16),
                pltpu.SemaphoreType.DMA((2, PARTS)),
            ],
        ),
        out_shape=[jax.ShapeDtypeStruct((SEQ_LEN, FF), jnp.bfloat16)] * 2
        + [jax.ShapeDtypeStruct((SEQ_LEN, D), jnp.float32)],
        compiler_params=pltpu.CompilerParams(vmem_limit_bytes=48 << 20),
        cost_estimate=pl.CostEstimate(
            flops=SEQ_LEN * D * FF, bytes_accessed=1 << 16, transcendentals=0
        ),
        name="feed",
    )(place, rows, bias, source)


def feed_back_kernel(starts, place_ref, grad_ref, slope_ref, source_ref, pre_ref, out_ref, bias_ref, expand_held, reduce_held, sems):
    held = (expand_held, reduce_held)
    step = pl.program_id(0)
    @pl.when(step == 0)
    def _():
        start_parts(place_ref, source_ref, starts, held, sems)

    reduce = wait_part(source_ref, 1, held, sems, step)
    expand = wait_part(source_ref, 0, held, sems, step)
    total = jnp.zeros((1, D), jnp.float32)
    for at in range(0, SEQ_LEN, SEQ_LEN):
        spot = slice(at, at + SEQ_LEN)
        grad = row_dot(grad_ref[spot, :], reduce) * slope_ref[spot, :].astype(jnp.float32)
        low = grad.astype(jnp.bfloat16)
        pre_ref[spot, :] = low
        total = total + jnp.sum(low.astype(jnp.float32), axis=0, keepdims=True)
        part = jnp.dot(low, expand, preferred_element_type=jnp.float32)
        out_ref[spot, :] = jnp.where(step == 0, 0.0, out_ref[spot, :]) + part
    bias_ref[...] = total


def feed_back_call(place, grad, slope, source, starts):
    whole = lambda step, place: (0, 0)
    chunk = pl.BlockSpec((SEQ_LEN, D), lambda step, place: (0, step))
    return pl.pallas_call(
        partial(feed_back_kernel, starts),
        grid_spec=pltpu.PrefetchScalarGridSpec(
            num_scalar_prefetch=1,
            grid=(PARTS,),
            in_specs=[
                pl.BlockSpec((SEQ_LEN, D), whole),
                chunk,
                pl.BlockSpec(memory_space=pl.ANY),
            ],
            out_specs=[
                chunk,
                pl.BlockSpec((SEQ_LEN, D), whole),
                pl.BlockSpec((1, D), lambda step, place: (0, step)),
            ],
            scratch_shapes=[
                pltpu.VMEM((PARTS, PART_BLOCKS, BLOCK, D), jnp.bfloat16),
                pltpu.VMEM((PARTS, PART_BLOCKS, BLOCK, D), jnp.bfloat16),
                pltpu.SemaphoreType.DMA((2, PARTS)),
            ],
        ),
        out_shape=[
            jax.ShapeDtypeStruct((SEQ_LEN, FF), jnp.bfloat16),
            jax.ShapeDtypeStruct((SEQ_LEN, D), jnp.float32),
            jax.ShapeDtypeStruct((1, FF), jnp.float32),
        ],
        compiler_params=pltpu.CompilerParams(vmem_limit_bytes=48 << 20),
        cost_estimate=pl.CostEstimate(
            flops=SEQ_LEN * D * FF, bytes_accessed=1 << 16, transcendentals=0
        ),
        name="feed_back",
    )(place, grad, slope, source)


def adam_step(weight, mean_state, square, gradient, step_rate, decay_rate, step_count):
    mean_next = ADAM_BETA1 * mean_state + (1.0 - ADAM_BETA1) * gradient
    square_next = ADAM_BETA2 * square + (1.0 - ADAM_BETA2) * gradient * gradient
    step_float = step_count.astype(jnp.float32)
    mean_hat = mean_next / (1.0 - ADAM_BETA1**step_float)
    square_hat = square_next / (1.0 - ADAM_BETA2**step_float)
    updated = weight - step_rate * (
        mean_hat / (jnp.sqrt(square_hat) + ADAM_EPS) + decay_rate * weight
    )
    return (updated, mean_next, square_next)


def on_device(
    codons,
    offsets,
    positions,
    targets,
    table_weight,
    attend_weight,
    mixing_weight,
    expand_weight,
    reduce_weight,
    vector_params,
    attend_moment,
    mixing_moment,
    expand_moment,
    reduce_moment,
    table_mean,
    table_square,
    vector_mean,
    vector_square,
    step_count,
):
    low_type = jnp.bfloat16
    wide_at = lax.axis_index("wide")
    me = my_index()
    devices = lax.axis_size(BOTH)
    masks = wide_masks()
    narrow_size = lax.axis_size("narrow")
    wide_size = lax.axis_size("wide")
    hidden_masks = masks[:-1] + [2, masks[-1], 1]
    all_masks = masks + [2, 1]
    small = jnp.concatenate([table_weight, vector_params], axis=0).astype(low_type)
    small = gather_blocks(small[None], masks)
    packed = (expand_weight, reduce_weight, mixing_weight, attend_weight)
    units = [weight.shape[0] // narrow_size for weight in packed]
    starts = np.cumsum([0] + [unit + -unit % 16 for unit in units])
    packed_low, attend_own = pack_rows(packed, lax.axis_index("narrow"))
    weights_low = lax.all_gather(packed_low, BOTH, axis=0)

    def weight_rows(number, unit):
        start = int(starts[number])
        return weights_low[:, start : start + unit].reshape(-1, D)

    codons, positions, targets = gate((codons, positions, targets), small)
    small = in_order(small, masks, narrow_size, wide_at)
    small = jnp.transpose(small, (1, 0, 2)).reshape(VOCAB + 15, D)
    table_low = small[:VOCAB]
    vector_full = small[VOCAB:].astype(jnp.float32)
    gain_one = vector_full[0]
    bias_one = vector_full[1]
    gain_two = vector_full[2]
    bias_two = vector_full[3]
    gain_last = vector_full[4]
    bias_last = vector_full[5]
    attend_bias = vector_full[6:9].reshape(1, 3 * D)
    mixing_bias = vector_full[9]
    reduce_bias = vector_full[10]
    expand_bias = out_of_order(
        vector_full[11:15].reshape(devices, FF // devices), hidden_masks, 1, me
    ).reshape(FF)
    embed_scale = math.sqrt(D)
    table_stream = embed_scale * table_low.astype(jnp.float32)
    table_normed = norm_forward(table_stream, gain_one, bias_one)[0].astype(low_type)
    table_own = times_trans(table_normed, attend_own)
    place = jnp.asarray(places_of(all_masks, 1), jnp.int32)[jnp.arange(devices) ^ me]
    tables = heads_table(gather_blocks(table_own[None], all_masks), place, attend_bias)

    unit = FF // devices
    hidden_place = jnp.asarray(offsets_of(hidden_masks)) ^ me
    if unit == BLOCK:
        feed_place, feed_source, feed_starts = hidden_place, weights_low, tuple(starts[:2])
    else:
        feed_source = jnp.concatenate(
            [
                take_blocks(weights_low[:, start : start + unit], hidden_place).reshape(-1, BLOCK, D)
                for start in (int(starts[0]), int(starts[1]))
            ],
            axis=1,
        )
        feed_place, feed_starts = jnp.arange(FF // BLOCK), (0, BLOCK)
    feed_place = feed_place.astype(jnp.int32)
    feed_starts = tuple(int(start) for start in feed_starts)

    seq_count = codons.shape[0]
    row_count = seq_count * SEQ_LEN
    window = jax.vmap(partial(lax.dynamic_slice_in_dim, slice_size=SEQ_LEN))(codons, offsets)
    vocab_ids = jnp.arange(VOCAB, dtype=jnp.int32)
    token_hot = window.reshape(row_count)[:, None] == vocab_ids[None, :]
    token_low = token_hot.astype(low_type)
    target_hot = (targets.reshape(row_count)[:, None] == vocab_ids[None, :]).astype(jnp.float32)
    stream = embed_scale * times_plain(token_low, table_low)
    token_ids = window.reshape(row_count)
    lane_ids = jnp.arange(2 * LANES, dtype=jnp.int32) % LANES
    hot = (token_ids[:, None] == lane_ids[None, :]).astype(low_type)
    hot_turned = (token_ids[None, :] == lane_ids[:LANES, None]).astype(low_type)
    cosine, sine_table = rotary_tables(positions.reshape(row_count))
    cosine = jnp.concatenate([cosine] * 4, axis=1)
    sine_table = jnp.concatenate([-sine_table, sine_table] * 2, axis=1)
    pairs = D // PAIR // ATTEND_CALLS
    attended = []

    for number in range(ATTEND_CALLS):
        attended.append(
            attend_call(hot, tables, cosine, sine_table, number * pairs, pairs)
        )
    last_mask = masks[-1]
    mixed_low = jnp.concatenate([parts[3] for parts in attended], axis=1)
    mixing_low = weight_rows(2, D // devices)
    attend_low = lax.all_gather(gate(attend_own, mixed_low), BOTH, axis=0)
    branch = times_trans(mixed_low, mixing_low) + mixing_bias
    middle = stream + branch
    normed_two, normal_two, inverse_two = norm_forward(middle, gain_two, bias_two)
    normed_two_low = normed_two.astype(low_type)
    hidden_low, slope_low, feed_out = feed_call(
        feed_place, normed_two_low, expand_bias[None, :], feed_source, feed_starts
    )
    feed_out = feed_out + reduce_bias
    output = middle + feed_out
    final_norm, normal_last, inverse_last = norm_forward(output, gain_last, bias_last)
    final_low = final_norm.astype(low_type)
    logits = times_trans(final_low, table_low)
    row_peak = jnp.max(logits, axis=-1, keepdims=True)
    shifted = jnp.exp(logits - row_peak)
    prob_rows = shifted / jnp.sum(shifted, axis=-1, keepdims=True)
    prob_sum = jnp.sum(prob_rows, axis=0)
    logit_grad = (prob_rows - target_hot).astype(low_type)
    final_grad = times_plain(logit_grad, table_low)
    table_head = trans_times(logit_grad, final_low)
    output_grad, gain_last_grad, bias_last_grad = norm_backward(
        final_grad, normal_last, inverse_last, gain_last
    )
    feed_low = output_grad.astype(low_type)
    reduce_bias_grad = jnp.sum(feed_low, axis=0, dtype=jnp.float32)
    half_ff = FF // 2
    static_marks = [masks[-1], 2] + list(reversed(masks[:-1]))
    static_shape = (2,) * len(static_marks) + (unit, D)

    reduce_send = trans_times(hidden_low[:, half_ff:], feed_low).astype(low_type)
    pre_grad, normed_two_grad, expand_bias_grad = feed_back_call(
        feed_place, gate(feed_low, reduce_send), slope_low, feed_source, feed_starts
    )
    reduce_got = gate(swap(reduce_send, 1), pre_grad)
    reduce_sum = trans_times(hidden_low[:, :half_ff], feed_low) + reduce_got
    reduce_chain = sum_chain([(reduce_sum.reshape(static_shape), static_marks, False)], low_type)
    reduce_sent = next(reduce_chain)
    expand_send = trans_times(
        gate(pre_grad, reduce_sent)[:, half_ff:], normed_two_low
    ).astype(low_type)
    expand_sum = trans_times(pre_grad[:, :half_ff], normed_two_low) + swap(expand_send, 1)
    middle_part, gain_two_grad, bias_two_grad = norm_backward(
        normed_two_grad, normal_two, inverse_two, gain_two
    )
    middle_grad = output_grad + middle_part
    branch_low = middle_grad.astype(low_type)
    mixing_bias_grad = jnp.sum(branch_low, axis=0, dtype=jnp.float32)
    mixing_sum = trans_times(branch_low, mixed_low).reshape(
        bits_shape(devices, (D // devices, D))
    )
    (mixing_item,) = finish_hop(hop([(mixing_sum, all_masks, True)], 1, low_type))
    mixed_grad = times_plain(branch_low, mixing_low).astype(low_type)
    expand_chain = sum_chain(
        [(expand_sum.reshape(static_shape), static_marks, False), mixing_item], low_type
    )
    expand_sent = next(expand_chain)

    backs = []
    back_pairs = D // PAIR // BACK_CALLS

    def back_step(waits):
        number = len(backs)
        first = number * back_pairs
        source = attended[first // pairs]
        order = (backs[-1][1],) if backs else ()
        backs.append(
            attend_back_call(
                hot_turned,
                *source[:3],
                gate(mixed_grad, (waits, order)),
                source[4],
                cosine,
                sine_table,
                first,
                first % pairs,
                back_pairs,
            )
        )
        return backs[-1][1]

    mixed_grad, attend_low = lax.optimization_barrier((mixed_grad, attend_low))
    back_step(expand_sent)
    token = back_step(())
    expand_sent = expand_chain.send(token)
    reduce_sent = reduce_chain.send(token)
    token = back_step((expand_sent, reduce_sent))
    expand_sent = expand_chain.send(token)
    reduce_sent = reduce_chain.send(token)
    token = back_step((expand_sent, reduce_sent))
    reduce_sent = reduce_chain.send(token)
    token = back_step(reduce_sent)
    expand_sent = expand_chain.send(token)
    token = back_step(expand_sent)
    (reduce_sum,) = drain(reduce_chain, token)
    expand_sum, mixing_sum = drain(expand_chain, token)
    dense = jnp.concatenate([reduce_sum, expand_sum, mixing_sum], axis=0)
    spot = lax.axis_index("narrow")
    dense, backs = together((dense, backs))

    def one_chain(value, mask):
        (got,) = yield [(value, mask)]
        return got

    columns = D // wide_size
    rows_hist = -(-VOCAB // columns)

    def make_small(backs):
        entry_gradient, one_sums, table_sum = entry_call(
            embed_scale,
            hot,
            jnp.pad(table_low, ((0, LANES - VOCAB), (0, 0))),
            gain_one[None, :],
            middle_grad,
            attend_low.reshape(3 * D, D),
            [back[0] for back in backs],
        )
        hist_part = jnp.pad(prob_sum, (0, rows_hist * columns - VOCAB)).reshape(rows_hist, columns)
        expand_ordered = in_order(
            expand_bias_grad.reshape(devices, FF // devices), hidden_masks, 1, me
        )
        small_grads = small_blocks(
            [back[1] for back in backs],
            table_sum,
            table_head,
            hist_part,
            (
                (one_sums, 0),
                (gain_two_grad[None, :], 2),
                (bias_two_grad[None, :], 3),
                (gain_last_grad[None, :], 4),
                (bias_last_grad[None, :], 5),
                (mixing_bias_grad[None, :], 9),
                (reduce_bias_grad[None, :], 10),
                (expand_ordered.reshape(1, FF), 11),
            ),
            wide_size,
        )
        return entry_gradient, small_grads

    beside_chain = Chain(one_chain(dense, 2))
    entry_gradient, small_grads = advance([beside_chain], make_small, backs)
    beside = beside_chain.result
    cores = [Chain(one_chain(dense, 1)), Chain(one_chain(beside, 1))]
    small_chain = Chain(sum_small(small_grads))
    advance(cores + [small_chain])
    pieces = (dense, beside, cores[0].result, cores[1].result)

    def make_dense(pieces):
        return dense_step(
            spot,
            (unit, unit, D // devices),
            pieces,
            attend_moment,
            (reduce_moment, expand_moment, mixing_moment),
        )

    dense_totals, dense_next, dense_rows, gram_own = advance([small_chain], make_dense, pieces)
    reduce_total, expand_total, mixing_total = dense_totals
    reduce_next, expand_next, mixing_next = dense_next

    def step_of(moment, gradient):
        moment_next = MUON_MU * moment + (1.0 - MUON_MU) * gradient
        return moment_next, (1.0 - MUON_MU) * gradient + MUON_MU * moment_next

    gram_chain = Chain(sum_gram(gram_own))
    while small_chain.request:
        advance([chain for chain in (gram_chain, small_chain) if chain.request])
    small_total = small_chain.result
    token_sums = small_total[:VOCAB, : 3 * D // wide_size]
    small_total = small_total[:, 3 * D // wide_size :]
    attend_total = lax.dot_general(
        token_sums,
        table_normed.astype(jnp.float32),
        (((0,), (0,)), ((), ())),
        precision=lax.Precision.HIGHEST,
        preferred_element_type=jnp.float32,
    )
    attend_next, attend_step = step_of(attend_moment, attend_total)
    gradient_rate = (1.0 - MUON_MU) * (1.0 + MUON_MU)
    crossed = exact_times(
        token_sums, jnp.concatenate([attend_moment, token_sums.T], axis=1)
    )
    crossed_chain = Chain(sum_wide(crossed))
    while crossed_chain.request:
        advance([chain for chain in (gram_chain, crossed_chain) if chain.request])
    while gram_chain.request:
        advance([gram_chain])
    crossed = crossed_chain.result
    gram_parts = gram_chain.result
    table_wide = table_normed.astype(jnp.float32)
    added = gradient_rate * (
        (MUON_MU * MUON_MU) * crossed[:, :D]
        + (0.5 * gradient_rate) * exact_times(crossed[:, D:], table_wide)
    )
    added = jnp.where(spot == 0, added, 0.0)
    table_total = small_total[:VOCAB]
    vector_total = small_total[VOCAB : VOCAB + 15]
    prob_total = small_total[VOCAB + 15 :].reshape(rows_hist * columns)[:VOCAB]
    histogram = prob_total * (VOCAB / (row_count * devices))
    totals = (attend_total, mixing_total, expand_total, reduce_total)
    moment_next = (attend_next, mixing_next, expand_next, reduce_next)
    most = dense_rows.shape[0]
    attend_rows = jnp.pad(attend_step, ((0, most - attend_step.shape[0]), (0, 0)))
    rows = jnp.where(spot == 0, attend_rows, dense_rows)
    ortho = newton_rows(gram_parts, rows, added, table_normed)
    ortho, table_total, vector_total = together((ortho, table_total, vector_total))
    across = swap(ortho, 2)
    table_new, table_mean_next, table_square_next = adam_step(
        table_weight, table_mean, table_square, table_total, TABLE_RATE, TABLE_DECAY, step_count
    )
    vector_new, vector_mean_next, vector_square_next = adam_step(
        vector_params, vector_mean, vector_square, vector_total, VECTOR_RATE, 0.0, step_count
    )
    across, adam_results = together(
        (
            across,
            (
                table_new,
                table_mean_next,
                table_square_next,
                vector_new,
                vector_mean_next,
                vector_square_next,
            ),
        )
    )
    orthos = (ortho, swap(ortho, 1), across, swap(across, 1))
    matrices = (attend_weight, mixing_weight, expand_weight, reduce_weight)
    rates = tuple(
        MUON_RATE * SHAPE_FACTOR * math.sqrt(max(rows, D)) for rows in (3 * D, D, FF, FF)
    )
    matrix_new = tuple(update_rows(spot, orthos, matrices, rates))
    results = (
        totals
        + (table_total, vector_total)
        + matrix_new
        + moment_next
        + (
            *adam_results,
        )
    )
    block_output = output.astype(low_type).reshape(seq_count, SEQ_LEN, D)
    return (block_output, entry_gradient.reshape(seq_count, SEQ_LEN, D)) + results + (histogram,)


def solution(mesh):
    in_specs = (
        P(("wide", "narrow"), None),
        P(("wide", "narrow")),
        P(("wide", "narrow"), None),
        P(("wide", "narrow"), None),
        P(None, "wide"),
        P("wide", None),
        P("wide", None),
        P("wide", None),
        P("wide", None),
        P(None, "wide"),
        P("wide", None),
        P("wide", None),
        P("wide", None),
        P("wide", None),
        P(None, "wide"),
        P(None, "wide"),
        P(None, "wide"),
        P(None, "wide"),
        P(),
    )
    out_specs = (
        P(("wide", "narrow"), None, None),
        P(("wide", "narrow"), None, None),
        P("wide", None),
        P("wide", None),
        P("wide", None),
        P("wide", None),
        P(None, "wide"),
        P(None, "wide"),
        P("wide", None),
        P("wide", None),
        P("wide", None),
        P("wide", None),
        P("wide", None),
        P("wide", None),
        P("wide", None),
        P("wide", None),
        P(None, "wide"),
        P(None, "wide"),
        P(None, "wide"),
        P(None, "wide"),
        P(None, "wide"),
        P(None, "wide"),
        P(),
    )
    return jax.shard_map(
        on_device, mesh=mesh, in_specs=in_specs, out_specs=out_specs, check_vma=False
    )
```

```python
from functools import partial
import math

import jax
import jax.numpy as jnp
import numpy as np
from jax import lax
from jax.experimental import pallas as pl
from jax.experimental.pallas import tpu as pltpu
from jax.sharding import PartitionSpec as P

D = 768
HEADS = 12
HEAD_DIM = 64
FF = 3072
VOCAB = 70
SEQ_LEN = 912
NS_ITERS = 5


NORM_EPS = 1e-05
ROPE_BASE = 10000.0
NEWTON_A = 3.4445
NEWTON_B = -4.775
NEWTON_C = 2.0315
MUON_MU = 0.95
MUON_RATE = 0.3
MUON_DECAY = 0.1
SHAPE_FACTOR = 0.2
ADAM_BETA1 = 0.9
ADAM_BETA2 = 0.95
ADAM_EPS = 1e-08
TABLE_RATE = 0.03
TABLE_DECAY = 0.01
VECTOR_RATE = 0.2


def times_plain(left_side, right_side):
    return jnp.dot(left_side, right_side, preferred_element_type=jnp.float32)


def times_trans(left_side, right_side):
    return lax.dot_general(
        left_side, right_side, (((1,), (1,)), ((), ())), preferred_element_type=jnp.float32
    )


def trans_times(left_side, right_side):
    return lax.dot_general(
        left_side, right_side, (((0,), (0,)), ((), ())), preferred_element_type=jnp.float32
    )


def exact_times(left_side, right_side):
    return jnp.dot(
        left_side, right_side, precision=lax.Precision.HIGHEST, preferred_element_type=jnp.float32
    )


def norm_forward(values, gain_row, bias_row):
    center = values - jnp.mean(values, axis=-1, keepdims=True)
    spread = jnp.mean(center * center, axis=-1, keepdims=True)
    inverse = lax.rsqrt(spread + NORM_EPS)
    normal = center * inverse
    return (normal * gain_row + bias_row, normal, inverse)


def norm_backward(upstream, normal, inverse, gain_row):
    scaled = upstream * gain_row
    inner_part = (
        scaled
        - jnp.mean(scaled, axis=-1, keepdims=True)
        - normal * jnp.mean(scaled * normal, axis=-1, keepdims=True)
    )
    return (inverse * inner_part, jnp.sum(upstream * normal, axis=0), jnp.sum(upstream, axis=0))


def rotary_tables(positions):
    half_dim = HEAD_DIM // 2
    frequency = ROPE_BASE ** (-(jnp.arange(half_dim, dtype=jnp.float32) * 2.0 / HEAD_DIM))
    turned = positions.astype(jnp.float32)[..., None] * frequency
    return (jnp.cos(turned), jnp.sin(turned))


PAIR = 2 * HEAD_DIM
SPAN = 1024
STRIP = 256
PARTS = 4
FEED_STRIP = 304
BLOCK = 96
PART_BLOCKS = D // BLOCK
LANES = 128
ATTEND_CALLS = 3
BACK_CALLS = 6


BOTH = ("wide", "narrow")
GRAM_TILE = 256
GRAM_SPOTS = ((0, 0), (0, 1), (0, 2), (1, 1), (1, 2), (2, 2))


def swap(value, mask):
    total = lax.axis_size(BOTH)
    return lax.ppermute(value, BOTH, [(spot, spot ^ mask) for spot in range(total)])


def my_index():
    return lax.axis_index("wide") * lax.axis_size("narrow") + lax.axis_index("narrow")


def wide_masks():
    narrow_size = lax.axis_size("narrow")
    count = lax.axis_size("wide").bit_length() - 1
    return [narrow_size << bit for bit in reversed(range(count))]


def offsets_of(masks):
    table = [0]
    for mask in masks:
        table = table + [offset ^ mask for offset in table]
    return np.array(table)


def gate(value, others):
    leaves, form = jax.tree.flatten(value)
    held = lax.optimization_barrier(tuple(leaves) + tuple(jax.tree.leaves(others)))
    return jax.tree.unflatten(form, held[: len(leaves)])


def padded_rows(array):
    return jnp.pad(array, ((0, -array.shape[0] % 16), (0, 0)))


def together(values):
    leaves, form = jax.tree.flatten(values)
    return jax.tree.unflatten(form, lax.optimization_barrier(tuple(leaves)))


def gather_blocks(piece, masks):
    for mask in masks:
        piece = jnp.concatenate([piece, swap(piece, mask)], axis=0)
    return piece


def take_blocks(array, index):
    return jnp.take(array, index, axis=0, mode="clip")


def places_of(masks, unit):
    offsets = offsets_of(masks) // unit
    place = np.zeros_like(offsets)
    place[offsets] = np.arange(offsets.size)
    return place


def in_order(blocks, masks, unit, base):
    place = places_of(masks, unit)
    return take_blocks(blocks, jnp.asarray(place)[jnp.arange(place.size) ^ base])


def out_of_order(blocks, masks, unit, base):
    offsets = offsets_of(masks) // unit
    return take_blocks(blocks, jnp.asarray(offsets) ^ base)


def quarter_rows(array):
    count = array.shape[0] // lax.axis_size("narrow")
    return lax.dynamic_slice_in_dim(array, lax.axis_index("narrow") * count, count, 0)


def side_of(mask):
    return (my_index() // mask) % 2


def split_static(array, axis):
    return lax.index_in_dim(array, 0, axis, False), lax.index_in_dim(array, 1, axis, False)


def split_sided(array, axis, mask):
    side = side_of(mask)
    return (
        lax.dynamic_index_in_dim(array, side, axis, False),
        lax.dynamic_index_in_dim(array, 1 - side, axis, False),
    )


def halves(item, mask):
    array, marks, sided = item
    axis = marks.index(mask)
    keep, send = split_sided(array, axis, mask) if sided else split_static(array, axis)
    return (keep, marks[:axis] + marks[axis + 1 :], sided), send


def hop(items, mask, kind):
    pairs = [halves(item, mask) for item in items]
    rows = [send.astype(kind).reshape(-1, send.shape[-1]) for _, send in pairs]
    flat = jnp.concatenate(rows, axis=0) if len(rows) > 1 else rows[0]
    token = yield flat
    got = gate(swap(flat, mask), token)
    results, at = [], 0
    for ((keep, marks, sided), send), row in zip(pairs, rows):
        part = got[at : at + row.shape[0]].reshape(send.shape).astype(jnp.float32)
        results.append((keep + part, marks, sided))
        at += row.shape[0]
    return results


def finish(steps, token):
    try:
        steps.send(token)
    except StopIteration as stop:
        return stop.value


def finish_hop(steps):
    next(steps)
    return finish(steps, ())


def columns_of(items, start, stop):
    return [(array[..., start:stop], marks, sided) for array, marks, sided in items]


def sum_chain(items, kind):
    masks = wide_masks()
    width = items[0][0].shape[-1]
    ways = [columns_of(items, 0, width // 2), columns_of(items, width // 2, width)]
    for pair in ((masks[-1], 2), (2, masks[-1])):
        steps = [hop(way, mask, jnp.bfloat16) for way, mask in zip(ways, pair)]
        token = yield tuple(next(step) for step in steps)
        ways = [finish(step, token) for step in steps]
    items = [
        (jnp.concatenate([left[0], right[0]], axis=-1), left[1], left[2])
        for left, right in zip(*ways)
    ]
    for mask in reversed(masks[:-1]):
        items = yield from hop(items, mask, kind)
    return [item[0] for item in items]


def drain(chain, token):
    while True:
        try:
            chain.send(token)
        except StopIteration as stop:
            return stop.value


def bits_shape(count, tail):
    return (2,) * (count.bit_length() - 1) + tuple(tail)


class Chain:
    def __init__(self, steps):
        self.steps, self.result = steps, None
        self.request = next(steps)

    def give(self, got):
        try:
            self.request = self.steps.send(got)
        except StopIteration as stop:
            self.request, self.result = [], stop.value


def advance(chains, meanwhile=None, needs=()):
    sends, needs = together(([[array for array, _ in chain.request] for chain in chains], needs))
    gots = [
        [swap(array, mask) for array, (_, mask) in zip(send, chain.request)]
        for send, chain in zip(sends, chains)
    ]
    made = meanwhile(needs) if meanwhile else ()
    gots, made = together((gots, made))
    for chain, got in zip(chains, gots):
        chain.give(got)
    return made


def sum_small(blocks):
    (got,) = yield [(blocks, 1)]
    total = (blocks + got).reshape(bits_shape(blocks.shape[0], blocks.shape[1:]))
    masks = wide_masks()
    while masks:
        mask = masks[-1]
        keep, send = split_sided(total, len(masks) - 1, mask)
        (got,) = yield [(send, mask)]
        total = keep + got
        masks = masks[:-1]
    (got,) = yield [(total, 2)]
    return total + got


def sum_wide(value):
    for mask in reversed(wide_masks()):
        (got,) = yield [(value, mask)]
        value = value + got
    return value


def sum_gram(parts):
    masks = list(reversed(wide_masks()))
    ways = [masks, [masks[1], masks[0]] + masks[2:]]
    parts = list(parts)
    for step in range(len(masks)):
        pairs = [
            split_sided(part.reshape((2, part.shape[0] // 2) + part.shape[1:]), 0, way[step])
            for part, way in zip(parts, ways)
        ]
        gots = yield [(send, way[step]) for (_, send), way in zip(pairs, ways)]
        parts = [keep + got for (keep, _), got in zip(pairs, gots)]
    for step in reversed(range(len(masks))):
        gots = yield [(part, way[step]) for part, way in zip(parts, ways)]
        parts = [
            jnp.where(
                side_of(way[step]) == 0,
                jnp.concatenate([part, got], axis=0),
                jnp.concatenate([got, part], axis=0),
            )
            for part, got, way in zip(parts, gots, ways)
        ]
    return parts


def row_dot(left_side, right_side):
    return lax.dot_general(
        left_side, right_side, (((1,), (1,)), ((), ())), preferred_element_type=jnp.float32
    )


def split_two(values):
    high = values.astype(jnp.bfloat16)
    return high, (values - high.astype(jnp.float32)).astype(jnp.bfloat16)


def newton_kernel(
    low_ref, high_ref, rows_ref, added_ref, table_ref, out_ref,
    gram_now, other, left, right, rows_left,
):
    tile = GRAM_TILE
    trace = jnp.zeros((1, 1), jnp.float32)
    diagonal = lax.broadcasted_iota(jnp.int32, (tile, tile), 0) == lax.broadcasted_iota(
        jnp.int32, (tile, tile), 1
    )

    def span(number):
        return slice(number * tile, (number + 1) * tile)

    def turned_dot(left_side, right_side):
        return lax.dot_general(
            left_side,
            right_side,
            (((0,), (0,)), ((), ())),
            preferred_element_type=jnp.float32,
        )

    added_high, added_low = split_two(added_ref[...])
    added_rest = added_ref[...] - added_high.astype(jnp.float32) - added_low.astype(jnp.float32)
    added_parts = (added_high, added_low, added_rest.astype(jnp.bfloat16))
    half = len(GRAM_SPOTS) // 2
    for number, (row, column) in enumerate(GRAM_SPOTS):
        source = low_ref if number < half else high_ref
        block = source[span(number % half), :]
        for part in added_parts:
            block = block + turned_dot(part[:, span(row)], table_ref[:, span(column)])
            block = block + turned_dot(table_ref[:, span(row)], part[:, span(column)])
        gram_now[span(row), span(column)] = block
        if row == column:
            picked = jnp.where(diagonal, block, 0.0)
            trace = trace + jnp.sum(jnp.sum(picked, axis=0, keepdims=True), axis=1, keepdims=True)
    inverse = 1.0 / (jnp.sqrt(trace) + 1e-07)
    scale = inverse * inverse
    for row, column in GRAM_SPOTS:
        block = gram_now[span(row), span(column)] * scale
        gram_now[span(row), span(column)] = block
        if row != column:
            gram_now[span(column), span(row)] = block.T

    def set_left(values):
        high, low = split_two(values)
        left[:, 0:D] = high
        left[:, D : 2 * D] = high
        left[:, 2 * D : 3 * D] = low

    def set_right(values):
        high, low = split_two(values)
        right[0:D, :] = high
        right[D : 2 * D, :] = low
        right[2 * D : 3 * D, :] = high

    def set_rows(values):
        high, low = split_two(values)
        rows_left[:, 0:D] = high
        rows_left[:, D : 2 * D] = high
        rows_left[:, 2 * D : 3 * D] = low

    def product(target, finish):
        for column in range(D // tile):
            rows = (column + 1) * tile
            block = jnp.dot(left[0:rows, :], right[:, span(column)], preferred_element_type=jnp.float32)
            for row in range(column + 1):
                piece = finish(block[span(row), :], row, column)
                target[span(row), span(column)] = piece
                if row != column:
                    target[span(column), span(row)] = piece.T

    def same(block, row, column):
        return block

    def factor(block, row, column):
        block = NEWTON_B * gram_now[span(row), span(column)] + NEWTON_C * block
        if row == column:
            block = block + jnp.where(diagonal, NEWTON_A, 0.0)
        return block

    def set_factor():
        set_left(gram_now[...])
        set_right(gram_now[...])
        product(other, factor)
        set_right(other[...])

    def rows_product():
        return jnp.dot(rows_left[...], right[...], preferred_element_type=jnp.float32)

    set_rows(rows_ref[...] * inverse)

    def body(step, carry):
        set_factor()
        product(other, same)
        set_left(other[...])
        product(gram_now, same)
        set_rows(rows_product())
        return carry

    lax.fori_loop(0, NS_ITERS - 1, body, 0)
    set_factor()
    out_ref[...] = rows_product().astype(out_ref.dtype)


def newton_rows(gram_parts, rows, added, table):
    count = rows.shape[0]
    return pl.pallas_call(
        newton_kernel,
        out_shape=jax.ShapeDtypeStruct((count, D), jnp.bfloat16),
        in_specs=[pl.BlockSpec(memory_space=pltpu.VMEM)] * 5,
        out_specs=pl.BlockSpec(memory_space=pltpu.VMEM),
        scratch_shapes=[
            pltpu.VMEM((D, D), jnp.float32),
            pltpu.VMEM((D, D), jnp.float32),
            pltpu.VMEM((D, 3 * D), jnp.bfloat16),
            pltpu.VMEM((3 * D, D), jnp.bfloat16),
            pltpu.VMEM((count, 3 * D), jnp.bfloat16),
        ],
        compiler_params=pltpu.CompilerParams(vmem_limit_bytes=48 << 20),
        cost_estimate=pl.CostEstimate(flops=60 * D * D * D, bytes_accessed=4 << 20, transcendentals=0),
        name="newton",
    )(*gram_parts, rows, added, table)


def pack_kernel(spot_ref, *refs):
    *refs, last_ref, out_ref, last_out_ref = refs
    at = 0
    for number, ref in enumerate(refs):
        count = ref.shape[0]
        out_ref[at : at + count, :] = ref[...].astype(jnp.bfloat16)
        at += count + (-count % 16 if number + 1 < len(refs) else 0)
    last_out_ref[...] = last_ref[...].astype(jnp.bfloat16)


def pack_rows(weights, spot):
    units = [weight.shape[0] // lax.axis_size("narrow") for weight in weights]
    if any(unit % 8 for unit in units) or any(unit % 16 for unit in units[:-2]):
        rows = [quarter_rows(weight).astype(jnp.bfloat16) for weight in weights]
        return jnp.concatenate([padded_rows(row) for row in rows[:-2]] + rows[-2:-1], axis=0), rows[-1]
    return pl.pallas_call(
        pack_kernel,
        grid_spec=pltpu.PrefetchScalarGridSpec(
            num_scalar_prefetch=1,
            grid=(1,),
            in_specs=[pl.BlockSpec((unit, D), lambda step, spot: (spot[0], 0)) for unit in units],
            out_specs=[
                pl.BlockSpec((sum(units[:-1]), D), lambda step, spot: (0, 0)),
                pl.BlockSpec((units[-1], D), lambda step, spot: (0, 0)),
            ],
        ),
        out_shape=[
            jax.ShapeDtypeStruct((sum(units[:-1]), D), jnp.bfloat16),
            jax.ShapeDtypeStruct((units[-1], D), jnp.bfloat16),
        ],
        name="pack",
    )(spot[None].astype(jnp.int32), *weights)


def entry_kernel(scale, *refs):
    (hot_ref, table_ref, gain_ref, middle_ref, weight_ref), refs = refs[:5], refs[5:]
    *low_refs, entry_ref, sums_ref, table_sum_ref = refs
    step = pl.program_id(0)
    hot = hot_ref[:, 0:LANES]
    stream = scale * jnp.dot(hot, table_ref[...], preferred_element_type=jnp.float32)
    grads = None
    for kind in range(3):
        low = jnp.concatenate([ref[kind] for ref in low_refs], axis=1)
        part = jnp.dot(
            low, weight_ref[kind * D : (kind + 1) * D, :], preferred_element_type=jnp.float32
        )
        grads = part if grads is None else grads + part
    center = stream - jnp.mean(stream, axis=-1, keepdims=True)
    inverse = lax.rsqrt(jnp.mean(center * center, axis=-1, keepdims=True) + NORM_EPS)
    normal = center * inverse
    scaled = grads * gain_ref[...]
    inner = (
        scaled
        - jnp.mean(scaled, axis=-1, keepdims=True)
        - normal * jnp.mean(scaled * normal, axis=-1, keepdims=True)
    )
    entry = middle_ref[...] + inverse * inner
    entry_ref[...] = entry
    sums = jnp.concatenate(
        [
            jnp.sum(grads * normal, axis=0, keepdims=True),
            jnp.sum(grads, axis=0, keepdims=True),
        ],
        axis=0,
    )
    high = entry.astype(jnp.bfloat16)
    rest = entry - high.astype(jnp.float32)
    middle = rest.astype(jnp.bfloat16)
    low = (rest - middle.astype(jnp.float32)).astype(jnp.bfloat16)
    table_sum = None
    for part in (high, middle, low):
        part = lax.dot_general(
            hot, part, (((0,), (0,)), ((), ())), preferred_element_type=jnp.float32
        )
        table_sum = part if table_sum is None else table_sum + part

    @pl.when(step == 0)
    def _():
        sums_ref[...] = sums
        table_sum_ref[...] = scale * table_sum

    @pl.when(step > 0)
    def _():
        sums_ref[...] += sums
        table_sum_ref[...] += scale * table_sum


def entry_call(scale, hot, table, gain, middle_grad, weight, lows):
    rows = SEQ_LEN // 3
    whole = lambda step: (0, 0)
    own = lambda step: (step, 0)
    return pl.pallas_call(
        partial(entry_kernel, scale),
        grid=(3,),
        in_specs=[
            pl.BlockSpec((rows, hot.shape[1]), own),
            pl.BlockSpec(table.shape, whole),
            pl.BlockSpec(gain.shape, whole),
            pl.BlockSpec((rows, D), own),
            pl.BlockSpec(weight.shape, whole),
        ]
        + [pl.BlockSpec((3, rows, low.shape[2]), lambda step: (0, step, 0)) for low in lows],
        out_specs=[
            pl.BlockSpec((rows, D), own),
            pl.BlockSpec((2, D), whole),
            pl.BlockSpec((LANES, D), whole),
        ],
        out_shape=[
            jax.ShapeDtypeStruct((SEQ_LEN, D), jnp.float32),
            jax.ShapeDtypeStruct((2, D), jnp.float32),
            jax.ShapeDtypeStruct((LANES, D), jnp.float32),
        ],
        compiler_params=pltpu.CompilerParams(vmem_limit_bytes=48 << 20),
        cost_estimate=pl.CostEstimate(flops=1 << 20, bytes_accessed=1 << 16, transcendentals=0),
        name="entry",
    )(hot, table, gain, middle_grad, weight, *lows)


def small_kernel(parts, spot_rows, table_sum_ref, head_ref, hist_ref, *refs):
    part_refs, refs = refs[:parts], refs[parts:]
    *row_refs, out_ref, sums, held = refs
    for number, part in enumerate(part_refs):
        width = part.shape[2]
        for kind in range(3):
            start = kind * D + number * width
            sums[:, start : start + width] = part[kind]
    held[0:VOCAB, :] = table_sum_ref[0:VOCAB, :] + head_ref[...]
    bias = jnp.sum(sums[...], axis=0, keepdims=True)
    for kind in range(3):
        held[VOCAB + 6 + kind : VOCAB + 7 + kind, :] = bias[:, kind * D : (kind + 1) * D]
    for ref, at in zip(row_refs, spot_rows):
        if len(ref.shape) == 1:
            held[at : at + 1, :] = ref[...][None, :]
            continue
        for row in range(ref.shape[0]):
            for part in range(ref.shape[1] // D):
                held[at : at + 1, :] = ref[row : row + 1, part * D : (part + 1) * D]
                at += 1
    count, rows, columns = out_ref.shape
    narrow = D // count
    wide = columns - narrow
    base = held.shape[0]
    for number in range(count):
        out_ref[number, 0:VOCAB, 0:wide] = sums[0:VOCAB, number * wide : (number + 1) * wide]
        out_ref[number, VOCAB:rows, 0:wide] = jnp.zeros((rows - VOCAB, wide), jnp.float32)
        out_ref[number, 0:base, wide:columns] = held[:, number * narrow : (number + 1) * narrow]
        out_ref[number, base:rows, wide:columns] = hist_ref[...]


def small_blocks(parts, table_sum, head, hist, rows, wide_size):
    whole = pl.BlockSpec(memory_space=pltpu.VMEM)
    total = VOCAB + 15 + hist.shape[0]
    arrays = [array for array, _ in rows]
    return pl.pallas_call(
        partial(small_kernel, len(parts), tuple(VOCAB + place for _, place in rows)),
        in_specs=[whole] * (3 + len(parts) + len(rows)),
        out_specs=whole,
        out_shape=jax.ShapeDtypeStruct((wide_size, total, 4 * D // wide_size), jnp.float32),
        scratch_shapes=[
            pltpu.VMEM((LANES, 3 * D), jnp.float32),
            pltpu.VMEM((VOCAB + 15, D), jnp.float32),
        ],
        cost_estimate=pl.CostEstimate(flops=1 << 20, bytes_accessed=1 << 16, transcendentals=0),
        name="small_grads",
    )(table_sum, head, hist, *parts, *arrays)


def dense_kernel(units, spot_ref, own_ref, beside_ref, core_ref, cross_ref, *refs):
    base_ref, *refs = refs
    count = len(units)
    moment_refs, refs = refs[:count], refs[count:]
    total_refs, next_refs, refs = refs[:count], refs[count : 2 * count], refs[2 * count :]
    rows_ref, low_ref, high_ref, left, right = refs
    spot = spot_ref[0]
    for device in range(4):
        way = spot ^ device
        for kind, source in enumerate((own_ref, core_ref, beside_ref, cross_ref)):

            @pl.when(way == kind)
            def _():
                at = 0
                for total_ref, unit in zip(total_refs, units):
                    total_ref[device * unit : (device + 1) * unit, :] = source[at : at + unit, :]
                    at += unit

    rows_ref[...] = jnp.zeros_like(rows_ref)

    @pl.when(spot == 0)
    def _():
        rows_ref[0 : base_ref.shape[0], :] = (MUON_MU * MUON_MU) * base_ref[...]

    for number in range(count):
        gradient = total_refs[number][...]
        moment_next = MUON_MU * moment_refs[number][...] + (1.0 - MUON_MU) * gradient
        next_refs[number][...] = moment_next
        place = count - number

        @pl.when(spot == place)
        def _():
            rows_ref[0 : gradient.shape[0], :] = (
                1.0 - MUON_MU
            ) * gradient + MUON_MU * moment_next

    high, low = split_two(rows_ref[...])
    depth = rows_ref.shape[0]
    right[0:depth, :] = high
    right[depth : 2 * depth, :] = low
    right[2 * depth : 3 * depth, :] = high
    turned_high, turned_low = split_two(rows_ref[...].T)
    left[:, 0:depth] = turned_high
    left[:, depth : 2 * depth] = turned_high
    left[:, 2 * depth : 3 * depth] = turned_low
    half = len(GRAM_SPOTS) // 2
    for number, (row, column) in enumerate(GRAM_SPOTS):
        target = low_ref if number < half else high_ref
        at = (number % half) * GRAM_TILE
        target[at : at + GRAM_TILE, :] = jnp.dot(
            left[row * GRAM_TILE : (row + 1) * GRAM_TILE, :],
            right[:, column * GRAM_TILE : (column + 1) * GRAM_TILE],
            preferred_element_type=jnp.float32,
        )


def dense_step(spot, units, pieces, base, moments):
    whole = pl.BlockSpec(memory_space=pltpu.VMEM)
    most = max(moment.shape[0] for moment in moments)
    shapes = [jax.ShapeDtypeStruct(moment.shape, jnp.float32) for moment in moments]
    half = jax.ShapeDtypeStruct((len(GRAM_SPOTS) // 2 * GRAM_TILE, GRAM_TILE), jnp.float32)
    results = pl.pallas_call(
        partial(dense_kernel, units),
        in_specs=[pl.BlockSpec(memory_space=pltpu.SMEM)] + [whole] * (5 + len(moments)),
        out_specs=[whole] * (2 * len(moments) + 3),
        out_shape=shapes + shapes + [jax.ShapeDtypeStruct((most, D), jnp.float32), half, half],
        scratch_shapes=[
            pltpu.VMEM((D, 3 * most), jnp.bfloat16),
            pltpu.VMEM((3 * most, D), jnp.bfloat16),
        ],
        compiler_params=pltpu.CompilerParams(vmem_limit_bytes=48 << 20),
        cost_estimate=pl.CostEstimate(flops=1 << 20, bytes_accessed=1 << 16, transcendentals=0),
        name="dense_step",
    )(spot[None].astype(jnp.int32), *pieces, base, *moments)
    count = len(moments)
    return results[:count], results[count : 2 * count], results[2 * count], results[2 * count + 1 :]


def update_kernel(rates, spot_ref, *refs):
    count = len(rates)
    sources, refs = refs[:4], refs[4:]
    for number in range(count):
        weight_ref, out_ref = refs[number], refs[count + number]
        rows = weight_ref.shape[0]
        way = spot_ref[0] ^ number
        for kind, source in enumerate(sources):

            @pl.when(way == kind)
            def _():
                out_ref[...] = weight_ref[...] * (1.0 - MUON_RATE * MUON_DECAY) - rates[
                    number
                ] * source[0:rows, :].astype(jnp.float32)


def update_rows(spot, orthos, weights, rates):
    whole = pl.BlockSpec(memory_space=pltpu.VMEM)
    return pl.pallas_call(
        partial(update_kernel, rates),
        in_specs=[pl.BlockSpec(memory_space=pltpu.SMEM)] + [whole] * (4 + len(weights)),
        out_specs=[whole] * len(weights),
        out_shape=[jax.ShapeDtypeStruct(weight.shape, jnp.float32) for weight in weights],
        compiler_params=pltpu.CompilerParams(vmem_limit_bytes=40 << 20),
        cost_estimate=pl.CostEstimate(flops=1 << 20, bytes_accessed=1 << 16, transcendentals=0),
        name="update",
    )(spot[None].astype(jnp.int32), *orthos, *weights)


def heads_kernel(place_ref, blocks_ref, bias_ref, out_ref, held):
    count, rows, columns = blocks_ref.shape
    held[rows : held.shape[0], :] = jnp.zeros((held.shape[0] - rows, 3 * D), jnp.float32)
    for number in range(count):
        spot = slice(number * columns, (number + 1) * columns)
        held[0:rows, spot] = blocks_ref[place_ref[number]] + bias_ref[:, spot]
    high, low = split_two(held[...])
    some = held.shape[0]
    none = jnp.zeros((LANES - some, 3 * D), jnp.bfloat16)
    out_ref[0:some, :] = high
    out_ref[some:LANES, :] = none
    out_ref[LANES : LANES + some, :] = low
    out_ref[LANES + some : 2 * LANES, :] = none


def heads_table(blocks, place, bias):
    return pl.pallas_call(
        heads_kernel,
        grid_spec=pltpu.PrefetchScalarGridSpec(
            num_scalar_prefetch=1,
            grid=(1,),
            in_specs=[
                pl.BlockSpec(blocks.shape, lambda step, place: (0, 0, 0)),
                pl.BlockSpec(bias.shape, lambda step, place: (0, 0)),
            ],
            out_specs=pl.BlockSpec((2 * LANES, 3 * D), lambda step, place: (0, 0)),
            scratch_shapes=[pltpu.VMEM((VOCAB + -VOCAB % 16, 3 * D), jnp.float32)],
        ),
        out_shape=jax.ShapeDtypeStruct((2 * LANES, 3 * D), jnp.bfloat16),
        name="heads_table",
    )(place, blocks, bias)


def turn(values, cosine, sine_table):
    lane = lax.broadcasted_iota(jnp.int32, values.shape, 1)
    half = HEAD_DIM // 2
    partner = jnp.where(
        lane % HEAD_DIM < half,
        pltpu.roll(values, PAIR - half, 1),
        pltpu.roll(values, half, 1),
    )
    return values * cosine + partner * sine_table


def attend_kernel(
    hot_ref, tq_ref, tk_ref, tv_ref, cos_ref, sin_ref,
    q_ref, k_ref, v_ref, mixed_ref, log_ref,
    q_all, v_turned, mixed_turned, prob_all,
):
    hot = hot_ref[...]
    cosine = cos_ref[...]
    sine_table = sin_ref[...]
    queries = jnp.dot(hot, tq_ref[...], preferred_element_type=jnp.float32)
    queries = turn(queries, cosine, sine_table).astype(jnp.bfloat16) * HEAD_DIM ** (-0.5)
    queries = queries.astype(jnp.bfloat16)
    q_ref[...] = queries
    q_all[0:SEQ_LEN, :] = queries
    q_all[SEQ_LEN:SPAN, :] = jnp.zeros((SPAN - SEQ_LEN, PAIR), jnp.bfloat16)
    keys = jnp.dot(hot, tk_ref[...], preferred_element_type=jnp.float32)
    keys = turn(keys, cosine, sine_table).astype(jnp.bfloat16)
    k_ref[...] = keys
    values = jnp.dot(hot, tv_ref[...], preferred_element_type=jnp.float32)
    v_ref[...] = values.astype(jnp.bfloat16)
    v_turned[...] = values.T.astype(jnp.bfloat16)

    def one_head(head, carry):
        lane = lax.broadcasted_iota(jnp.int32, (SEQ_LEN, PAIR), 1)
        keys_head = jnp.where(lane // HEAD_DIM == head, k_ref[...], jnp.zeros((), jnp.bfloat16))
        head_rows = pl.ds(pl.multiple_of(head * HEAD_DIM, HEAD_DIM), HEAD_DIM)
        values_head = v_turned[head_rows, :]

        def body(step, carry):
            at = pl.multiple_of(step * STRIP, STRIP)
            scores = row_dot(keys_head, q_all[pl.ds(at, STRIP), :])
            peak = jnp.max(scores, axis=0, keepdims=True)
            powers = jnp.exp(scores - peak)
            total = jnp.sum(powers, axis=0, keepdims=True)
            prob_low = (powers * (1.0 / total)).astype(jnp.bfloat16)
            prob_all[:, pl.ds(at, STRIP)] = prob_low
            log_ref[0, pl.ds(head, 1), pl.ds(at, STRIP)] = peak + jnp.log(total)
            return carry

        lax.fori_loop(0, SPAN // STRIP, body, 0, unroll=SPAN // STRIP)
        mixed_turned[head_rows, :] = jnp.dot(
            values_head, prob_all[...], preferred_element_type=jnp.float32
        )
        return carry

    lax.fori_loop(0, 2, one_head, 0, unroll=2)
    mixed_ref[...] = mixed_turned[...].T[0:SEQ_LEN, :].astype(jnp.bfloat16)


def attend_call(hot, tables, cosine, sine_table, first, count):
    whole = lambda step: (0, 0)
    source = lambda step: (0, step + first)
    own = lambda step: (0, step)
    rows_low = jax.ShapeDtypeStruct((SEQ_LEN, count * PAIR), jnp.bfloat16)
    return pl.pallas_call(
        attend_kernel,
        grid=(count,),
        in_specs=[
            pl.BlockSpec(hot.shape, whole),
            pl.BlockSpec((hot.shape[1], PAIR), source),
            pl.BlockSpec((hot.shape[1], PAIR), lambda step: (0, step + first + D // PAIR)),
            pl.BlockSpec((hot.shape[1], PAIR), lambda step: (0, step + first + 2 * D // PAIR)),
            pl.BlockSpec((SEQ_LEN, PAIR), whole),
            pl.BlockSpec((SEQ_LEN, PAIR), whole),
        ],
        out_specs=[
            pl.BlockSpec((SEQ_LEN, PAIR), own),
            pl.BlockSpec((SEQ_LEN, PAIR), own),
            pl.BlockSpec((SEQ_LEN, PAIR), own),
            pl.BlockSpec((SEQ_LEN, PAIR), own),
            pl.BlockSpec((1, 2, SPAN), lambda step: (step, 0, 0)),
        ],
        out_shape=[rows_low] * 4 + [jax.ShapeDtypeStruct((count, 2, SPAN), jnp.float32)],
        scratch_shapes=[
            pltpu.VMEM((SPAN, PAIR), jnp.bfloat16),
            pltpu.VMEM((PAIR, SEQ_LEN), jnp.bfloat16),
            pltpu.VMEM((PAIR, SPAN), jnp.float32),
            pltpu.VMEM((SEQ_LEN, SPAN), jnp.bfloat16),
        ],
        compiler_params=pltpu.CompilerParams(vmem_limit_bytes=40 << 20),
        cost_estimate=pl.CostEstimate(
            flops=count * SPAN * SPAN, bytes_accessed=1 << 16,
            transcendentals=0,
        ),
        name="attend",
    )(hot, tables, tables, tables, cosine, sine_table)


def attend_back_kernel(
    hot_ref, q_ref, k_ref, v_ref, grad_ref, log_ref, cos_ref, sin_ref,
    low_ref, sums_ref,
    q_all, grad_all, k_turned, prob_all, score_all, query_turned, key_sum, value_sum,
):
    rest = jnp.zeros((SPAN - SEQ_LEN, PAIR), jnp.bfloat16)
    q_all[0:SEQ_LEN, :] = q_ref[...]
    q_all[SEQ_LEN:SPAN, :] = rest
    grad_all[0:SEQ_LEN, :] = grad_ref[...]
    grad_all[SEQ_LEN:SPAN, :] = rest
    k_turned[...] = k_ref[...].astype(jnp.float32).T.astype(jnp.bfloat16)
    lane = lax.broadcasted_iota(jnp.int32, (SEQ_LEN, PAIR), 1)
    none = jnp.zeros((), jnp.bfloat16)

    def one_head(head, carry):
        head_rows = pl.ds(pl.multiple_of(head * HEAD_DIM, HEAD_DIM), HEAD_DIM)
        keys_head = jnp.where(lane // HEAD_DIM == head, k_ref[...], none)
        values_head = jnp.where(lane // HEAD_DIM == head, v_ref[...], none)

        def body(step, carry):
            at = pl.multiple_of(step * STRIP, STRIP)
            scores = row_dot(keys_head, q_all[pl.ds(at, STRIP), :])
            prob_rows = jnp.exp(scores - log_ref[0, pl.ds(head, 1), pl.ds(at, STRIP)])
            prob_all[:, pl.ds(at, STRIP)] = prob_rows.astype(jnp.bfloat16)
            prob_grad = row_dot(values_head, grad_all[pl.ds(at, STRIP), :])
            delta = jnp.sum(prob_grad * prob_rows, axis=0, keepdims=True)
            score_all[:, pl.ds(at, STRIP)] = (prob_rows * (prob_grad - delta)).astype(jnp.bfloat16)
            return carry

        lax.fori_loop(0, SPAN // STRIP, body, 0, unroll=SPAN // STRIP)
        value_part = jnp.dot(prob_all[...], grad_all[...], preferred_element_type=jnp.float32)
        key_part = jnp.dot(score_all[...], q_all[...], preferred_element_type=jnp.float32)
        value_sum[...] = jnp.where(lane // HEAD_DIM == head, value_part, value_sum[...])
        key_sum[...] = jnp.where(lane // HEAD_DIM == head, key_part, key_sum[...])
        query_turned[head_rows, :] = (
            jnp.dot(k_turned[head_rows, :], score_all[...], preferred_element_type=jnp.float32)
            * HEAD_DIM ** (-0.5)
        )
        return carry

    lax.fori_loop(0, 2, one_head, 0, unroll=2)
    cosine = cos_ref[...]
    sine_table = -sin_ref[...]
    hot = hot_ref[...]
    query_low = turn(query_turned[...].T[0:SEQ_LEN, :], cosine, sine_table).astype(jnp.bfloat16)
    key_low = turn(key_sum[...], cosine, sine_table).astype(jnp.bfloat16)
    value_low = value_sum[...].astype(jnp.bfloat16)
    for number, low in enumerate((query_low, key_low, value_low)):
        low_ref[number] = low
        sums_ref[number] = jnp.dot(hot, low, preferred_element_type=jnp.float32)


def attend_back_call(
    hot_turned, queries, keys, values, gradients, logs, cosine, sine_table, first, inside, count
):
    whole = lambda step: (0, 0)
    rows = pl.BlockSpec((SEQ_LEN, PAIR), lambda step: (0, step + inside))
    whole_rows = pl.BlockSpec((SEQ_LEN, PAIR), whole)
    return pl.pallas_call(
        attend_back_kernel,
        grid=(count,),
        in_specs=[
            pl.BlockSpec(hot_turned.shape, whole),
            rows,
            rows,
            rows,
            pl.BlockSpec((SEQ_LEN, PAIR), lambda step: (0, step + first)),
            pl.BlockSpec((1, 2, SPAN), lambda step: (step + inside, 0, 0)),
            whole_rows,
            whole_rows,
        ],
        out_specs=[
            pl.BlockSpec((3, SEQ_LEN, PAIR), lambda step: (0, 0, step)),
            pl.BlockSpec((3, hot_turned.shape[0], PAIR), lambda step: (0, 0, step)),
        ],
        out_shape=[
            jax.ShapeDtypeStruct((3, SEQ_LEN, count * PAIR), jnp.bfloat16),
            jax.ShapeDtypeStruct((3, hot_turned.shape[0], count * PAIR), jnp.float32),
        ],
        scratch_shapes=[
            pltpu.VMEM((SPAN, PAIR), jnp.bfloat16),
            pltpu.VMEM((SPAN, PAIR), jnp.bfloat16),
            pltpu.VMEM((PAIR, SEQ_LEN), jnp.bfloat16),
            pltpu.VMEM((SEQ_LEN, SPAN), jnp.bfloat16),
            pltpu.VMEM((SEQ_LEN, SPAN), jnp.bfloat16),
            pltpu.VMEM((PAIR, SPAN), jnp.float32),
            pltpu.VMEM((SEQ_LEN, PAIR), jnp.float32),
            pltpu.VMEM((SEQ_LEN, PAIR), jnp.float32),
        ],
        compiler_params=pltpu.CompilerParams(vmem_limit_bytes=48 << 20),
        cost_estimate=pl.CostEstimate(
            flops=count * SPAN * SPAN, bytes_accessed=1 << 16,
            transcendentals=0,
        ),
        name="attend_back",
    )(hot_turned, queries, keys, values, gradients, logs, cosine, sine_table)


ERF_P = 0.3275911
ERF_A = (0.254829592, -0.284496736, 1.421413741, -1.453152027, 1.061405429)

def normal_parts(values):
    size = jnp.abs(values)
    bell = jnp.exp(values * values * -0.5)
    step = 1.0 / (1.0 + (ERF_P * 0.5**0.5) * size)
    series = ERF_A[4]
    for factor in (ERF_A[3], ERF_A[2], ERF_A[1], ERF_A[0]):
        series = series * step + factor
    tail = (0.5 * series) * step * bell
    return jnp.where(values < 0.0, tail, 1.0 - tail), bell * (1.0 / math.sqrt(2.0 * math.pi))

def start_parts(place_ref, source_ref, starts, held, sems):
    for part in range(PARTS):
        for number, start in enumerate(starts):

            def body(spot, carry):
                pltpu.make_async_copy(
                    source_ref.at[place_ref[part * PART_BLOCKS + spot], pl.ds(start, BLOCK), :],
                    held[number].at[part, spot],
                    sems.at[number, part],
                ).start()
                return carry

            lax.fori_loop(0, PART_BLOCKS, body, 0)


def wait_part(source_ref, number, held, sems, step):
    pltpu.make_async_copy(
        source_ref.at[pl.ds(0, PART_BLOCKS), pl.ds(0, BLOCK), :],
        held[number].at[step],
        sems.at[number, step],
    ).wait()
    return held[number][step].reshape(D, D)


def feed_kernel(starts, place_ref, rows_ref, bias_ref, source_ref, hidden_ref, slope_ref, out_ref, expand_held, reduce_held, sems):
    held = (expand_held, reduce_held)
    step = pl.program_id(0)
    @pl.when(step == 0)
    def _():
        start_parts(place_ref, source_ref, starts, held, sems)

    expand = wait_part(source_ref, 0, held, sems, step)
    reduce = wait_part(source_ref, 1, held, sems, step)
    for at in range(0, SEQ_LEN, FEED_STRIP):
        spot = slice(at, at + FEED_STRIP)
        values = row_dot(rows_ref[spot, :], expand) + bias_ref[...]
        below, bell = normal_parts(values)
        hidden = (values * below).astype(jnp.bfloat16)
        hidden_ref[spot, :] = hidden
        slope_ref[spot, :] = (below + values * bell).astype(jnp.bfloat16)
        part = jnp.dot(hidden, reduce, preferred_element_type=jnp.float32)
        out_ref[spot, :] = jnp.where(step == 0, 0.0, out_ref[spot, :]) + part


def feed_call(place, rows, bias, source, starts):
    whole = lambda step, place: (0, 0)
    chunk = pl.BlockSpec((SEQ_LEN, D), lambda step, place: (0, step))
    return pl.pallas_call(
        partial(feed_kernel, starts),
        grid_spec=pltpu.PrefetchScalarGridSpec(
            num_scalar_prefetch=1,
            grid=(PARTS,),
            in_specs=[
                pl.BlockSpec((SEQ_LEN, D), whole),
                pl.BlockSpec((1, D), lambda step, place: (0, step)),
                pl.BlockSpec(memory_space=pl.ANY),
            ],
            out_specs=[chunk, chunk, pl.BlockSpec((SEQ_LEN, D), whole)],
            scratch_shapes=[
                pltpu.VMEM((PARTS, PART_BLOCKS, BLOCK, D), jnp.bfloat16),
                pltpu.VMEM((PARTS, PART_BLOCKS, BLOCK, D), jnp.bfloat16),
                pltpu.SemaphoreType.DMA((2, PARTS)),
            ],
        ),
        out_shape=[jax.ShapeDtypeStruct((SEQ_LEN, FF), jnp.bfloat16)] * 2
        + [jax.ShapeDtypeStruct((SEQ_LEN, D), jnp.float32)],
        compiler_params=pltpu.CompilerParams(vmem_limit_bytes=48 << 20),
        cost_estimate=pl.CostEstimate(
            flops=SEQ_LEN * D * FF, bytes_accessed=1 << 16, transcendentals=0
        ),
        name="feed",
    )(place, rows, bias, source)


def feed_back_kernel(starts, place_ref, grad_ref, slope_ref, source_ref, pre_ref, out_ref, bias_ref, expand_held, reduce_held, sems):
    held = (expand_held, reduce_held)
    step = pl.program_id(0)
    @pl.when(step == 0)
    def _():
        start_parts(place_ref, source_ref, starts, held, sems)

    reduce = wait_part(source_ref, 1, held, sems, step)
    expand = wait_part(source_ref, 0, held, sems, step)
    total = jnp.zeros((1, D), jnp.float32)
    for at in range(0, SEQ_LEN, SEQ_LEN):
        spot = slice(at, at + SEQ_LEN)
        grad = row_dot(grad_ref[spot, :], reduce) * slope_ref[spot, :].astype(jnp.float32)
        low = grad.astype(jnp.bfloat16)
        pre_ref[spot, :] = low
        total = total + jnp.sum(low.astype(jnp.float32), axis=0, keepdims=True)
        part = jnp.dot(low, expand, preferred_element_type=jnp.float32)
        out_ref[spot, :] = jnp.where(step == 0, 0.0, out_ref[spot, :]) + part
    bias_ref[...] = total


def feed_back_call(place, grad, slope, source, starts):
    whole = lambda step, place: (0, 0)
    chunk = pl.BlockSpec((SEQ_LEN, D), lambda step, place: (0, step))
    return pl.pallas_call(
        partial(feed_back_kernel, starts),
        grid_spec=pltpu.PrefetchScalarGridSpec(
            num_scalar_prefetch=1,
            grid=(PARTS,),
            in_specs=[
                pl.BlockSpec((SEQ_LEN, D), whole),
                chunk,
                pl.BlockSpec(memory_space=pl.ANY),
            ],
            out_specs=[
                chunk,
                pl.BlockSpec((SEQ_LEN, D), whole),
                pl.BlockSpec((1, D), lambda step, place: (0, step)),
            ],
            scratch_shapes=[
                pltpu.VMEM((PARTS, PART_BLOCKS, BLOCK, D), jnp.bfloat16),
                pltpu.VMEM((PARTS, PART_BLOCKS, BLOCK, D), jnp.bfloat16),
                pltpu.SemaphoreType.DMA((2, PARTS)),
            ],
        ),
        out_shape=[
            jax.ShapeDtypeStruct((SEQ_LEN, FF), jnp.bfloat16),
            jax.ShapeDtypeStruct((SEQ_LEN, D), jnp.float32),
            jax.ShapeDtypeStruct((1, FF), jnp.float32),
        ],
        compiler_params=pltpu.CompilerParams(vmem_limit_bytes=48 << 20),
        cost_estimate=pl.CostEstimate(
            flops=SEQ_LEN * D * FF, bytes_accessed=1 << 16, transcendentals=0
        ),
        name="feed_back",
    )(place, grad, slope, source)


def adam_step(weight, mean_state, square, gradient, step_rate, decay_rate, step_count):
    mean_next = ADAM_BETA1 * mean_state + (1.0 - ADAM_BETA1) * gradient
    square_next = ADAM_BETA2 * square + (1.0 - ADAM_BETA2) * gradient * gradient
    step_float = step_count.astype(jnp.float32)
    mean_hat = mean_next / (1.0 - ADAM_BETA1**step_float)
    square_hat = square_next / (1.0 - ADAM_BETA2**step_float)
    updated = weight - step_rate * (
        mean_hat / (jnp.sqrt(square_hat) + ADAM_EPS) + decay_rate * weight
    )
    return (updated, mean_next, square_next)


def on_device(
    codons,
    offsets,
    positions,
    targets,
    table_weight,
    attend_weight,
    mixing_weight,
    expand_weight,
    reduce_weight,
    vector_params,
    attend_moment,
    mixing_moment,
    expand_moment,
    reduce_moment,
    table_mean,
    table_square,
    vector_mean,
    vector_square,
    step_count,
):
    low_type = jnp.bfloat16
    wide_at = lax.axis_index("wide")
    me = my_index()
    devices = lax.axis_size(BOTH)
    masks = wide_masks()
    narrow_size = lax.axis_size("narrow")
    wide_size = lax.axis_size("wide")
    hidden_masks = masks[:-1] + [2, masks[-1], 1]
    all_masks = masks + [2, 1]
    small = jnp.concatenate([table_weight, vector_params], axis=0).astype(low_type)
    small = gather_blocks(small[None], masks)
    packed = (expand_weight, reduce_weight, mixing_weight, attend_weight)
    units = [weight.shape[0] // narrow_size for weight in packed]
    starts = np.cumsum([0] + [unit + -unit % 16 for unit in units])
    packed_low, attend_own = pack_rows(packed, lax.axis_index("narrow"))
    weights_low = lax.all_gather(packed_low, BOTH, axis=0)

    def weight_rows(number, unit):
        start = int(starts[number])
        return weights_low[:, start : start + unit].reshape(-1, D)

    codons, positions, targets = gate((codons, positions, targets), small)
    small = in_order(small, masks, narrow_size, wide_at)
    small = jnp.transpose(small, (1, 0, 2)).reshape(VOCAB + 15, D)
    table_low = small[:VOCAB]
    vector_full = small[VOCAB:].astype(jnp.float32)
    gain_one = vector_full[0]
    bias_one = vector_full[1]
    gain_two = vector_full[2]
    bias_two = vector_full[3]
    gain_last = vector_full[4]
    bias_last = vector_full[5]
    attend_bias = vector_full[6:9].reshape(1, 3 * D)
    mixing_bias = vector_full[9]
    reduce_bias = vector_full[10]
    expand_bias = out_of_order(
        vector_full[11:15].reshape(devices, FF // devices), hidden_masks, 1, me
    ).reshape(FF)
    embed_scale = math.sqrt(D)
    table_stream = embed_scale * table_low.astype(jnp.float32)
    table_normed = norm_forward(table_stream, gain_one, bias_one)[0].astype(low_type)
    table_own = times_trans(table_normed, attend_own)
    place = jnp.asarray(places_of(all_masks, 1), jnp.int32)[jnp.arange(devices) ^ me]
    tables = heads_table(gather_blocks(table_own[None], all_masks), place, attend_bias)

    unit = FF // devices
    hidden_place = jnp.asarray(offsets_of(hidden_masks)) ^ me
    if unit == BLOCK:
        feed_place, feed_source, feed_starts = hidden_place, weights_low, tuple(starts[:2])
    else:
        feed_source = jnp.concatenate(
            [
                take_blocks(weights_low[:, start : start + unit], hidden_place).reshape(-1, BLOCK, D)
                for start in (int(starts[0]), int(starts[1]))
            ],
            axis=1,
        )
        feed_place, feed_starts = jnp.arange(FF // BLOCK), (0, BLOCK)
    feed_place = feed_place.astype(jnp.int32)
    feed_starts = tuple(int(start) for start in feed_starts)

    seq_count = codons.shape[0]
    row_count = seq_count * SEQ_LEN
    window = jax.vmap(partial(lax.dynamic_slice_in_dim, slice_size=SEQ_LEN))(codons, offsets)
    vocab_ids = jnp.arange(VOCAB, dtype=jnp.int32)
    token_hot = window.reshape(row_count)[:, None] == vocab_ids[None, :]
    token_low = token_hot.astype(low_type)
    target_hot = (targets.reshape(row_count)[:, None] == vocab_ids[None, :]).astype(jnp.float32)
    stream = embed_scale * times_plain(token_low, table_low)
    token_ids = window.reshape(row_count)
    lane_ids = jnp.arange(2 * LANES, dtype=jnp.int32) % LANES
    hot = (token_ids[:, None] == lane_ids[None, :]).astype(low_type)
    hot_turned = (token_ids[None, :] == lane_ids[:LANES, None]).astype(low_type)
    cosine, sine_table = rotary_tables(positions.reshape(row_count))
    cosine = jnp.concatenate([cosine] * 4, axis=1)
    sine_table = jnp.concatenate([-sine_table, sine_table] * 2, axis=1)
    pairs = D // PAIR // ATTEND_CALLS
    attended = []

    for number in range(ATTEND_CALLS):
        attended.append(
            attend_call(hot, tables, cosine, sine_table, number * pairs, pairs)
        )
    last_mask = masks[-1]
    mixed_low = jnp.concatenate([parts[3] for parts in attended], axis=1)
    mixing_low = weight_rows(2, D // devices)
    attend_low = lax.all_gather(gate(attend_own, mixed_low), BOTH, axis=0)
    branch = times_trans(mixed_low, mixing_low) + mixing_bias
    middle = stream + branch
    normed_two, normal_two, inverse_two = norm_forward(middle, gain_two, bias_two)
    normed_two_low = normed_two.astype(low_type)
    hidden_low, slope_low, feed_out = feed_call(
        feed_place, normed_two_low, expand_bias[None, :], feed_source, feed_starts
    )
    feed_out = feed_out + reduce_bias
    output = middle + feed_out
    final_norm, normal_last, inverse_last = norm_forward(output, gain_last, bias_last)
    final_low = final_norm.astype(low_type)
    logits = times_trans(final_low, table_low)
    row_peak = jnp.max(logits, axis=-1, keepdims=True)
    shifted = jnp.exp(logits - row_peak)
    prob_rows = shifted / jnp.sum(shifted, axis=-1, keepdims=True)
    prob_sum = jnp.sum(prob_rows, axis=0)
    logit_grad = (prob_rows - target_hot).astype(low_type)
    final_grad = times_plain(logit_grad, table_low)
    table_head = trans_times(logit_grad, final_low)
    output_grad, gain_last_grad, bias_last_grad = norm_backward(
        final_grad, normal_last, inverse_last, gain_last
    )
    feed_low = output_grad.astype(low_type)
    reduce_bias_grad = jnp.sum(feed_low, axis=0, dtype=jnp.float32)
    half_ff = FF // 2
    static_marks = [masks[-1], 2] + list(reversed(masks[:-1]))
    static_shape = (2,) * len(static_marks) + (unit, D)

    reduce_send = trans_times(hidden_low[:, half_ff:], feed_low).astype(low_type)
    pre_grad, normed_two_grad, expand_bias_grad = feed_back_call(
        feed_place, gate(feed_low, reduce_send), slope_low, feed_source, feed_starts
    )
    reduce_got = gate(swap(reduce_send, 1), pre_grad)
    reduce_sum = trans_times(hidden_low[:, :half_ff], feed_low) + reduce_got
    reduce_chain = sum_chain([(reduce_sum.reshape(static_shape), static_marks, False)], low_type)
    reduce_sent = next(reduce_chain)
    expand_send = trans_times(
        gate(pre_grad, reduce_sent)[:, half_ff:], normed_two_low
    ).astype(low_type)
    expand_sum = trans_times(pre_grad[:, :half_ff], normed_two_low) + swap(expand_send, 1)
    middle_part, gain_two_grad, bias_two_grad = norm_backward(
        normed_two_grad, normal_two, inverse_two, gain_two
    )
    middle_grad = output_grad + middle_part
    branch_low = middle_grad.astype(low_type)
    mixing_bias_grad = jnp.sum(branch_low, axis=0, dtype=jnp.float32)
    mixing_sum = trans_times(branch_low, mixed_low).reshape(
        bits_shape(devices, (D // devices, D))
    )
    (mixing_item,) = finish_hop(hop([(mixing_sum, all_masks, True)], 1, low_type))
    mixed_grad = times_plain(branch_low, mixing_low).astype(low_type)
    expand_chain = sum_chain(
        [(expand_sum.reshape(static_shape), static_marks, False), mixing_item], low_type
    )
    expand_sent = next(expand_chain)

    backs = []
    back_pairs = D // PAIR // BACK_CALLS

    def back_step(waits):
        number = len(backs)
        first = number * back_pairs
        source = attended[first // pairs]
        order = (backs[-1][1],) if backs else ()
        backs.append(
            attend_back_call(
                hot_turned,
                *source[:3],
                gate(mixed_grad, (waits, order)),
                source[4],
                cosine,
                sine_table,
                first,
                first % pairs,
                back_pairs,
            )
        )
        return backs[-1][1]

    mixed_grad, attend_low = lax.optimization_barrier((mixed_grad, attend_low))
    back_step(expand_sent)
    token = back_step(())
    expand_sent = expand_chain.send(token)
    reduce_sent = reduce_chain.send(token)
    token = back_step((expand_sent, reduce_sent))
    expand_sent = expand_chain.send(token)
    reduce_sent = reduce_chain.send(token)
    token = back_step((expand_sent, reduce_sent))
    reduce_sent = reduce_chain.send(token)
    token = back_step(reduce_sent)
    expand_sent = expand_chain.send(token)
    token = back_step(expand_sent)
    (reduce_sum,) = drain(reduce_chain, token)
    expand_sum, mixing_sum = drain(expand_chain, token)
    dense = jnp.concatenate([reduce_sum, expand_sum, mixing_sum], axis=0)
    spot = lax.axis_index("narrow")
    dense, backs = together((dense, backs))

    def one_chain(value, mask):
        (got,) = yield [(value, mask)]
        return got

    columns = D // wide_size
    rows_hist = -(-VOCAB // columns)

    def make_small(backs):
        entry_gradient, one_sums, table_sum = entry_call(
            embed_scale,
            hot,
            jnp.pad(table_low, ((0, LANES - VOCAB), (0, 0))),
            gain_one[None, :],
            middle_grad,
            attend_low.reshape(3 * D, D),
            [back[0] for back in backs],
        )
        hist_part = jnp.pad(prob_sum, (0, rows_hist * columns - VOCAB)).reshape(rows_hist, columns)
        expand_ordered = in_order(
            expand_bias_grad.reshape(devices, FF // devices), hidden_masks, 1, me
        )
        small_grads = small_blocks(
            [back[1] for back in backs],
            table_sum,
            table_head,
            hist_part,
            (
                (one_sums, 0),
                (gain_two_grad, 2),
                (bias_two_grad, 3),
                (gain_last_grad, 4),
                (bias_last_grad, 5),
                (mixing_bias_grad, 9),
                (reduce_bias_grad, 10),
                (expand_ordered.reshape(1, FF), 11),
            ),
            wide_size,
        )
        return entry_gradient, small_grads

    beside_chain = Chain(one_chain(dense, 2))
    entry_gradient, small_grads = advance([beside_chain], make_small, backs)
    beside = beside_chain.result
    cores = [Chain(one_chain(dense, 1)), Chain(one_chain(beside, 1))]
    small_chain = Chain(sum_small(small_grads))
    advance(cores + [small_chain])
    pieces = (dense, beside, cores[0].result, cores[1].result)

    def make_dense(pieces):
        return dense_step(
            spot,
            (unit, unit, D // devices),
            pieces,
            attend_moment,
            (reduce_moment, expand_moment, mixing_moment),
        )

    dense_totals, dense_next, dense_rows, gram_own = advance([small_chain], make_dense, pieces)
    reduce_total, expand_total, mixing_total = dense_totals
    reduce_next, expand_next, mixing_next = dense_next

    def step_of(moment, gradient):
        moment_next = MUON_MU * moment + (1.0 - MUON_MU) * gradient
        return moment_next, (1.0 - MUON_MU) * gradient + MUON_MU * moment_next

    gram_chain = Chain(sum_gram(gram_own))
    while small_chain.request:
        advance([chain for chain in (gram_chain, small_chain) if chain.request])
    small_total = small_chain.result
    token_sums = small_total[:VOCAB, : 3 * D // wide_size]
    small_total = small_total[:, 3 * D // wide_size :]
    attend_total = lax.dot_general(
        token_sums,
        table_normed.astype(jnp.float32),
        (((0,), (0,)), ((), ())),
        precision=lax.Precision.HIGHEST,
        preferred_element_type=jnp.float32,
    )
    attend_next, attend_step = step_of(attend_moment, attend_total)
    gradient_rate = (1.0 - MUON_MU) * (1.0 + MUON_MU)
    crossed = exact_times(
        token_sums, jnp.concatenate([attend_moment, token_sums.T], axis=1)
    )
    crossed_chain = Chain(sum_wide(crossed))
    while crossed_chain.request:
        advance([chain for chain in (gram_chain, crossed_chain) if chain.request])
    while gram_chain.request:
        advance([gram_chain])
    crossed = crossed_chain.result
    gram_parts = gram_chain.result
    table_wide = table_normed.astype(jnp.float32)
    added = gradient_rate * (
        (MUON_MU * MUON_MU) * crossed[:, :D]
        + (0.5 * gradient_rate) * exact_times(crossed[:, D:], table_wide)
    )
    added = jnp.where(spot == 0, added, 0.0)
    table_total = small_total[:VOCAB]
    vector_total = small_total[VOCAB : VOCAB + 15]
    prob_total = small_total[VOCAB + 15 :].reshape(rows_hist * columns)[:VOCAB]
    histogram = prob_total * (VOCAB / (row_count * devices))
    totals = (attend_total, mixing_total, expand_total, reduce_total)
    moment_next = (attend_next, mixing_next, expand_next, reduce_next)
    most = dense_rows.shape[0]
    attend_rows = jnp.pad(attend_step, ((0, most - attend_step.shape[0]), (0, 0)))
    rows = jnp.where(spot == 0, attend_rows, dense_rows)
    ortho = newton_rows(gram_parts, rows, added, table_normed)
    ortho, table_total, vector_total = together((ortho, table_total, vector_total))
    across = swap(ortho, 2)
    table_new, table_mean_next, table_square_next = adam_step(
        table_weight, table_mean, table_square, table_total, TABLE_RATE, TABLE_DECAY, step_count
    )
    vector_new, vector_mean_next, vector_square_next = adam_step(
        vector_params, vector_mean, vector_square, vector_total, VECTOR_RATE, 0.0, step_count
    )
    across, adam_results = together(
        (
            across,
            (
                table_new,
                table_mean_next,
                table_square_next,
                vector_new,
                vector_mean_next,
                vector_square_next,
            ),
        )
    )
    orthos = (ortho, swap(ortho, 1), across, swap(across, 1))
    matrices = (attend_weight, mixing_weight, expand_weight, reduce_weight)
    rates = tuple(
        MUON_RATE * SHAPE_FACTOR * math.sqrt(max(rows, D)) for rows in (3 * D, D, FF, FF)
    )
    matrix_new = tuple(update_rows(spot, orthos, matrices, rates))
    results = (
        totals
        + (table_total, vector_total)
        + matrix_new
        + moment_next
        + (
            *adam_results,
        )
    )
    block_output = output.astype(low_type).reshape(seq_count, SEQ_LEN, D)
    return (block_output, entry_gradient.reshape(seq_count, SEQ_LEN, D)) + results + (histogram,)


def solution(mesh):
    in_specs = (
        P(("wide", "narrow"), None),
        P(("wide", "narrow")),
        P(("wide", "narrow"), None),
        P(("wide", "narrow"), None),
        P(None, "wide"),
        P("wide", None),
        P("wide", None),
        P("wide", None),
        P("wide", None),
        P(None, "wide"),
        P("wide", None),
        P("wide", None),
        P("wide", None),
        P("wide", None),
        P(None, "wide"),
        P(None, "wide"),
        P(None, "wide"),
        P(None, "wide"),
        P(),
    )
    out_specs = (
        P(("wide", "narrow"), None, None),
        P(("wide", "narrow"), None, None),
        P("wide", None),
        P("wide", None),
        P("wide", None),
        P("wide", None),
        P(None, "wide"),
        P(None, "wide"),
        P("wide", None),
        P("wide", None),
        P("wide", None),
        P("wide", None),
        P("wide", None),
        P("wide", None),
        P("wide", None),
        P("wide", None),
        P(None, "wide"),
        P(None, "wide"),
        P(None, "wide"),
        P(None, "wide"),
        P(None, "wide"),
        P(None, "wide"),
        P(),
    )
    return jax.shard_map(
        on_device, mesh=mesh, in_specs=in_specs, out_specs=out_specs, check_vma=False
    )
```
